128 devices in a mesh: lat: 16 (over x, y), lon: 8 (over z, core).
Axes of the slice: x: 4, y: 4, z: 4, core: 2. Of those that a mesh axis runs over, the one named last changes fastest.
Arguments:
- state: float32 [3, 384, 49152], P(None, 'lat', 'lon'), may hold values from -6 to 6
- sigma: float32 [3, 384, 768], P(None, 'lat', 'lon'), may hold values from 0.3 to 3
- vert: float32 [3, 64, 64], replicated, may hold values from -0.75 to 0.75
- bal_temp: float32 [64, 64], replicated, may hold values from -0.75 to 0.75
- chi_coef: float32 [64], replicated, may hold values from -1 to 1
- scales: float32 [8], replicated, may hold values from 6 to 40
- classes: int32 [192], replicated, may hold values from 0 to 7
- owner: int32 [192], replicated, may hold values from 0 to 127, as said below
Outputs:
- applied: float32 [3, 384, 49152], P(None, 'lat', 'lon')
- slab_energy: float32 [128, 3], P(('lat', 'lon'))
The draws below stay inside these ranges and needn't reach their ends.
Inputs may be any that keep to these rules, and one draw needn't show every extreme that they name: `owner`: every device owns at most 3 slabs, and some device owns exactly 3.
All inputs are finite; a program needn't handle non-finite values.
Results may differ from the reference program's by a relative error of at most 0.0003.
Values sent between devices are 32-bit elements; how exact they have to be, the bound alone decides.
A program may use at most 64 MiB of HBM per device.

```python
import math
import jax
import jax.numpy as jnp
from jax import lax

NLAT = 384
NLON = 768
L = 64
NVAR = 3
NCLASS = 8
CAP = 3
N_LAT = 16
N_LON = 8


def draw_owner(key, part):
    slots = N_LAT * N_LON * CAP
    count = NVAR * L
    perm = jax.random.permutation(jax.random.fold_in(key, 11), slots)
    rank = jnp.argsort(perm)
    chosen = perm[0] // CAP
    score = rank + jnp.where(jnp.arange(slots) // CAP == chosen, -slots, 0)
    picked = jnp.argsort(score)[:count]
    order = jax.random.permutation(jax.random.fold_in(key, 12), count)
    return (picked[order] // CAP).astype(jnp.int32)


def place_ends(values, key, smallest, high):
    extent = values.shape
    index_at = [jax.random.randint(jax.random.fold_in(key, axis), (), 0, extent[axis]) for axis in range(len(extent))]
    values = values.at[tuple(index_at)].set(smallest)
    longest = extent.index(max(extent))
    index_at[longest] = (index_at[longest] + 1) % extent[longest]
    return values.at[tuple(index_at)].set(high)


def block_levels(rng, extent, shards, smallest, top_value):
    level = 1.0
    for axis_at, parts in shards:
        steps = jax.random.uniform(jax.random.fold_in(jax.random.fold_in(rng, 6), axis_at), (parts,), jnp.float32, smallest / len(shards), top_value / len(shards))
        level = level * jnp.repeat(jnp.exp(steps), extent[axis_at] // parts).reshape((-1,) + (1,) * (len(extent) - 1 - axis_at))
    return level


def noise(own_key, shape, width, bound, shards=(), kind=jnp.bfloat16):
    drawn = width * jax.random.normal(own_key, shape, jnp.float32)
    if shards:
        drawn = drawn * block_levels(own_key, shape, shards, -0.22, 0.18)
    return jnp.clip(drawn, -bound, bound).astype(kind)


def setup_inputs(seed: int = 0) -> dict:
    arg_keys = jax.random.split(jax.random.key(seed), 9)
    state = noise(arg_keys[0], (NVAR, NLAT, NLON * L), 1.0, 6.0, ((1, 16), (2, 8)), jnp.float32)
    sigma = jnp.clip(jnp.exp(math.log(3.0) - 2.3025851 * jax.random.uniform(arg_keys[1], (NVAR, NLAT, NLON), jnp.float32) ** block_levels(arg_keys[1], (NVAR, NLAT, NLON), ((1, 16), (2, 8)), -0.2, 0.2)), 0.3, 3.0)
    vert = noise(arg_keys[2], (NVAR, L, L), L ** -0.5, 0.75, (), jnp.float32)
    bal_temp = noise(arg_keys[3], (L, L), L ** -0.5, 0.75, (), jnp.float32)
    chi_coef = jnp.clip(jax.random.uniform(arg_keys[4], (L,), jnp.float32, -1.0, 1.0), -1.0, 1.0)
    scales = jnp.clip(jnp.exp(jax.random.uniform(arg_keys[5], (NCLASS,), jnp.float32, math.log(6.0), math.log(40.0))), 6.0, 40.0)
    classes = place_ends(jax.random.randint(arg_keys[6], (NVAR * L,), 0, NCLASS), jax.random.fold_in(arg_keys[6], 1), 0, NCLASS - 1).astype(jnp.int32)
    owner = draw_owner(jax.random.fold_in(arg_keys[8], 71), 0)
    return {"state": state, "sigma": sigma, "vert": vert, "bal_temp": bal_temp, "chi_coef": chi_coef, "scales": scales, "classes": classes, "owner": owner}


def laplace(field):
    pad_spec = [(0, 0)] * (field.ndim - 2) + [(1, 1), (1, 1)]
    padded = jnp.pad(field, pad_spec)
    return (4.0 * field - padded[..., 2:, 1:-1] - padded[..., :-2, 1:-1]
            - padded[..., 1:-1, 2:] - padded[..., 1:-1, :-2])


def recur(field, coef, axis, backward):
    moved = jnp.moveaxis(field, axis, 0)
    if backward:
        moved = moved[::-1]
    decay = coef[:, None]

    def step(state, item):
        nxt = decay * state + (1.0 - decay) * item
        return nxt, nxt

    start = jnp.zeros(moved.shape[1:], jnp.float32)
    _, out = lax.scan(step, start, moved)
    if backward:
        out = out[::-1]
    return jnp.moveaxis(out, 0, axis)


def smooth(field, coef, amp):
    field = recur(field, coef, 2, False)
    field = recur(field, coef, 2, True)
    field = recur(field, coef, 1, False)
    field = recur(field, coef, 1, True)
    return field * amp[:, None, None]


def reference(state, sigma, vert, bal_temp, chi_coef, scales, classes, owner):
    highest = lax.Precision.HIGHEST
    field = state.reshape(NVAR, NLAT, NLON, L).transpose(0, 3, 1, 2)
    psi = field[0]
    chi = field[1]
    temp = field[2]
    folded = jnp.einsum('lk,lij->kij', bal_temp, temp, precision=highest)
    adj_psi = psi + chi_coef[:, None, None] * chi + laplace(folded)
    scaled = jnp.stack([adj_psi, chi, temp]) * sigma[:, None]
    w = jnp.einsum('vkl,vkij->vlij', vert, scaled, precision=highest)
    length = jnp.take(scales, classes)
    coef = jnp.exp(-1.0 / length).reshape(NVAR, L)
    amp = (length ** 0.75).reshape(NVAR, L)

    def per_var(items):
        slabs, decay, gain = items
        ctrl = smooth(slabs, decay, gain)
        energy = jnp.mean(ctrl * ctrl, axis=(1, 2))
        return smooth(ctrl, decay, gain), energy

    back, energy = lax.map(per_var, (w, coef, amp))
    count = NVAR * L
    index = jnp.arange(count, dtype=jnp.int32)
    same = (owner[:, None] == owner[None, :]) & (index[None, :] < index[:, None])
    slot = jnp.sum(same.astype(jnp.int32), axis=1).astype(jnp.int32)
    devices = N_LAT * N_LON
    flat = jnp.zeros((devices * CAP,), jnp.float32).at[owner * CAP + slot].set(energy.reshape(-1))
    slab_energy = flat.reshape(devices, CAP)
    z = jnp.einsum('vlk,vkij->vlij', vert, back, precision=highest) * sigma[:, None]
    out_chi = z[1] + chi_coef[:, None, None] * z[0]
    out_temp = z[2] + jnp.einsum('lk,kij->lij', bal_temp, laplace(z[0]), precision=highest)
    mixed = jnp.stack([z[0], out_chi, out_temp])
    applied = mixed.transpose(0, 2, 3, 1).reshape(NVAR, NLAT, NLON * L)
    return applied, slab_energy
```

```python
import functools

import jax
import jax.numpy as jnp
from jax import lax
from jax.experimental import pallas as pl
from jax.experimental.pallas import tpu as pltpu
from jax.sharding import PartitionSpec as P

F32 = jnp.float32
BF16 = jnp.bfloat16
MESH = pl.DeviceIdType.MESH


def split_product(x, w):
    hi = x.astype(BF16)
    lo = (x - hi.astype(F32)).astype(BF16)
    y = jnp.dot(jnp.concatenate([hi, lo], axis=1), w, preferred_element_type=F32)
    return y[:, :128] + y[:, 128:]


def swap(x):
    return pltpu.roll(x, 64, 1)


def rows_of(parts):
    return jnp.concatenate(parts, axis=0)


def kernel(
    dims,
    state_ref,
    sigma_ref,
    vert_ref,
    bal_ref,
    small_ref,
    out_ref,
    energy_ref,
    mats,
    pad,
    sig,
    temp,
    w,
    xs,
    xu,
    yf,
    ys,
    yu,
    xtab,
    ytab,
    edge_rows,
    halo_send,
    halo_recv,
    x_send,
    x_recv,
    x_back,
    x_home,
    y_send,
    y_recv,
    y_back,
    y_home,
    e_send,
    e_recv,
    f_send,
    f_recv,
    halo_ss,
    halo_rs,
    x_ss,
    x_rs,
    xb_ss,
    xb_rs,
    y_ss,
    y_rs,
    yb_ss,
    yb_rs,
    e_ss,
    e_rs,
    f_ss,
    f_rs,
):
    n_lat, n_lon, rows, cols = dims
    half = cols // 2
    jj_n = half // n_lat
    y_rows = 3 * jj_n * 4 + 4
    x_rows = 24
    v_base = (0, half + 8, 2 * half + 8)
    y_stride = 3 * half + 8
    la = lax.axis_index("lat")
    lo = lax.axis_index("lon")

    barrier = pltpu.get_barrier_semaphore()
    for o in range(1, n_lat):
        pl.semaphore_signal(barrier, inc=1, device_id=(lax.rem(la + o, n_lat), lo), device_id_type=MESH)
    for o in range(1, n_lon):
        pl.semaphore_signal(barrier, inc=1, device_id=(la, lax.rem(lo + o, n_lon)), device_id_type=MESH)

    lane = lax.broadcasted_iota(jnp.int32, (8, 128), 1)
    low1 = lane[:1] < 64

    def low(x):
        return jnp.broadcast_to(low1, x.shape)

    def pick(a, b):
        return jnp.where(low(a), a, b)

    small = small_ref[...]
    length = [small[v : v + 1] for v in range(3)]
    coupling = small[3:4]
    decay = [jnp.exp(-1.0 / r) for r in length]

    def power(v, k):
        return jnp.exp(-float(k) / length[v])

    def through(v, n):
        a = decay[v]
        return float(n) * power(v, n), a * (1.0 - power(v, 2 * n)) / (1.0 - a * a)

    def fill_table(ref, n):
        pos = lax.broadcasted_iota(jnp.int32, (n, 128), 0).astype(F32)
        for v in range(3):
            a, r = decay[v], length[v]
            first = jnp.exp(-(pos + 1.0) / r)
            tail = 1.0 - jnp.exp(-2.0 * (n - 1.0 - pos) / r)
            second = (pos + 1.0) * first + first * (a * a) * tail / (1.0 - a * a)
            ref[pl.ds(v * n, n), :] = first
            ref[pl.ds((3 + v) * n, n), :] = second

    fill_table(xtab, half)
    fill_table(ytab, rows)

    gain = []
    for v in range(3):
        a = decay[v]
        c = (1.0 - a) / (1.0 + a)
        gain.append(length[v] * jnp.sqrt(length[v]) * (c * c) * (c * c))

    def put_matrix(slot, m):
        pad[:, :64] = m
        top = pad[...]
        full = rows_of([top, swap(top)])
        hi = full.astype(BF16)
        low_part = (full - hi.astype(F32)).astype(BF16)
        mats[slot] = rows_of(
            [
                jnp.concatenate([hi, low_part], axis=1),
                jnp.concatenate([hi, jnp.zeros_like(hi)], axis=1),
            ]
        )

    pad[...] = jnp.zeros_like(pad)
    for v in range(3):
        put_matrix(v, vert_ref[v])
        put_matrix(3 + v, (vert_ref[v] * gain[v][:, :64]).T)
    put_matrix(6, bal_ref[...])
    put_matrix(7, bal_ref[...].T)

    for v in range(3):
        sig[pl.ds(v * rows, rows), :] = jnp.zeros((rows, 128), F32)
        sig[pl.ds(v * rows, rows), :cols] = sigma_ref[v]
    column = jnp.where(lax.broadcasted_iota(jnp.int32, (rows, 128), 1) < 64, 0, half)

    def spread(tile, j):
        return jnp.take_along_axis(tile, column + j, axis=1, mode="promise_in_bounds")

    def block(ref, at):
        return ref[pl.ds(pl.multiple_of(at, 8), rows), :]

    def put_block(ref, at, value):
        ref[pl.ds(pl.multiple_of(at, 8), rows), :] = value

    def pair(k, _):
        for v in range(3):
            n1 = state_ref[v, :, pl.ds(pl.multiple_of(k * 128, 128), 128)]
            n2 = state_ref[v, :, pl.ds(pl.multiple_of((k + half // 2) * 128, 128), 128)]
            even = pick(n1, swap(n2))
            odd = pick(swap(n1), n2)
            if v == 2:
                put_block(temp, (2 * k + 1) * rows, even)
                put_block(temp, (2 * k + 2) * rows, odd)
            else:
                put_block(w, (2 * k * 3 + v) * rows, even)
                put_block(w, ((2 * k + 1) * 3 + v) * rows, odd)
        return 0

    lax.fori_loop(0, half // 2, pair, 0)

    sig0 = sig[pl.ds(0, rows), :]
    msg_r, msg_c = half + rows, 2 * rows
    halo_send[pl.ds(0, half), :] = temp[pl.ds(rows, half, stride=rows), :]
    halo_send[pl.ds(half, rows), :] = sig0
    halo_send[pl.ds(msg_r, half), :] = temp[pl.ds(2 * rows - 1, half, stride=rows), :]
    halo_send[pl.ds(msg_r + half, rows), :] = sig0
    halo_send[pl.ds(2 * msg_r, rows), :] = temp[pl.ds(rows, rows), :]
    halo_send[pl.ds(2 * msg_r + rows, rows), :] = sig0
    halo_send[pl.ds(2 * msg_r + msg_c, rows), :] = temp[pl.ds(half * rows, rows), :]
    halo_send[pl.ds(2 * msg_r + msg_c + rows, rows), :] = sig0

    pl.semaphore_wait(barrier, n_lat + n_lon - 2)

    up = (lax.rem(la + n_lat - 1, n_lat), lo)
    down = (lax.rem(la + 1, n_lat), lo)
    left = (la, lax.rem(lo + n_lon - 1, n_lon))
    right = (la, lax.rem(lo + 1, n_lon))
    starts = (0, msg_r, 2 * msg_r, 2 * msg_r + msg_c)
    sizes = (msg_r, msg_r, msg_c, msg_c)
    halo = []
    for q, device in enumerate((up, down, left, right)):
        here = pl.ds(starts[q], sizes[q])
        copy = pltpu.make_async_remote_copy(
            src_ref=halo_send.at[here],
            dst_ref=halo_recv.at[here],
            send_sem=halo_ss.at[q],
            recv_sem=halo_rs.at[q],
            device_id=device,
            device_id_type=MESH,
        )
        copy.start()
        halo.append(copy)

    def batch(b):
        return [b * 8 + t for t in range(8)]

    def mix_in(b, _):
        js = batch(b)
        chi = [block(w, (j * 3 + 1) * rows) for j in js]
        for t, j in enumerate(js):
            at = j * 3 * rows
            put_block(w, at, block(w, at) + coupling * chi[t])
        for v, parts in ((1, chi), (2, [block(temp, (j + 1) * rows) for j in js])):
            y = split_product(rows_of(parts), mats[v])
            tile = sig[pl.ds(v * rows, rows), :]
            for t, j in enumerate(js):
                put_block(w, (j * 3 + v) * rows, y[t * rows : (t + 1) * rows] * spread(tile, j))
        return 0

    lax.fori_loop(0, half // 8, mix_in, 0)

    for copy in halo:
        copy.wait()
    has_up = jnp.where(la > 0, 1.0, 0.0).astype(F32)
    has_down = jnp.where(la < n_lat - 1, 1.0, 0.0).astype(F32)
    has_left = jnp.where(lo > 0, 1.0, 0.0).astype(F32)
    has_right = jnp.where(lo < n_lon - 1, 1.0, 0.0).astype(F32)
    edge_rows[pl.ds(0, half), :] = halo_recv[pl.ds(msg_r, half), :] * has_up
    edge_rows[pl.ds(half, half), :] = halo_recv[pl.ds(0, half), :] * has_down
    from_right = halo_recv[pl.ds(2 * msg_r, rows), :] * has_right
    from_left = halo_recv[pl.ds(2 * msg_r + msg_c, rows), :] * has_left

    def close_columns(lo_edge, hi_edge):
        put_block(temp, 0, pick(lo_edge, swap(temp[pl.ds(half * rows, rows), :])))
        put_block(temp, (half + 1) * rows, pick(swap(temp[pl.ds(rows, rows), :]), hi_edge))

    close_columns(swap(from_left), swap(from_right))
    row_id = lax.broadcasted_iota(jnp.int32, (rows, 128), 0)

    def laplace(j):
        x = block(temp, (j + 1) * rows)
        above = jnp.where(row_id == 0, edge_rows[pl.ds(j, 1), :], pltpu.roll(x, 1, 0))
        below = jnp.where(row_id == rows - 1, edge_rows[pl.ds(half + j, 1), :], pltpu.roll(x, rows - 1, 0))
        return 4.0 * x - above - below - block(temp, j * rows) - block(temp, (j + 2) * rows)

    def mix_psi(b, _):
        js = batch(b)
        y = split_product(rows_of([laplace(j) for j in js]), mats[6])
        y = y + rows_of([block(w, j * 3 * rows) for j in js])
        y = split_product(y, mats[0])
        for t, j in enumerate(js):
            put_block(w, j * 3 * rows, y[t * rows : (t + 1) * rows] * spread(sig0, j))
        return 0

    lax.fori_loop(0, half // 8, mix_psi, 0)

    def tall(per_v):
        return rows_of([jnp.broadcast_to(c, (rows, 128)) for c in per_v])

    ax = tall(decay)
    full = 3 * rows
    zero_x = jnp.zeros((full, 128), F32)

    def line(ref, j):
        return ref[pl.ds(pl.multiple_of(j * full, 8), full), :]

    def put_line(ref, j, value):
        ref[pl.ds(pl.multiple_of(j * full, 8), full), :] = value

    def x_forward(src):
        def step(j, s):
            s = ax * s + line(src, j)
            put_line(xs, j, s)
            return s

        return lax.fori_loop(0, half, step, zero_x, unroll=4)

    def x_backward(src, dst):
        def step(q, t):
            j = half - 1 - q
            t = ax * t
            put_line(dst, j, line(xs, j) + t)
            return line(src, j) + t

        return lax.fori_loop(0, half, step, zero_x, unroll=4)

    s1 = x_forward(w)
    t1 = x_backward(w, xu)
    s2 = x_forward(xu)
    t2 = x_backward(xu, xs)

    ah = tall([power(v, half) for v in range(3)])
    g1 = tall([through(v, half)[0] for v in range(3)])
    g2 = tall([through(v, half)[1] for v in range(3)])
    s1r, t1r, s2r, t2r = swap(s1), swap(t1), swap(s2), swap(t2)
    q0 = pick(ah * s1 + s1r, s2 + g1 * s1r + ah * (s2r + g2 * t1))
    q1 = pick(t1 + ah * t1r, t2r + g1 * t1 + ah * (t2 + g2 * s1r))
    groups = rows // 8

    for i, q in enumerate((q0, q1)):
        for v in range(3):
            for g in range(groups):
                at = v * rows + g * 8
                x_send[pl.ds((v * groups + g) * 2 + i, 8, stride=x_rows), :] = q[at : at + 8]

    def exchange(axis, me, n, size, src, dst, ss, rs):
        copies = []
        for o in range(1, n):
            other = lax.rem(me + o, n)
            device = (other, lo) if axis == "lat" else (la, other)
            copy = pltpu.make_async_remote_copy(
                src_ref=src.at[pl.ds(pl.multiple_of(other * size, 8), size)],
                dst_ref=dst.at[pl.ds(pl.multiple_of(me * size, 8), size)],
                send_sem=ss.at[other],
                recv_sem=rs.at[me],
                device_id=device,
                device_id_type=MESH,
            )
            copy.start()
            copies.append(copy)
        mine = pl.ds(pl.multiple_of(me * size, 8), size)
        dst[mine, :] = src[mine, :]
        return copies

    def arrive(axis, me, n, size, src, dst, ss, rs):
        for o in range(1, n):
            other = lax.rem(me + o, n)
            device = (other, lo) if axis == "lat" else (la, other)
            pltpu.make_async_remote_copy(
                src_ref=src.at[pl.ds(pl.multiple_of(other * size, 8), size)],
                dst_ref=dst.at[pl.ds(pl.multiple_of(other * size, 8), size)],
                send_sem=ss.at[other],
                recv_sem=rs.at[other],
                device_id=device,
                device_id_type=MESH,
            ).wait_recv()

    def sent(copies):
        for copy in copies:
            copy.wait_send()

    xa = ("lon", lo, n_lon, x_rows, x_send, x_recv, x_ss, x_rs)
    out_going = exchange(*xa)
    arrive(*xa)

    def by_row(count, jumps, per_v):
        r = lax.broadcasted_iota(jnp.int32, (count, 128), 0)
        out = jnp.broadcast_to(per_v[0], (count, 128))
        for v in (1, 2):
            inside = (r >= v * jumps) & (r < (v + 1) * jumps)
            out = jnp.where(inside, jnp.broadcast_to(per_v[v], (count, 128)), out)
        return out

    def scan_states(n, s, t, an, a):
        s_in, total = [], jnp.zeros_like(s[0])
        for e in range(n):
            s_in.append(total)
            total = an * total + s[e]
        t_in, total = [None] * n, -a * total
        for e in reversed(range(n)):
            t_in[e] = total
            total = t[e] + an * total
        return s_in, t_in

    cx = 3 * groups
    a_r = by_row(cx, groups, decay)
    an_r = by_row(cx, groups, [power(v, cols) for v in range(3)])
    g1_r = by_row(cx, groups, [through(v, cols)[0] for v in range(3)])
    g2_r = by_row(cx, groups, [through(v, cols)[1] for v in range(3)])
    p0 = [x_recv[pl.ds(e * x_rows, cx, stride=2), :] for e in range(n_lon)]
    p1 = [x_recv[pl.ds(e * x_rows + 1, cx, stride=2), :] for e in range(n_lon)]
    s_in, t_in = scan_states(n_lon, p0, p1, an_r, a_r)
    sr = [swap(x) for x in s_in]
    tr = [swap(x) for x in t_in]
    s_in2, t_in2 = scan_states(
        n_lon,
        [p0[e] + g1_r * sr[e] + g2_r * tr[e] for e in range(n_lon)],
        [p1[e] + g1_r * tr[e] + g2_r * sr[e] for e in range(n_lon)],
        an_r,
        a_r,
    )
    for e in range(n_lon):
        x_back[pl.ds(e * x_rows, cx, stride=2), :] = pick(s_in[e], s_in2[e])
        x_back[pl.ds(e * x_rows + 1, cx, stride=2), :] = pick(t_in[e], t_in2[e])

    xb = ("lon", lo, n_lon, x_rows, x_back, x_home, xb_ss, xb_rs)
    out_going += exchange(*xb)
    arrive(*xb)

    def home(i):
        return rows_of(
            [
                x_home[pl.ds((v * groups + g) * 2 + i, 8, stride=x_rows), :]
                for v in range(3)
                for g in range(groups)
            ]
        )

    q0, q1 = home(0), home(1)
    q0r, q1r = swap(q0), swap(q1)
    si, s2i = pick(q0, q0r), pick(q0r, q0)
    ti, t2i = pick(q1, q1r), pick(q1r, q1)
    s_en = pick(si, s1r + ah * si)
    t_en = pick(t1r + ah * ti, ti)
    s_own = s2 + g1 * s_en + g2 * t_en
    t_own = t2 + g1 * t_en + g2 * s_en
    s2_en = pick(s2i, swap(s_own) + ah * s2i)
    t2_en = pick(swap(t_own) + ah * t2i, t2i)
    side = pick(s2i + ax * (t_own + ah * t2_en), ax * (s_own + ah * s2_en) + t2i)[:rows]
    yf[pl.ds(half, rows, stride=y_stride), :] = side
    for z in range(1, 8):
        yf[pl.ds(half + z, rows, stride=y_stride), :] = jnp.zeros((rows, 128), F32)

    xu[pl.ds(0, full), :] = s_en
    xu[pl.ds(full, full), :] = t_en
    xu[pl.ds(2 * full, full), :] = s2_en
    xu[pl.ds(3 * full, full), :] = t2_en

    def x_correct(j, _):
        for v in range(3):
            f0 = xtab[pl.ds(v * half + j, 1), :]
            b0 = xtab[pl.ds(v * half + half - 1 - j, 1), :]
            f1 = xtab[pl.ds((3 + v) * half + j, 1), :]
            b1 = xtab[pl.ds((3 + v) * half + half - 1 - j, 1), :]
            at = v * rows
            value = block(xs, j * full + at)
            value = value + xu[pl.ds(at, rows), :] * f1 + xu[pl.ds(full + at, rows), :] * b1
            value = value + xu[pl.ds(2 * full + at, rows), :] * f0 + xu[pl.ds(3 * full + at, rows), :] * b0
            yf[pl.ds(v_base[v] + j, rows, stride=y_stride), :] = value
        return 0

    lax.fori_loop(0, half, x_correct, 0, unroll=2)

    heights = (half + 8, half, half)

    def y_line(ref, i, v):
        return ref[pl.ds(pl.multiple_of(i * y_stride + v_base[v], 8), heights[v]), :]

    def put_y(ref, i, v, value):
        ref[pl.ds(pl.multiple_of(i * y_stride + v_base[v], 8), heights[v]), :] = value

    zero_y = tuple(jnp.zeros((h, 128), F32) for h in heights)

    def y_forward(src):
        def step(i, s):
            new = []
            for v in range(3):
                x = decay[v] * s[v] + y_line(src, i, v)
                put_y(ys, i, v, x)
                new.append(x)
            return tuple(new)

        return lax.fori_loop(0, rows, step, zero_y, unroll=2)

    def y_backward(src, dst):
        def step(q, t):
            i = rows - 1 - q
            new = []
            for v in range(3):
                x = decay[v] * t[v]
                put_y(dst, i, v, y_line(ys, i, v) + x)
                new.append(y_line(src, i, v) + x)
            return tuple(new)

        return lax.fori_loop(0, rows, step, zero_y, unroll=2)

    y_s1 = y_forward(yf)
    y_t1 = y_backward(yf, yu)
    y_s2 = y_forward(yu)
    y_t2 = y_backward(yu, ys)

    for k, states in enumerate((y_s1, y_t1, y_s2, y_t2)):
        for v in range(3):
            for q in range(jj_n):
                y_send[pl.ds((v * jj_n + q) * 4 + k, n_lat, stride=y_rows), :] = states[v][
                    q * n_lat : (q + 1) * n_lat
                ]
        last = 3 * jj_n * 4 + k
        y_send[pl.ds(last, n_lat, stride=y_rows), :] = jnp.zeros((n_lat, 128), F32)
        y_send[pl.ds(last, 1), :] = states[0][half : half + 1]

    ya = ("lat", la, n_lat, y_rows, y_send, y_recv, y_ss, y_rs)
    out_going += exchange(*ya)
    arrive(*ya)

    cy = 3 * jj_n + 1
    a_r = by_row(cy, jj_n, decay)
    an_r = by_row(cy, jj_n, [power(v, rows) for v in range(3)])
    g1_r = by_row(cy, jj_n, [through(v, rows)[0] for v in range(3)])
    g2_r = by_row(cy, jj_n, [through(v, rows)[1] for v in range(3)])

    def got(k):
        return [y_recv[pl.ds(e * y_rows + k, cy, stride=4), :] for e in range(n_lat)]

    s_in, t_in = scan_states(n_lat, got(0), got(1), an_r, a_r)
    for e in range(n_lat):
        y_back[pl.ds(e * y_rows, cy, stride=4), :] = s_in[e]
        y_back[pl.ds(e * y_rows + 1, cy, stride=4), :] = t_in[e]
    p2, p3 = got(2), got(3)
    s_in2, t_in2 = scan_states(
        n_lat,
        [p2[e] + g1_r * s_in[e] + g2_r * t_in[e] for e in range(n_lat)],
        [p3[e] + g1_r * t_in[e] + g2_r * s_in[e] for e in range(n_lat)],
        an_r,
        a_r,
    )
    for e in range(n_lat):
        y_back[pl.ds(e * y_rows + 2, cy, stride=4), :] = s_in2[e]
        y_back[pl.ds(e * y_rows + 3, cy, stride=4), :] = t_in2[e]

    yb = ("lat", la, n_lat, y_rows, y_back, y_home, yb_ss, yb_rs)
    out_going += exchange(*yb)
    arrive(*yb)

    def y_entering(v, k):
        parts = [
            y_home[pl.ds((v * jj_n + q) * 4 + k, n_lat, stride=y_rows), :] for q in range(jj_n)
        ]
        if v == 0:
            last = 3 * jj_n * 4 + k
            parts.append(jnp.broadcast_to(y_home[pl.ds(last, 1), :], (8, 128)))
        return rows_of(parts)

    for v in range(3):
        s_en, t_en, s2_en, t2_en = (y_entering(v, k) for k in range(4))
        if v == 0:
            g1v, g2v = through(0, rows)
            an = power(0, rows)
            first = s2_en + decay[0] * (y_t2[0] + g1v * t_en + g2v * s_en + an * t2_en)
            after = decay[0] * (y_s2[0] + g1v * s_en + g2v * t_en + an * s2_en) + t2_en
            edge_rows[pl.ds(0, half), :] = first[:half]
            edge_rows[pl.ds(half, half), :] = after[:half]

        def y_correct(i, _, v=v, s_en=s_en, t_en=t_en, s2_en=s2_en, t2_en=t2_en):
            f0 = ytab[pl.ds(v * rows + i, 1), :]
            b0 = ytab[pl.ds(v * rows + rows - 1 - i, 1), :]
            f1 = ytab[pl.ds((3 + v) * rows + i, 1), :]
            b1 = ytab[pl.ds((3 + v) * rows + rows - 1 - i, 1), :]
            value = y_line(ys, i, v) + s_en * f1 + t_en * b1
            put_y(yf, i, v, value + s2_en * f0 + t2_en * b0)
            return 0

        lax.fori_loop(0, rows, y_correct, 0)

    def mix_out(b, acc):
        js = batch(b)
        acc = list(acc)
        z0 = None
        for v in range(3):
            parts = []
            for j in js:
                x = yf[pl.ds(v_base[v] + j, rows, stride=y_stride), :]
                acc[v] = acc[v] + x * block(w, (j * 3 + v) * rows)
                parts.append(x)
            y = split_product(rows_of(parts), mats[3 + v])
            tile = sig[pl.ds(v * rows, rows), :]
            zs = [y[t * rows : (t + 1) * rows] * spread(tile, j) for t, j in enumerate(js)]
            for t, j in enumerate(js):
                if v == 0:
                    put_block(temp, (j + 1) * rows, zs[t])
                elif v == 1:
                    put_block(w, (j * 3 + 1) * rows, zs[t] + coupling * z0[t])
                else:
                    put_block(w, (j * 3 + 2) * rows, zs[t])
            if v == 0:
                z0 = zs
        return tuple(acc)

    zero_b = jnp.zeros((rows, 128), F32)
    acc = lax.fori_loop(0, half // 8, mix_out, (zero_b, zero_b, zero_b))

    e_send[...] = jnp.zeros_like(e_send)
    for v in range(3):
        e_send[pl.ds(v, 1), :] = jnp.sum(acc[v], axis=0, keepdims=True)

    def gather_start(axis, me, n, src, dst, ss, rs):
        copies = []
        for o in range(1, n):
            other = lax.rem(me + o, n)
            device = (other, lo) if axis == "lat" else (la, other)
            copy = pltpu.make_async_remote_copy(
                src_ref=src,
                dst_ref=dst.at[pl.ds(pl.multiple_of(me * 8, 8), 8)],
                send_sem=ss.at[other],
                recv_sem=rs.at[me],
                device_id=device,
                device_id_type=MESH,
            )
            copy.start()
            copies.append(copy)
        dst[pl.ds(pl.multiple_of(me * 8, 8), 8), :] = src[...]
        return copies

    def gather_sum(axis, me, n, src, dst, ss, rs):
        for o in range(1, n):
            other = lax.rem(me + o, n)
            device = (other, lo) if axis == "lat" else (la, other)
            pltpu.make_async_remote_copy(
                src_ref=src,
                dst_ref=dst.at[pl.ds(pl.multiple_of(other * 8, 8), 8)],
                send_sem=ss.at[other],
                recv_sem=rs.at[other],
                device_id=device,
                device_id_type=MESH,
            ).wait_recv()
        total = dst[pl.ds(0, 8), :]
        for e in range(1, n):
            total = total + dst[pl.ds(e * 8, 8), :]
        return total

    ea = ("lat", la, n_lat, e_send, e_recv, e_ss, e_rs)
    out_going += gather_start(*ea)

    sig_down = halo_recv[pl.ds(half, rows), :] * has_down
    sig_up = halo_recv[pl.ds(msg_r + half, rows), :] * has_up
    sig_right = halo_recv[pl.ds(2 * msg_r + rows, rows), :] * has_right
    sig_left = halo_recv[pl.ds(2 * msg_r + msg_c + rows, rows), :] * has_left
    wide = jnp.broadcast_to(low1, (half, 128))

    def row_sigma(tile, r):
        t = jnp.concatenate([tile, jnp.zeros((128 - rows, 128), F32)], axis=0).T
        a = jnp.broadcast_to(t[:half, r : r + 1], (half, 128))
        b = jnp.broadcast_to(t[half : 2 * half, r : r + 1], (half, 128))
        return jnp.where(wide, a, b)

    edges = split_product(
        rows_of([edge_rows[...], yf[pl.ds(half, rows, stride=y_stride), :]]), mats[3]
    )
    edge_rows[pl.ds(0, half), :] = edges[:half] * row_sigma(sig_up, rows - 1)
    edge_rows[pl.ds(half, half), :] = edges[half : 2 * half] * row_sigma(sig_down, 0)
    lane_r = lax.broadcasted_iota(jnp.int32, (rows, 128), 1)
    side_sig = jnp.where(
        lane_r < 64,
        jnp.take_along_axis(sig_left, jnp.full((rows, 128), cols - 1), axis=1, mode="promise_in_bounds"),
        jnp.take_along_axis(sig_right, jnp.zeros((rows, 128), jnp.int32), axis=1, mode="promise_in_bounds"),
    )
    side = edges[2 * half :] * side_sig
    close_columns(side, side)

    def unpair(v, js, values):
        for t in range(0, len(js), 2):
            even, odd = values[t], values[t + 1]
            k = lax.div(js[t], 2)
            out_ref[v, :, pl.ds(pl.multiple_of(k * 128, 128), 128)] = pick(even, swap(odd))
            out_ref[v, :, pl.ds(pl.multiple_of((k + half // 2) * 128, 128), 128)] = pick(swap(even), odd)

    def finish(b, _):
        js = batch(b)
        y = split_product(rows_of([laplace(j) for j in js]), mats[7])
        unpair(0, js, [block(temp, (j + 1) * rows) for j in js])
        unpair(1, js, [block(w, (j * 3 + 1) * rows) for j in js])
        unpair(
            2,
            js,
            [y[t * rows : (t + 1) * rows] + block(w, (j * 3 + 2) * rows) for t, j in enumerate(js)],
        )
        return 0

    lax.fori_loop(0, half // 8, finish, 0)

    f_send[...] = gather_sum(*ea)
    fa = ("lon", lo, n_lon, f_send, f_recv, f_ss, f_rs)
    out_going += gather_start(*fa)
    total = gather_sum(*fa)
    total = total + swap(total)

    rank = (la * n_lon + lo).astype(F32)
    keep = lane[:1] < 64
    strict = (
        lax.broadcasted_iota(jnp.int32, (128, 128), 0) < lax.broadcasted_iota(jnp.int32, (128, 128), 1)
    ).astype(F32)
    before = jnp.zeros((1, 1), F32)
    outs = [jnp.zeros((1, 1), F32)] * 3
    scale = 1.0 / float(rows * n_lat * cols * n_lon)
    for v in range(3):
        mine = jnp.where(keep & (small[4 + v : 5 + v] == rank), 1.0, 0.0)
        slot = jnp.dot(jnp.broadcast_to(mine, (8, 128)), strict, preferred_element_type=F32)[:1] + before
        before = before + jnp.sum(mine, axis=1, keepdims=True)
        value = total[v : v + 1] * gain[v] * scale * mine
        for k in range(3):
            outs[k] = outs[k] + jnp.sum(jnp.where(slot == float(k), value, 0.0), axis=1, keepdims=True)
    l8 = lane[:1]
    row = jnp.where(l8 == 0, outs[0], jnp.where(l8 == 1, outs[1], outs[2]))
    energy_ref[...] = row

    sent(out_going)


def shards(state, sigma, vert, bal_temp, chi_coef, scales, classes, owner):
    n_lat = lax.axis_size("lat")
    n_lon = lax.axis_size("lon")
    rows, cols = state.shape[1], sigma.shape[2]
    half = cols // 2
    ids = jnp.arange(scales.shape[0], dtype=jnp.int32)
    length = jnp.sum(jnp.where(classes[:, None] == ids[None, :], scales[None, :], 0.0), axis=1)
    small = jnp.concatenate(
        [length.reshape(3, 64), chi_coef.reshape(1, 64), owner.astype(F32).reshape(3, 64), jnp.ones((1, 64), F32)]
    )
    small = jnp.concatenate([small, small], axis=1)
    jj_n = half // n_lat
    y_rows = 3 * jj_n * 4 + 4
    y_stride = 3 * half + 8
    halo_rows = 2 * (half + rows) + 4 * rows
    vm = lambda r, d=F32: pltpu.VMEM((r, 128), d)
    dma = lambda n: pltpu.SemaphoreType.DMA((n,))
    body = functools.partial(kernel, (n_lat, n_lon, rows, cols))
    spec = pl.BlockSpec(memory_space=pltpu.VMEM)
    applied, energy = pl.pallas_call(
        body,
        out_shape=(
            jax.ShapeDtypeStruct(state.shape, F32),
            jax.ShapeDtypeStruct((1, 128), F32),
        ),
        in_specs=[spec] * 5,
        out_specs=(spec, spec),
        scratch_shapes=[
            pltpu.VMEM((8, 256, 256), BF16),
            vm(64),
            vm(3 * rows),
            vm((half + 2) * rows),
            vm(half * 3 * rows),
            vm(half * 3 * rows),
            vm(half * 3 * rows),
            vm(rows * y_stride),
            vm(rows * y_stride),
            vm(rows * y_stride),
            vm(6 * half),
            vm(6 * rows),
            vm(2 * half),
            vm(halo_rows),
            vm(halo_rows),
            vm(n_lon * 24),
            vm(n_lon * 24),
            vm(n_lon * 24),
            vm(n_lon * 24),
            vm(n_lat * y_rows),
            vm(n_lat * y_rows),
            vm(n_lat * y_rows),
            vm(n_lat * y_rows),
            vm(8),
            vm(8 * n_lat),
            vm(8),
            vm(8 * n_lon),
            dma(4),
            dma(4),
        ]
        + [dma(n_lon)] * 4
        + [dma(n_lat)] * 6
        + [dma(n_lon)] * 2,
        compiler_params=pltpu.CompilerParams(
            collective_id=0, has_side_effects=True, vmem_limit_bytes=56 * 1024 * 1024
        ),
    )(state, sigma, vert, bal_temp, small)
    return applied, energy[:, :3]


def solution(mesh):
    return jax.shard_map(
        shards,
        mesh=mesh,
        in_specs=(P(None, "lat", "lon"), P(None, "lat", "lon"), P(), P(), P(), P(), P(), P()),
        out_specs=(P(None, "lat", "lon"), P(("lat", "lon"), None)),
        check_vma=False,
    )
```

```python
import functools

import jax
import jax.numpy as jnp
from jax import lax
from jax.experimental import pallas as pl
from jax.experimental.pallas import tpu as pltpu
from jax.sharding import PartitionSpec as P

F32 = jnp.float32
BF16 = jnp.bfloat16
MESH = pl.DeviceIdType.MESH


def split_product(x, w):
    hi = x.astype(BF16)
    lo = (x - hi.astype(F32)).astype(BF16)
    y = jnp.dot(jnp.concatenate([hi, lo], axis=1), w, preferred_element_type=F32)
    return y[:, :128] + y[:, 128:]


def swap(x):
    return pltpu.roll(x, 64, 1)


def rows_of(parts):
    return jnp.concatenate(parts, axis=0)


def layout(n_lat, n_lon, rows, cols, n_class):
    half = cols // 2
    jj_n = half // n_lat
    groups = rows // 8
    spec = {}
    for c, count in enumerate((1, 2)):
        spec[f"x_rows{c}"] = -(-count * groups * 2 // 8) * 8
        spec[f"y_rows{c}"] = -(-(count * jj_n * 4 + (4 if c == 0 else 0)) // 8) * 8
        spec[f"y_stride{c}"] = count * half + (8 if c == 0 else 0)
    shapes = {
        "in_sem": 3,
        "small_sem": 7,
        "halo_ss": 4,
        "halo_rs": 4,
        "e_ss": 1,
        "e_rs": 1,
        "f_ss": 1,
        "f_rs": 1,
    }
    for name in shapes:
        shapes[name] = pltpu.SemaphoreType.DMA((shapes[name],))
    vm = lambda r: pltpu.VMEM((r, 128), F32)
    shapes["state"] = pltpu.VMEM((3, rows, cols * 64), F32)
    shapes["sigma"] = pltpu.VMEM((3, rows, cols), F32)
    shapes["vert"] = pltpu.VMEM((3, 64, 64), F32)
    shapes["bal"] = pltpu.VMEM((64, 64), F32)
    shapes["chi"] = pltpu.VMEM((1, 64), F32)
    shapes["scales"] = pltpu.VMEM((1, n_class), F32)
    shapes["classes"] = pltpu.VMEM((1, 192), jnp.int32)
    shapes["owner"] = pltpu.VMEM((1, 192), jnp.int32)
    shapes["mats"] = pltpu.VMEM((8, 256, 256), BF16)
    sizes = {
        "table": 8,
        "pad": 64,
        "sig": 3 * rows,
        "temp": (half + 2) * rows,
        "xtab": 6 * half,
        "ytab": 6 * rows,
        "edge_rows": 2 * half,
        "halo_send": 2 * (half + rows) + 4 * rows,
        "halo_recv": 2 * (half + rows) + 4 * rows,
        "e_send": 8,
        "e_recv": 8 * n_lat,
        "f_send": 8,
        "f_recv": 8 * n_lon,
    }
    for c, count in enumerate((1, 2)):
        for name in ("w", "xs", "xt", "xu", "xv"):
            sizes[f"{name}{c}"] = half * count * rows
        sizes[f"xe{c}"] = 4 * count * rows
        for name in ("yf", "ys", "yt", "yv", "yu"):
            sizes[f"{name}{c}"] = rows * spec[f"y_stride{c}"]
        for name in ("send", "recv", "back", "home"):
            sizes[f"x_{name}{c}"] = n_lon * spec[f"x_rows{c}"]
            sizes[f"y_{name}{c}"] = n_lat * spec[f"y_rows{c}"]
        for name in ("ss", "rs", "bss", "brs"):
            shapes[f"x_{name}{c}"] = pltpu.SemaphoreType.DMA((1,))
            shapes[f"y_{name}{c}"] = pltpu.SemaphoreType.DMA((1,))
    for name, size in sizes.items():
        shapes[name] = vm(size)
    return spec, shapes


CHUNKS = ((0,), (1, 2))


class Names:
    def __init__(self, names, refs):
        for name, ref in zip(names, refs):
            setattr(self, name, ref)

    def at(self, name, c):
        return getattr(self, f"{name}{c}")


def kernel(
    dims,
    spec,
    names,
    state_hbm,
    sigma_hbm,
    vert_hbm,
    bal_hbm,
    chi_hbm,
    scales_hbm,
    class_hbm,
    owner_hbm,
    out_ref,
    energy_ref,
    *refs,
):
    n_lat, n_lon, rows, cols = dims
    half = cols // 2
    jj_n = half // n_lat
    groups = rows // 8
    R = Names(names, refs)
    state_ref, table, mats, pad, sig, temp = R.state, R.table, R.mats, R.pad, R.sig, R.temp
    xtab, ytab, edge_rows = R.xtab, R.ytab, R.edge_rows
    halo_send, halo_recv = R.halo_send, R.halo_recv
    la = lax.axis_index("lat")
    lo = lax.axis_index("lon")

    barrier = pltpu.get_barrier_semaphore()
    for o in range(1, n_lat):
        pl.semaphore_signal(barrier, inc=1, device_id=(lax.rem(la + o, n_lat), lo), device_id_type=MESH)
    for o in range(1, n_lon):
        pl.semaphore_signal(barrier, inc=1, device_id=(la, lax.rem(lo + o, n_lon)), device_id_type=MESH)

    sigma_ref, vert_ref, bal_ref = R.sigma, R.vert, R.bal
    chi_ref, scales_ref, class_ref, owner_ref = R.chi, R.scales, R.classes, R.owner
    small = []
    for i, (src, dst) in enumerate(
        (
            (class_hbm, class_ref),
            (scales_hbm, scales_ref),
            (vert_hbm, vert_ref),
            (bal_hbm, bal_ref),
            (sigma_hbm, sigma_ref),
            (chi_hbm, chi_ref),
            (owner_hbm, owner_ref),
        )
    ):
        small.append(pltpu.make_async_copy(src, dst, R.small_sem.at[i]))
        small[-1].start()
    loads = {}
    for v in (2, 1, 0):
        loads[v] = pltpu.make_async_copy(state_hbm.at[v], state_ref.at[v], R.in_sem.at[v])
        loads[v].start()

    lane = lax.broadcasted_iota(jnp.int32, (8, 128), 1)
    low1 = lane[:1] < 64

    def low(x):
        return jnp.broadcast_to(low1, x.shape)

    def pick(a, b):
        return jnp.where(low(a), a, b)

    for copy in small:
        copy.wait()

    table[...] = jnp.zeros_like(table)

    def levels(row):
        table[0:1, :] = row[:, :128]
        table[1:2, :64] = row[:, 128:]
        pair01 = table[...]
        flip01 = swap(pair01)
        first, second = pick(pair01, flip01), pick(flip01, pair01)
        return [first[0:1], second[0:1], first[1:2]]

    classes = class_ref[...]
    lengths = jnp.zeros(classes.shape, F32)
    for c in range(scales_ref.shape[1]):
        lengths = jnp.where(classes == c, scales_ref[:, c : c + 1], lengths)
    length = levels(lengths)
    owners = levels(owner_ref[...].astype(F32))
    table[0:1, :64] = chi_ref[...]
    coupling = table[...]
    coupling = pick(coupling, swap(coupling))[0:1]
    decay = [jnp.exp(-1.0 / r) for r in length]

    def power(v, k):
        return jnp.exp(-float(k) / length[v])

    def through(v, n):
        a = decay[v]
        return float(n) * power(v, n), a * (1.0 - power(v, 2 * n)) / (1.0 - a * a)

    def fill_table(ref, n):
        pos = lax.broadcasted_iota(jnp.int32, (n, 128), 0).astype(F32)
        for v in range(3):
            a, r = decay[v], length[v]
            first = jnp.exp(-(pos + 1.0) / r)
            tail = 1.0 - jnp.exp(-2.0 * (n - 1.0 - pos) / r)
            second = (pos + 1.0) * first + first * (a * a) * tail / (1.0 - a * a)
            ref[pl.ds(v * n, n), :] = first
            ref[pl.ds((3 + v) * n, n), :] = second

    fill_table(xtab, half)
    fill_table(ytab, rows)

    gain = []
    for v in range(3):
        a = decay[v]
        c = (1.0 - a) / (1.0 + a)
        gain.append(length[v] * jnp.sqrt(length[v]) * (c * c) * (c * c))

    def put_matrix(slot, m):
        pad[:, :64] = m
        top = pad[...]
        full = rows_of([top, swap(top)])
        hi = full.astype(BF16)
        low_part = (full - hi.astype(F32)).astype(BF16)
        mats[slot] = rows_of(
            [
                jnp.concatenate([hi, low_part], axis=1),
                jnp.concatenate([hi, jnp.zeros_like(hi)], axis=1),
            ]
        )

    pad[...] = jnp.zeros_like(pad)
    for v in range(3):
        put_matrix(v, vert_ref[v])
        put_matrix(3 + v, (vert_ref[v] * gain[v][:, :64]).T)
    put_matrix(6, bal_ref[...])
    put_matrix(7, bal_ref[...].T)

    for v in range(3):
        sig[pl.ds(v * rows, rows), :] = jnp.zeros((rows, 128), F32)
        sig[pl.ds(v * rows, rows), :cols] = sigma_ref[v]
    column = jnp.where(lax.broadcasted_iota(jnp.int32, (rows, 128), 1) < 64, 0, half)

    def spread(tile, j):
        return jnp.take_along_axis(tile, column + j, axis=1, mode="promise_in_bounds")

    def block(ref, at):
        return ref[pl.ds(pl.multiple_of(at, 8), rows), :]

    def put_block(ref, at, value):
        ref[pl.ds(pl.multiple_of(at, 8), rows), :] = value


    def pair(v):
        def step(k, _):
            at1 = pl.ds(pl.multiple_of(k * 128, 128), 128)
            at2 = pl.ds(pl.multiple_of((k + half // 2) * 128, 128), 128)
            n1, n2 = state_ref[v, :, at1], state_ref[v, :, at2]
            if v == 0:
                n1 = n1 + coupling * state_ref[1, :, at1]
                n2 = n2 + coupling * state_ref[1, :, at2]
            even = pick(n1, swap(n2))
            odd = pick(swap(n1), n2)
            if v == 2:
                put_block(temp, (2 * k + 1) * rows, even)
                put_block(temp, (2 * k + 2) * rows, odd)
            elif v == 1:
                put_block(R.w1, 4 * k * rows, even)
                put_block(R.w1, (4 * k + 2) * rows, odd)
            else:
                put_block(R.w0, 2 * k * rows, even)
                put_block(R.w0, (2 * k + 1) * rows, odd)
            return 0

        lax.fori_loop(0, half // 2, step, 0, unroll=4)

    def batch(b):
        return [b * 8 + t for t in range(8)]

    def w_at(v, j):
        return j * rows if v == 0 else (2 * j + v - 1) * rows

    def w_ref(v):
        return R.w0 if v == 0 else R.w1

    loads[2].wait()
    pair(2)

    sig0 = sig[pl.ds(0, rows), :]
    msg_r, msg_c = half + rows, 2 * rows
    halo_send[pl.ds(0, half), :] = temp[pl.ds(rows, half, stride=rows), :]
    halo_send[pl.ds(half, rows), :] = sig0
    halo_send[pl.ds(msg_r, half), :] = temp[pl.ds(2 * rows - 1, half, stride=rows), :]
    halo_send[pl.ds(msg_r + half, rows), :] = sig0
    halo_send[pl.ds(2 * msg_r, rows), :] = temp[pl.ds(rows, rows), :]
    halo_send[pl.ds(2 * msg_r + rows, rows), :] = sig0
    halo_send[pl.ds(2 * msg_r + msg_c, rows), :] = temp[pl.ds(half * rows, rows), :]
    halo_send[pl.ds(2 * msg_r + msg_c + rows, rows), :] = sig0

    loads[1].wait()
    pair(1)

    def mix_in(b, _):
        js = batch(b)
        chi = [block(R.w1, w_at(1, j)) for j in js]
        for v, parts in ((1, chi), (2, [block(temp, (j + 1) * rows) for j in js])):
            y = split_product(rows_of(parts), mats[v])
            tile = sig[pl.ds(v * rows, rows), :]
            for t, j in enumerate(js):
                put_block(R.w1, w_at(v, j), y[t * rows : (t + 1) * rows] * spread(tile, j))
        return 0

    lax.fori_loop(0, half // 8, mix_in, 0, unroll=True)

    def tall(per_v):
        return rows_of([jnp.broadcast_to(c, (rows, 128)) for c in per_v])

    def both_ways(n, load, put_s, put_t, times, start):
        def step(q, carry):
            s, t = carry
            r = n - 1 - q
            s = [x + p for x, p in zip(times(s), load(q))]
            put_s(q, s)
            m = times(t)
            put_t(r, m)
            t = [x + p for x, p in zip(m, load(r))]
            return tuple(s), tuple(t)

        return lax.fori_loop(0, n, step, (start, start), unroll=4)

    def x_filter(c):
        vs = CHUNKS[c]
        full = len(vs) * rows
        ax = tall([decay[v] for v in vs])

        def line(ref, j):
            return ref[pl.ds(pl.multiple_of(j * full, 8), full), :]

        def put(ref):
            def go(j, value):
                ref[pl.ds(pl.multiple_of(j * full, 8), full), :] = value[0]

            return go

        w, xs, xt, xu, xv = (R.at(n, c) for n in ("w", "xs", "xt", "xu", "xv"))
        zero = (jnp.zeros((full, 128), F32),)
        times = lambda s: [ax * s[0]]
        (s1,), (t1,) = both_ways(half, lambda j: [line(w, j)], put(xs), put(xt), times, zero)
        second = lambda j: [line(xs, j) + line(xt, j)]
        (s2,), (t2,) = both_ways(half, second, put(xu), put(xv), times, zero)

        ah = tall([power(v, half) for v in vs])
        g1 = tall([through(v, half)[0] for v in vs])
        g2 = tall([through(v, half)[1] for v in vs])
        s1r, t1r, s2r, t2r = swap(s1), swap(t1), swap(s2), swap(t2)
        q0 = pick(ah * s1 + s1r, s2 + g1 * s1r + ah * (s2r + g2 * t1))
        q1 = pick(t1 + ah * t1r, t2r + g1 * t1 + ah * (t2 + g2 * s1r))
        send = R.at("x_send", c)
        for i, q in enumerate((q0, q1)):
            for g in range(full // 8):
                send[pl.ds(g * 2 + i, 8, stride=spec[f"x_rows{c}"]), :] = q[g * 8 : g * 8 + 8]
        return dict(s1r=s1r, t1r=t1r, s2=s2, t2=t2, ah=ah, g1=g1, g2=g2, ax=ax)

    def remote(axis, other, src, dst, ss, rs):
        device = (other, lo) if axis == "lat" else (la, other)
        return pltpu.make_async_remote_copy(
            src_ref=src,
            dst_ref=dst,
            send_sem=ss.at[0],
            recv_sem=rs.at[0],
            device_id=device,
            device_id_type=MESH,
        )

    def part(ref, slot, size):
        return ref.at[pl.ds(pl.multiple_of(slot * size, 8), size)]

    def way(axis, c, back):
        me, n = (la, n_lat) if axis == "lat" else (lo, n_lon)
        k = "y" if axis == "lat" else "x"
        size = spec[f"{k}_rows{c}"]
        a, b, ss, rs = ("back", "home", "bss", "brs") if back else ("send", "recv", "ss", "rs")
        return axis, me, n, size, *(R.at(f"{k}_{name}", c) for name in (a, b, ss, rs))

    def exchange(axis, me, n, size, src, dst, ss, rs, shared=False):
        for o in range(1, n):
            other = lax.rem(me + o, n)
            remote(axis, other, src if shared else part(src, other, size), part(dst, me, size), ss, rs).start()
        pltpu.make_async_copy(src if shared else part(src, me, size), part(dst, me, size), rs.at[0]).start()

    def arrive(axis, me, n, size, src, dst, ss, rs, shared=False):
        remote(axis, lax.rem(me + 1, n), dst, dst, ss, rs).wait_recv()

    def left_for_good(axis, me, n, size, src, dst, ss, rs):
        gone = dst.at[pl.ds(0, (n - 1) * size)]
        remote(axis, lax.rem(me + 1, n), gone, gone, ss, rs).wait_send()

    def by_row(count, jumps, per_v):
        r = lax.broadcasted_iota(jnp.int32, (count, 128), 0)
        out = jnp.broadcast_to(per_v[0], (count, 128))
        for v in range(1, len(per_v)):
            inside = (r >= v * jumps) & (r < (v + 1) * jumps)
            out = jnp.where(inside, jnp.broadcast_to(per_v[v], (count, 128)), out)
        return out

    def scan_states(n, s, t, an, a):
        s_in, total = [], jnp.zeros_like(s[0])
        for e in range(n):
            s_in.append(total)
            total = an * total + s[e]
        t_in, total = [None] * n, -a * total
        for e in reversed(range(n)):
            t_in[e] = total
            total = t[e] + an * total
        return s_in, t_in

    def scan_coefs(vs, count, jumps, n):
        return (
            by_row(count, jumps, [decay[v] for v in vs]),
            by_row(count, jumps, [power(v, n) for v in vs]),
            by_row(count, jumps, [through(v, n)[0] for v in vs]),
            by_row(count, jumps, [through(v, n)[1] for v in vs]),
        )

    def x_scan(c):
        vs = CHUNKS[c]
        count, size = len(vs) * groups, spec[f"x_rows{c}"]
        a_r, an_r, g1_r, g2_r = scan_coefs(vs, count, groups, cols)
        recv, back = R.at("x_recv", c), R.at("x_back", c)
        p0 = [recv[pl.ds(e * size, count, stride=2), :] for e in range(n_lon)]
        p1 = [recv[pl.ds(e * size + 1, count, stride=2), :] for e in range(n_lon)]
        s_in, t_in = scan_states(n_lon, p0, p1, an_r, a_r)
        sr = [swap(x) for x in s_in]
        tr = [swap(x) for x in t_in]
        s_in2, t_in2 = scan_states(
            n_lon,
            [p0[e] + g1_r * sr[e] + g2_r * tr[e] for e in range(n_lon)],
            [p1[e] + g1_r * tr[e] + g2_r * sr[e] for e in range(n_lon)],
            an_r,
            a_r,
        )
        for e in range(n_lon):
            back[pl.ds(e * size, count, stride=2), :] = pick(s_in[e], s_in2[e])
            back[pl.ds(e * size + 1, count, stride=2), :] = pick(t_in[e], t_in2[e])

    def x_finish(c, k):
        vs = CHUNKS[c]
        full = len(vs) * rows
        stride = spec[f"y_stride{c}"]
        home, yf, xe = R.at("x_home", c), R.at("yf", c), R.at("xe", c)
        xt, xv = R.at("xu", c), R.at("xv", c)

        def got(i):
            return rows_of(
                [home[pl.ds(g * 2 + i, 8, stride=spec[f"x_rows{c}"]), :] for g in range(full // 8)]
            )

        q0, q1 = got(0), got(1)
        q0r, q1r = swap(q0), swap(q1)
        si, s2i = pick(q0, q0r), pick(q0r, q0)
        ti, t2i = pick(q1, q1r), pick(q1r, q1)
        s_en = pick(si, k["s1r"] + k["ah"] * si)
        t_en = pick(k["t1r"] + k["ah"] * ti, ti)
        s_own = k["s2"] + k["g1"] * s_en + k["g2"] * t_en
        t_own = k["t2"] + k["g1"] * t_en + k["g2"] * s_en
        s2_en = pick(s2i, swap(s_own) + k["ah"] * s2i)
        t2_en = pick(swap(t_own) + k["ah"] * t2i, t2i)
        if c == 0:
            ax = k["ax"]
            side = pick(s2i + ax * (t_own + k["ah"] * t2_en), ax * (s_own + k["ah"] * s2_en) + t2i)
            yf[pl.ds(half, rows, stride=stride), :] = side
            for z in range(1, 8):
                yf[pl.ds(half + z, rows, stride=stride), :] = jnp.zeros((rows, 128), F32)
        for i, value in enumerate((s_en, t_en, s2_en, t2_en)):
            xe[pl.ds(i * full, full), :] = value

        def correct(j, _):
            for i, v in enumerate(vs):
                f0 = xtab[pl.ds(v * half + j, 1), :]
                b0 = xtab[pl.ds(v * half + half - 1 - j, 1), :]
                f1 = xtab[pl.ds((3 + v) * half + j, 1), :]
                b1 = xtab[pl.ds((3 + v) * half + half - 1 - j, 1), :]
                at = i * rows
                value = block(xt, j * full + at) + block(xv, j * full + at)
                value = value + xe[pl.ds(at, rows), :] * f1 + xe[pl.ds(full + at, rows), :] * b1
                value = value + xe[pl.ds(2 * full + at, rows), :] * f0 + xe[pl.ds(3 * full + at, rows), :] * b0
                yf[pl.ds(i * half + j, rows, stride=stride), :] = value
            return 0

        lax.fori_loop(0, half, correct, 0, unroll=4)

    def y_parts(c):
        return [(0, half + 8)] if c == 0 else [(0, half), (half, half)]

    def y_filter(c):
        vs = CHUNKS[c]
        stride = spec[f"y_stride{c}"]
        ends = []
        for v, (base, height) in zip(vs, y_parts(c)):

            def line(name, i):
                return R.at(name, c)[pl.ds(pl.multiple_of(i * stride + base, 8), height), :]

            def put(name):
                def go(i, value):
                    R.at(name, c)[pl.ds(pl.multiple_of(i * stride + base, 8), height), :] = value[0]

                return go

            zero = (jnp.zeros((height, 128), F32),)
            times = lambda s: [decay[v] * s[0]]
            (s1,), (t1,) = both_ways(rows, lambda i: [line("yf", i)], put("ys"), put("yt"), times, zero)
            second = lambda i: [line("ys", i) + line("yt", i)]
            (s2,), (t2,) = both_ways(rows, second, put("yv"), put("yu"), times, zero)
            ends.append((s1, t1, s2, t2))
        s1, t1, s2, t2 = zip(*ends)
        send, size = R.at("y_send", c), spec[f"y_rows{c}"]
        for k, states in enumerate((s1, t1, s2, t2)):
            for i in range(len(vs)):
                for q in range(jj_n):
                    send[pl.ds((i * jj_n + q) * 4 + k, n_lat, stride=size), :] = states[i][
                        q * n_lat : (q + 1) * n_lat
                    ]
            if c == 0:
                last = jj_n * 4 + k
                send[pl.ds(last, n_lat, stride=size), :] = jnp.zeros((n_lat, 128), F32)
                send[pl.ds(last, 1), :] = states[0][half : half + 1]
        return s2, t2

    def y_scan(c):
        vs = CHUNKS[c]
        count, size = len(vs) * jj_n + (1 if c == 0 else 0), spec[f"y_rows{c}"]
        jumps = jj_n if c else count
        a_r, an_r, g1_r, g2_r = scan_coefs(vs, count, jumps, rows)
        recv, back = R.at("y_recv", c), R.at("y_back", c)

        def got(k):
            return [recv[pl.ds(e * size + k, count, stride=4), :] for e in range(n_lat)]

        def give(k, values):
            for e in range(n_lat):
                back[pl.ds(e * size + k, count, stride=4), :] = values[e]

        s_in, t_in = scan_states(n_lat, got(0), got(1), an_r, a_r)
        give(0, s_in)
        give(1, t_in)
        p2, p3 = got(2), got(3)
        s_in2, t_in2 = scan_states(
            n_lat,
            [p2[e] + g1_r * s_in[e] + g2_r * t_in[e] for e in range(n_lat)],
            [p3[e] + g1_r * t_in[e] + g2_r * s_in[e] for e in range(n_lat)],
            an_r,
            a_r,
        )
        give(2, s_in2)
        give(3, t_in2)

    def y_finish(c, s2, t2):
        home, size = R.at("y_home", c), spec[f"y_rows{c}"]
        for i, v in enumerate(CHUNKS[c]):

            def entering(k):
                parts = [home[pl.ds((i * jj_n + q) * 4 + k, n_lat, stride=size), :] for q in range(jj_n)]
                if c == 0:
                    parts.append(jnp.broadcast_to(home[pl.ds(jj_n * 4 + k, 1), :], (8, 128)))
                return rows_of(parts)

            s_en, t_en, s2_en, t2_en = (entering(k) for k in range(4))
            if c == 0:
                g1v, g2v = through(0, rows)
                an = power(0, rows)
                first = s2_en + decay[0] * (t2[0] + g1v * t_en + g2v * s_en + an * t2_en)
                after = decay[0] * (s2[0] + g1v * s_en + g2v * t_en + an * s2_en) + t2_en
                edge_rows[pl.ds(0, half), :] = first[:half]
                edge_rows[pl.ds(half, half), :] = after[:half]
            base, height = y_parts(c)[i]
            stride = spec[f"y_stride{c}"]
            yt, yv, yf = R.at("yu", c), R.at("yv", c), R.at("yf", c)

            def correct(n, _):
                at = pl.ds(pl.multiple_of(n * stride + base, 8), height)
                f0 = ytab[pl.ds(v * rows + n, 1), :]
                b0 = ytab[pl.ds(v * rows + rows - 1 - n, 1), :]
                f1 = ytab[pl.ds((3 + v) * rows + n, 1), :]
                b1 = ytab[pl.ds((3 + v) * rows + rows - 1 - n, 1), :]
                value = yt[at, :] + yv[at, :] + s_en * f1 + t_en * b1
                yf[at, :] = value + s2_en * f0 + t2_en * b0
                return 0

            lax.fori_loop(0, rows, correct, 0, unroll=2)

    def mix_out(c):
        yf, stride = R.at("yf", c), spec[f"y_stride{c}"]

        def step(b, acc):
            js = batch(b)
            acc = list(acc)
            for i, v in enumerate(CHUNKS[c]):
                parts = []
                for j in js:
                    x = yf[pl.ds(i * half + j, rows, stride=stride), :]
                    acc[i] = acc[i] + x * block(w_ref(v), w_at(v, j))
                    parts.append(x)
                y = split_product(rows_of(parts), mats[3 + v])
                tile = sig[pl.ds(v * rows, rows), :]
                for t, j in enumerate(js):
                    z = y[t * rows : (t + 1) * rows] * spread(tile, j)
                    if v == 0:
                        put_block(temp, (j + 1) * rows, z)
                    else:
                        put_block(R.w1, w_at(v, j), z)
            return tuple(acc)

        start = tuple(jnp.zeros((rows, 128), F32) for _ in CHUNKS[c])
        acc = lax.fori_loop(0, half // 8, step, start, unroll=True)
        for i, v in enumerate(CHUNKS[c]):
            R.e_send[pl.ds(v, 1), :] = jnp.sum(acc[i], axis=0, keepdims=True)

    kept = {1: x_filter(1)}
    pl.semaphore_wait(barrier, n_lat + n_lon - 2)

    up = (lax.rem(la + n_lat - 1, n_lat), lo)
    down = (lax.rem(la + 1, n_lat), lo)
    left = (la, lax.rem(lo + n_lon - 1, n_lon))
    right = (la, lax.rem(lo + 1, n_lon))
    starts = (0, msg_r, 2 * msg_r, 2 * msg_r + msg_c)
    sizes = (msg_r, msg_r, msg_c, msg_c)
    halo = []
    for q, device in enumerate((up, down, left, right)):
        here = pl.ds(starts[q], sizes[q])
        copy = pltpu.make_async_remote_copy(
            src_ref=halo_send.at[here],
            dst_ref=halo_recv.at[here],
            send_sem=R.halo_ss.at[q],
            recv_sem=R.halo_rs.at[q],
            device_id=device,
            device_id_type=MESH,
        )
        copy.start()
        halo.append(copy)
    xa1, xb1, xa0, xb0 = way("lon", 1, False), way("lon", 1, True), way("lon", 0, False), way("lon", 0, True)
    ya1, yb1, ya0, yb0 = way("lat", 1, False), way("lat", 1, True), way("lat", 0, False), way("lat", 0, True)
    exchange(*xa1)

    loads[0].wait()
    pair(0)
    edge_rows[...] = jnp.zeros_like(edge_rows)

    def close_columns(lo_edge, hi_edge):
        put_block(temp, 0, pick(lo_edge, swap(temp[pl.ds(half * rows, rows), :])))
        put_block(temp, (half + 1) * rows, pick(swap(temp[pl.ds(rows, rows), :]), hi_edge))

    zero_block = jnp.zeros((rows, 128), F32)
    close_columns(zero_block, zero_block)
    row_id = lax.broadcasted_iota(jnp.int32, (rows, 128), 0)

    def laplace(j):
        x = block(temp, (j + 1) * rows)
        above = jnp.where(row_id == 0, edge_rows[pl.ds(j, 1), :], pltpu.roll(x, 1, 0))
        below = jnp.where(row_id == rows - 1, edge_rows[pl.ds(half + j, 1), :], pltpu.roll(x, rows - 1, 0))
        return 4.0 * x - above - below - block(temp, j * rows) - block(temp, (j + 2) * rows)

    def mix_psi(b, _):
        js = batch(b)
        y = split_product(rows_of([laplace(j) for j in js]), mats[6])
        y = y + rows_of([block(R.w0, j * rows) for j in js])
        y = split_product(y, mats[0])
        for t, j in enumerate(js):
            put_block(R.w0, j * rows, y[t * rows : (t + 1) * rows] * spread(sig0, j))
        return 0

    lax.fori_loop(0, half // 8, mix_psi, 0, unroll=True)

    wide = jnp.broadcast_to(low1, (half, 128))

    def row_sigma(tile, r):
        t = jnp.concatenate([tile, jnp.zeros((128 - rows, 128), F32)], axis=0).T
        a = jnp.broadcast_to(t[:half, r : r + 1], (half, 128))
        b = jnp.broadcast_to(t[half : 2 * half, r : r + 1], (half, 128))
        return jnp.where(wide, a, b)

    lane_r = lax.broadcasted_iota(jnp.int32, (rows, 128), 1)

    def side_sigma(a, at_a, b, at_b):
        take = lambda x, at: jnp.take_along_axis(
            x, jnp.full((rows, 128), at, jnp.int32), axis=1, mode="promise_in_bounds"
        )
        return jnp.where(lane_r < 64, take(a, at_a), take(b, at_b))

    own_up, own_down = row_sigma(sig0, 0), row_sigma(sig0, rows - 1)
    own_side = side_sigma(sig0, 0, sig0, cols - 1)

    arrive(*xa1)
    x_scan(1)
    exchange(*xb1)

    for copy in halo:
        copy.wait()
    has_up = jnp.where(la > 0, 1.0, 0.0).astype(F32)
    has_down = jnp.where(la < n_lat - 1, 1.0, 0.0).astype(F32)
    has_left = jnp.where(lo > 0, 1.0, 0.0).astype(F32)
    has_right = jnp.where(lo < n_lon - 1, 1.0, 0.0).astype(F32)
    from_right = swap(halo_recv[pl.ds(2 * msg_r, rows), :]) * has_right
    from_left = swap(halo_recv[pl.ds(2 * msg_r + msg_c, rows), :]) * has_left
    outside = rows_of(
        [
            halo_recv[pl.ds(msg_r, half), :] * has_up,
            halo_recv[pl.ds(0, half), :] * has_down,
            pick(from_left, from_right),
        ]
    )
    outside = split_product(split_product(outside, mats[6]), mats[0])
    first_rows = pl.ds(0, half, stride=rows)
    last_rows = pl.ds(rows - 1, half, stride=rows)
    R.w0[first_rows, :] = R.w0[first_rows, :] - outside[:half] * own_up
    R.w0[last_rows, :] = R.w0[last_rows, :] - outside[half : 2 * half] * own_down
    side = outside[2 * half :] * own_side
    at_last = pl.ds((half - 1) * rows, rows)
    R.w0[pl.ds(0, rows), :] = R.w0[pl.ds(0, rows), :] - pick(side, zero_block)
    R.w0[at_last, :] = R.w0[at_last, :] - pick(zero_block, side)

    kept[0] = x_filter(0)
    exchange(*xa0)

    arrive(*xb1)
    arrive(*xa0)
    x_scan(0)
    exchange(*xb0)
    x_finish(1, kept[1])
    ends1 = y_filter(1)
    exchange(*ya1)
    arrive(*xb0)
    x_finish(0, kept[0])
    ends0 = y_filter(0)
    exchange(*ya0)

    up_sigma = row_sigma(halo_recv[pl.ds(msg_r + half, rows), :] * has_up, rows - 1)
    down_sigma = row_sigma(halo_recv[pl.ds(half, rows), :] * has_down, 0)
    side_out = side_sigma(
        halo_recv[pl.ds(2 * msg_r + msg_c + rows, rows), :] * has_left,
        cols - 1,
        halo_recv[pl.ds(2 * msg_r + rows, rows), :] * has_right,
        0,
    )

    arrive(*ya1)
    y_scan(1)
    exchange(*yb1)
    arrive(*ya0)
    y_scan(0)
    exchange(*yb0)

    R.e_send[...] = jnp.zeros_like(R.e_send)
    arrive(*yb1)
    y_finish(1, *ends1)
    mix_out(1)
    arrive(*yb0)
    y_finish(0, *ends0)
    mix_out(0)
    ea = ("lat", la, n_lat, 8, R.e_send, R.e_recv, R.e_ss, R.e_rs)
    exchange(*ea, shared=True)

    edges = split_product(
        rows_of([edge_rows[...], R.yf0[pl.ds(half, rows, stride=spec["y_stride0"]), :]]), mats[3]
    )
    edge_rows[pl.ds(0, half), :] = edges[:half] * up_sigma
    edge_rows[pl.ds(half, half), :] = edges[half : 2 * half] * down_sigma
    side = edges[2 * half :] * side_out
    close_columns(side, side)

    def unpair(v, js, values):
        for t in range(0, len(js), 2):
            even, odd = values[t], values[t + 1]
            k = lax.div(js[t], 2)
            out_ref[v, :, pl.ds(pl.multiple_of(k * 128, 128), 128)] = pick(even, swap(odd))
            out_ref[v, :, pl.ds(pl.multiple_of((k + half // 2) * 128, 128), 128)] = pick(swap(even), odd)

    def finish(b, _):
        js = batch(b)
        y = split_product(rows_of([laplace(j) for j in js]), mats[7])
        z0 = [block(temp, (j + 1) * rows) for j in js]
        unpair(0, js, z0)
        unpair(1, js, [block(R.w1, w_at(1, j)) + coupling * z for j, z in zip(js, z0)])
        unpair(2, js, [y[t * rows : (t + 1) * rows] + block(R.w1, w_at(2, j)) for t, j in enumerate(js)])
        return 0

    lax.fori_loop(0, half // 8, finish, 0, unroll=True)

    def total_of(ref, n):
        total = ref[pl.ds(0, 8), :]
        for e in range(1, n):
            total = total + ref[pl.ds(e * 8, 8), :]
        return total

    arrive(*ea, shared=True)
    R.f_send[...] = total_of(R.e_recv, n_lat)
    fa = ("lon", lo, n_lon, 8, R.f_send, R.f_recv, R.f_ss, R.f_rs)
    exchange(*fa, shared=True)
    arrive(*fa, shared=True)
    total = total_of(R.f_recv, n_lon)
    total = total + swap(total)

    rank = (la * n_lon + lo).astype(F32)
    keep = lane[:1] < 64
    strict = (
        lax.broadcasted_iota(jnp.int32, (128, 128), 0) < lax.broadcasted_iota(jnp.int32, (128, 128), 1)
    ).astype(F32)
    before = jnp.zeros((1, 1), F32)
    outs = [jnp.zeros((1, 1), F32)] * 3
    scale = 1.0 / float(rows * n_lat * cols * n_lon)
    for v in range(3):
        mine = jnp.where(keep & (owners[v] == rank), 1.0, 0.0)
        slot = jnp.dot(jnp.broadcast_to(mine, (8, 128)), strict, preferred_element_type=F32)[:1] + before
        before = before + jnp.sum(mine, axis=1, keepdims=True)
        value = total[v : v + 1] * gain[v] * scale * mine
        for k in range(3):
            outs[k] = outs[k] + jnp.sum(jnp.where(slot == float(k), value, 0.0), axis=1, keepdims=True)
    for k in range(3):
        energy_ref[:, k : k + 1] = outs[k]

    for one in (xa1, xb1, xa0, xb0, ya1, yb1, ya0, yb0, ea, fa):
        left_for_good(*one)


def shards(state, sigma, vert, bal_temp, chi_coef, scales, classes, owner):
    dims = (lax.axis_size("lat"), lax.axis_size("lon"), state.shape[1], sigma.shape[2])
    spec, scratch = layout(*dims, scales.shape[0])
    vmem = pl.BlockSpec(memory_space=pltpu.VMEM)
    return pl.pallas_call(
        functools.partial(kernel, dims, spec, tuple(scratch)),
        out_shape=(pltpu.VMEM(state.shape, F32), pltpu.VMEM((1, 3), F32)),
        in_specs=[pl.BlockSpec(memory_space=pltpu.MemorySpace.HBM)] * 8,
        out_specs=(vmem, vmem),
        scratch_shapes=list(scratch.values()),
        compiler_params=pltpu.CompilerParams(
            collective_id=0, has_side_effects=True, vmem_limit_bytes=56 * 1024 * 1024
        ),
        name="covariance",
    )(
        state,
        sigma,
        vert,
        bal_temp,
        chi_coef.reshape(1, -1),
        scales.reshape(1, -1),
        classes.reshape(1, -1),
        owner.reshape(1, -1),
    )


def solution(mesh):
    return jax.shard_map(
        shards,
        mesh=mesh,
        in_specs=(P(None, "lat", "lon"), P(None, "lat", "lon"), P(), P(), P(), P(), P(), P()),
        out_specs=(P(None, "lat", "lon"), P(("lat", "lon"), None)),
        check_vma=False,
    )
```

```python
import functools

import jax
import jax.numpy as jnp
from jax import lax
from jax.experimental import pallas as pl
from jax.experimental.pallas import tpu as pltpu
from jax.sharding import PartitionSpec as P

F32 = jnp.float32
BF16 = jnp.bfloat16
MESH = pl.DeviceIdType.MESH


def split_product(x, w):
    hi = x.astype(BF16)
    lo = (x - hi.astype(F32)).astype(BF16)
    y = jnp.dot(jnp.concatenate([hi, lo], axis=1), w, preferred_element_type=F32)
    return y[:, :128] + y[:, 128:]


def swap(x):
    return pltpu.roll(x, 64, 1)


def rows_of(parts):
    return jnp.concatenate(parts, axis=0)


def layout(n_lat, n_lon, rows, cols, n_class):
    half = cols // 2
    jj_n = half // n_lat
    groups = rows // 8
    spec = {}
    for c, count in enumerate((1, 2)):
        spec[f"x_rows{c}"] = -(-count * groups * 2 // 8) * 8
        spec[f"y_rows{c}"] = -(-(count * jj_n * 4 + (4 if c == 0 else 0)) // 8) * 8
        spec[f"y_stride{c}"] = count * half + 8
    shapes = {
        "in_sem": 3,
        "small_sem": 7,
        "halo_ss": 4,
        "halo_rs": 4,
        "e_ss": 1,
        "e_rs": 1,
        "f_ss": 1,
        "f_rs": 1,
    }
    for name in shapes:
        shapes[name] = pltpu.SemaphoreType.DMA((shapes[name],))
    vm = lambda r: pltpu.VMEM((r, 128), F32)
    shapes["state"] = pltpu.VMEM((3, rows, cols * 64), F32)
    shapes["sigma"] = pltpu.VMEM((3, rows, cols), F32)
    shapes["vert"] = pltpu.VMEM((3, 64, 64), F32)
    shapes["bal"] = pltpu.VMEM((64, 64), F32)
    shapes["chi"] = pltpu.VMEM((1, 64), F32)
    shapes["scales"] = pltpu.VMEM((1, n_class), F32)
    shapes["classes"] = pltpu.VMEM((1, 192), jnp.int32)
    shapes["owner"] = pltpu.VMEM((1, 192), jnp.int32)
    shapes["mats"] = pltpu.VMEM((8, 256, 256), BF16)
    sizes = {
        "table": 8,
        "pad": 64,
        "sig": 3 * rows,
        "temp": (half + 2) * rows,
        "xtab": 6 * half,
        "ytab": 6 * rows,
        "edge_rows": 2 * half,
        "halo_send": 2 * (half + rows) + 4 * rows,
        "halo_recv": 2 * (half + rows) + 4 * rows,
        "e_send": 8,
        "e_recv": 8 * n_lat,
        "f_send": 8,
        "f_recv": 8 * n_lon,
    }
    for c, count in enumerate((1, 2)):
        for name in ("w", "xs", "xt", "xu", "xv"):
            sizes[f"{name}{c}"] = half * count * rows
        sizes[f"xe{c}"] = 4 * count * rows
        for name in ("yf", "ys", "yt", "yv", "yu"):
            sizes[f"{name}{c}"] = rows * spec[f"y_stride{c}"]
        for name in ("send", "recv", "back", "home"):
            sizes[f"x_{name}{c}"] = n_lon * spec[f"x_rows{c}"]
            sizes[f"y_{name}{c}"] = n_lat * spec[f"y_rows{c}"]
        for name in ("send", "recv"):
            sizes[f"z_{name}{c}"] = n_lat * spec[f"y_rows{c}"]
        for name in ("ss", "rs", "bss", "brs"):
            shapes[f"x_{name}{c}"] = pltpu.SemaphoreType.DMA((1,))
            shapes[f"z_{name}{c}"] = pltpu.SemaphoreType.DMA((1,))
            shapes[f"y_{name}{c}"] = pltpu.SemaphoreType.DMA((1,))
    for name, size in sizes.items():
        shapes[name] = vm(size)
    return spec, shapes


CHUNKS = ((0,), (1, 2))


class Names:
    def __init__(self, names, refs):
        for name, ref in zip(names, refs):
            setattr(self, name, ref)

    def at(self, name, c):
        return getattr(self, f"{name}{c}")


def kernel(
    dims,
    spec,
    names,
    state_hbm,
    sigma_hbm,
    vert_hbm,
    bal_hbm,
    chi_hbm,
    scales_hbm,
    class_hbm,
    owner_hbm,
    out_ref,
    energy_ref,
    *refs,
):
    n_lat, n_lon, rows, cols = dims
    half = cols // 2
    jj_n = half // n_lat
    groups = rows // 8
    R = Names(names, refs)
    state_ref, table, mats, pad, sig, temp = R.state, R.table, R.mats, R.pad, R.sig, R.temp
    xtab, ytab, edge_rows = R.xtab, R.ytab, R.edge_rows
    halo_send, halo_recv = R.halo_send, R.halo_recv
    la = lax.axis_index("lat")
    lo = lax.axis_index("lon")

    barrier = pltpu.get_barrier_semaphore()
    for o in range(1, n_lat):
        pl.semaphore_signal(barrier, inc=1, device_id=(lax.rem(la + o, n_lat), lo), device_id_type=MESH)
    for o in range(1, n_lon):
        pl.semaphore_signal(barrier, inc=1, device_id=(la, lax.rem(lo + o, n_lon)), device_id_type=MESH)

    sigma_ref, vert_ref, bal_ref = R.sigma, R.vert, R.bal
    chi_ref, scales_ref, class_ref, owner_ref = R.chi, R.scales, R.classes, R.owner
    small = []
    for i, (src, dst) in enumerate(
        (
            (class_hbm, class_ref),
            (scales_hbm, scales_ref),
            (vert_hbm, vert_ref),
            (bal_hbm, bal_ref),
            (sigma_hbm, sigma_ref),
            (chi_hbm, chi_ref),
            (owner_hbm, owner_ref),
        )
    ):
        small.append(pltpu.make_async_copy(src, dst, R.small_sem.at[i]))
        small[-1].start()
    loads = {}
    for v in (2, 1, 0):
        loads[v] = pltpu.make_async_copy(state_hbm.at[v], state_ref.at[v], R.in_sem.at[v])
        loads[v].start()

    lane = lax.broadcasted_iota(jnp.int32, (8, 128), 1)
    low1 = lane[:1] < 64

    def low(x):
        return jnp.broadcast_to(low1, x.shape)

    def pick(a, b):
        return jnp.where(low(a), a, b)

    for copy in small:
        copy.wait()

    table[...] = jnp.zeros_like(table)

    def levels(row):
        table[0:1, :] = row[:, :128]
        table[1:2, :64] = row[:, 128:]
        pair01 = table[...]
        flip01 = swap(pair01)
        first, second = pick(pair01, flip01), pick(flip01, pair01)
        return [first[0:1], second[0:1], first[1:2]]

    classes = class_ref[...]
    lengths = jnp.zeros(classes.shape, F32)
    for c in range(scales_ref.shape[1]):
        lengths = jnp.where(classes == c, scales_ref[:, c : c + 1], lengths)
    length = levels(lengths)
    owners = levels(owner_ref[...].astype(F32))
    table[0:1, :64] = chi_ref[...]
    coupling = table[...]
    coupling = pick(coupling, swap(coupling))[0:1]
    decay = [jnp.exp(-1.0 / r) for r in length]

    def power(v, k):
        return jnp.exp(-float(k) / length[v])

    def through(v, n):
        a = decay[v]
        return float(n) * power(v, n), a * (1.0 - power(v, 2 * n)) / (1.0 - a * a)

    def fill_table(ref, n):
        pos = lax.broadcasted_iota(jnp.int32, (n, 128), 0).astype(F32)
        for v in range(3):
            a, r = decay[v], length[v]
            first = jnp.exp(-(pos + 1.0) / r)
            tail = 1.0 - jnp.exp(-2.0 * (n - 1.0 - pos) / r)
            second = (pos + 1.0) * first + first * (a * a) * tail / (1.0 - a * a)
            ref[pl.ds(v * n, n), :] = first
            ref[pl.ds((3 + v) * n, n), :] = second

    fill_table(xtab, half)
    fill_table(ytab, rows)

    gain = []
    for v in range(3):
        a = decay[v]
        c = (1.0 - a) / (1.0 + a)
        gain.append(length[v] * jnp.sqrt(length[v]) * (c * c) * (c * c))

    def put_matrix(slot, m):
        pad[:, :64] = m
        top = pad[...]
        full = rows_of([top, swap(top)])
        hi = full.astype(BF16)
        low_part = (full - hi.astype(F32)).astype(BF16)
        mats[slot] = rows_of(
            [
                jnp.concatenate([hi, low_part], axis=1),
                jnp.concatenate([hi, jnp.zeros_like(hi)], axis=1),
            ]
        )

    pad[...] = jnp.zeros_like(pad)
    for v in range(3):
        put_matrix(v, vert_ref[v])
        put_matrix(3 + v, (vert_ref[v] * gain[v][:, :64]).T)
    put_matrix(6, bal_ref[...])
    put_matrix(7, bal_ref[...].T)

    for v in range(3):
        sig[pl.ds(v * rows, rows), :] = jnp.zeros((rows, 128), F32)
        sig[pl.ds(v * rows, rows), :cols] = sigma_ref[v]
    column = jnp.where(lax.broadcasted_iota(jnp.int32, (rows, 128), 1) < 64, 0, half)

    def spread(tile, j):
        return jnp.take_along_axis(tile, column + j, axis=1, mode="promise_in_bounds")

    def block(ref, at):
        return ref[pl.ds(pl.multiple_of(at, 8), rows), :]

    def put_block(ref, at, value):
        ref[pl.ds(pl.multiple_of(at, 8), rows), :] = value


    def pair(v):
        def step(k, _):
            at1 = pl.ds(pl.multiple_of(k * 128, 128), 128)
            at2 = pl.ds(pl.multiple_of((k + half // 2) * 128, 128), 128)
            n1, n2 = state_ref[v, :, at1], state_ref[v, :, at2]
            if v == 0:
                n1 = n1 + coupling * state_ref[1, :, at1]
                n2 = n2 + coupling * state_ref[1, :, at2]
            even = pick(n1, swap(n2))
            odd = pick(swap(n1), n2)
            if v == 2:
                put_block(temp, (2 * k + 1) * rows, even)
                put_block(temp, (2 * k + 2) * rows, odd)
            elif v == 1:
                put_block(R.w1, 4 * k * rows, even)
                put_block(R.w1, (4 * k + 2) * rows, odd)
            else:
                put_block(R.w0, 2 * k * rows, even)
                put_block(R.w0, (2 * k + 1) * rows, odd)
            return 0

        lax.fori_loop(0, half // 2, step, 0, unroll=4)

    def batch(b):
        return [b * 8 + t for t in range(8)]

    def w_at(v, j):
        return j * rows if v == 0 else (2 * j + v - 1) * rows

    def w_ref(v):
        return R.w0 if v == 0 else R.w1

    loads[2].wait()
    pair(2)

    sig0 = sig[pl.ds(0, rows), :]
    msg_r, msg_c = half + rows, 2 * rows
    halo_send[pl.ds(0, half), :] = temp[pl.ds(rows, half, stride=rows), :]
    halo_send[pl.ds(half, rows), :] = sig0
    halo_send[pl.ds(msg_r, half), :] = temp[pl.ds(2 * rows - 1, half, stride=rows), :]
    halo_send[pl.ds(msg_r + half, rows), :] = sig0
    halo_send[pl.ds(2 * msg_r, rows), :] = temp[pl.ds(rows, rows), :]
    halo_send[pl.ds(2 * msg_r + rows, rows), :] = sig0
    halo_send[pl.ds(2 * msg_r + msg_c, rows), :] = temp[pl.ds(half * rows, rows), :]
    halo_send[pl.ds(2 * msg_r + msg_c + rows, rows), :] = sig0

    loads[1].wait()
    pair(1)

    def mix_in(b, _):
        js = batch(b)
        chi = [block(R.w1, w_at(1, j)) for j in js]
        for v, parts in ((1, chi), (2, [block(temp, (j + 1) * rows) for j in js])):
            y = split_product(rows_of(parts), mats[v])
            tile = sig[pl.ds(v * rows, rows), :]
            for t, j in enumerate(js):
                put_block(R.w1, w_at(v, j), y[t * rows : (t + 1) * rows] * spread(tile, j))
        return 0

    lax.fori_loop(0, half // 8, mix_in, 0, unroll=True)

    def tall(per_v):
        return rows_of([jnp.broadcast_to(c, (rows, 128)) for c in per_v])

    def both_ways(n, load, put_s, put_t, times, start):
        def step(q, carry):
            s, t = carry
            r = n - 1 - q
            s = [x + p for x, p in zip(times(s), load(q))]
            put_s(q, s)
            m = times(t)
            put_t(r, m)
            t = [x + p for x, p in zip(m, load(r))]
            return tuple(s), tuple(t)

        return lax.fori_loop(0, n, step, (start, start), unroll=4)

    def x_filter(c):
        vs = CHUNKS[c]
        full = len(vs) * rows
        ax = tall([decay[v] for v in vs])

        def line(ref, j):
            return ref[pl.ds(pl.multiple_of(j * full, 8), full), :]

        def put(ref):
            def go(j, value):
                ref[pl.ds(pl.multiple_of(j * full, 8), full), :] = value[0]

            return go

        w, xs, xt, xu, xv = (R.at(n, c) for n in ("w", "xs", "xt", "xu", "xv"))
        zero = (jnp.zeros((full, 128), F32),)
        times = lambda s: [ax * s[0]]
        (s1,), (t1,) = both_ways(half, lambda j: [line(w, j)], put(xs), put(xt), times, zero)
        second = lambda j: [line(xs, j) + line(xt, j)]
        (s2,), (t2,) = both_ways(half, second, put(xu), put(xv), times, zero)

        ah = tall([power(v, half) for v in vs])
        g1 = tall([through(v, half)[0] for v in vs])
        g2 = tall([through(v, half)[1] for v in vs])
        s1r, t1r, s2r, t2r = swap(s1), swap(t1), swap(s2), swap(t2)
        q0 = pick(ah * s1 + s1r, s2 + g1 * s1r + ah * (s2r + g2 * t1))
        q1 = pick(t1 + ah * t1r, t2r + g1 * t1 + ah * (t2 + g2 * s1r))
        send = R.at("x_send", c)
        for i, q in enumerate((q0, q1)):
            for g in range(full // 8):
                send[pl.ds(g * 2 + i, 8, stride=spec[f"x_rows{c}"]), :] = q[g * 8 : g * 8 + 8]
        return dict(s1r=s1r, t1r=t1r, s2=s2, t2=t2, ah=ah, g1=g1, g2=g2, ax=ax)

    def remote(axis, other, src, dst, ss, rs):
        device = (other, lo) if axis == "lat" else (la, other)
        return pltpu.make_async_remote_copy(
            src_ref=src,
            dst_ref=dst,
            send_sem=ss.at[0],
            recv_sem=rs.at[0],
            device_id=device,
            device_id_type=MESH,
        )

    def part(ref, slot, size):
        return ref.at[pl.ds(pl.multiple_of(slot * size, 8), size)]

    def way(axis, c, back, k=None):
        me, n = (la, n_lat) if axis == "lat" else (lo, n_lon)
        k = k or ("y" if axis == "lat" else "x")
        size = spec[f"{k.replace('z', 'y')}_rows{c}"]
        a, b, ss, rs = ("back", "home", "bss", "brs") if back else ("send", "recv", "ss", "rs")
        return axis, me, n, size, *(R.at(f"{k}_{name}", c) for name in (a, b, ss, rs))

    def exchange(axis, me, n, size, src, dst, ss, rs, shared=False):
        for o in range(1, n):
            other = lax.rem(me + o, n)
            remote(axis, other, src if shared else part(src, other, size), part(dst, me, size), ss, rs).start()
        pltpu.make_async_copy(src if shared else part(src, me, size), part(dst, me, size), rs.at[0]).start()

    def arrive(axis, me, n, size, src, dst, ss, rs, shared=False):
        remote(axis, lax.rem(me + 1, n), dst, dst, ss, rs).wait_recv()

    def left_for_good(axis, me, n, size, src, dst, ss, rs):
        gone = dst.at[pl.ds(0, (n - 1) * size)]
        remote(axis, lax.rem(me + 1, n), gone, gone, ss, rs).wait_send()

    def by_row(count, jumps, per_v):
        r = lax.broadcasted_iota(jnp.int32, (count, 128), 0)
        out = jnp.broadcast_to(per_v[0], (count, 128))
        for v in range(1, len(per_v)):
            inside = (r >= v * jumps) & (r < (v + 1) * jumps)
            out = jnp.where(inside, jnp.broadcast_to(per_v[v], (count, 128)), out)
        return out

    def scan_states(n, s, t, an, a):
        s_in, total = [], jnp.zeros_like(s[0])
        for e in range(n):
            s_in.append(total)
            total = an * total + s[e]
        t_in, total = [None] * n, -a * total
        for e in reversed(range(n)):
            t_in[e] = total
            total = t[e] + an * total
        return s_in, t_in

    def scan_coefs(vs, count, jumps, n):
        return (
            by_row(count, jumps, [decay[v] for v in vs]),
            by_row(count, jumps, [power(v, n) for v in vs]),
            by_row(count, jumps, [through(v, n)[0] for v in vs]),
            by_row(count, jumps, [through(v, n)[1] for v in vs]),
        )

    def x_scan(c):
        vs = CHUNKS[c]
        count, size = len(vs) * groups, spec[f"x_rows{c}"]
        a_r, an_r, g1_r, g2_r = scan_coefs(vs, count, groups, cols)
        recv, back = R.at("x_recv", c), R.at("x_back", c)
        p0 = [recv[pl.ds(e * size, count, stride=2), :] for e in range(n_lon)]
        p1 = [recv[pl.ds(e * size + 1, count, stride=2), :] for e in range(n_lon)]
        s_in, t_in = scan_states(n_lon, p0, p1, an_r, a_r)
        sr = [swap(x) for x in s_in]
        tr = [swap(x) for x in t_in]
        s_in2, t_in2 = scan_states(
            n_lon,
            [p0[e] + g1_r * sr[e] + g2_r * tr[e] for e in range(n_lon)],
            [p1[e] + g1_r * tr[e] + g2_r * sr[e] for e in range(n_lon)],
            an_r,
            a_r,
        )
        for e in range(n_lon):
            back[pl.ds(e * size, count, stride=2), :] = pick(s_in[e], s_in2[e])
            back[pl.ds(e * size + 1, count, stride=2), :] = pick(t_in[e], t_in2[e])

    def x_finish(c, k):
        vs = CHUNKS[c]
        full = len(vs) * rows
        stride = spec[f"y_stride{c}"]
        home, yf, xe = R.at("x_home", c), R.at("yf", c), R.at("xe", c)
        xt, xv = R.at("xu", c), R.at("xv", c)

        def got(i):
            return rows_of(
                [home[pl.ds(g * 2 + i, 8, stride=spec[f"x_rows{c}"]), :] for g in range(full // 8)]
            )

        q0, q1 = got(0), got(1)
        q0r, q1r = swap(q0), swap(q1)
        si, s2i = pick(q0, q0r), pick(q0r, q0)
        ti, t2i = pick(q1, q1r), pick(q1r, q1)
        s_en = pick(si, k["s1r"] + k["ah"] * si)
        t_en = pick(k["t1r"] + k["ah"] * ti, ti)
        s_own = k["s2"] + k["g1"] * s_en + k["g2"] * t_en
        t_own = k["t2"] + k["g1"] * t_en + k["g2"] * s_en
        s2_en = pick(s2i, swap(s_own) + k["ah"] * s2i)
        t2_en = pick(swap(t_own) + k["ah"] * t2i, t2i)
        if c == 0:
            ax = k["ax"]
            side = pick(s2i + ax * (t_own + k["ah"] * t2_en), ax * (s_own + k["ah"] * s2_en) + t2i)
            yf[pl.ds(half, rows, stride=stride), :] = side
            for z in range(1, 8):
                yf[pl.ds(half + z, rows, stride=stride), :] = jnp.zeros((rows, 128), F32)
        for i, value in enumerate((s_en, t_en, s2_en, t2_en)):
            xe[pl.ds(i * full, full), :] = value

        def correct(j, _):
            for i, v in enumerate(vs):
                f0 = xtab[pl.ds(v * half + j, 1), :]
                b0 = xtab[pl.ds(v * half + half - 1 - j, 1), :]
                f1 = xtab[pl.ds((3 + v) * half + j, 1), :]
                b1 = xtab[pl.ds((3 + v) * half + half - 1 - j, 1), :]
                at = i * rows
                value = block(xt, j * full + at) + block(xv, j * full + at)
                value = value + xe[pl.ds(at, rows), :] * f1 + xe[pl.ds(full + at, rows), :] * b1
                value = value + xe[pl.ds(2 * full + at, rows), :] * f0 + xe[pl.ds(3 * full + at, rows), :] * b0
                yf[pl.ds(i * half + j, rows, stride=stride), :] = value
            return 0

        lax.fori_loop(0, half, correct, 0, unroll=4)

    def y_parts(c):
        return [(0, half + 8)] if c == 0 else [(0, half), (half, half)]

    def y_filter(c):
        vs = CHUNKS[c]
        stride = spec[f"y_stride{c}"]
        ends = []
        for v, (base, height) in zip(vs, y_parts(c)):

            def line(name, i):
                return R.at(name, c)[pl.ds(pl.multiple_of(i * stride + base, 8), height), :]

            def put(name):
                def go(i, value):
                    R.at(name, c)[pl.ds(pl.multiple_of(i * stride + base, 8), height), :] = value[0]

                return go

            zero = (jnp.zeros((height, 128), F32),)
            times = lambda s: [decay[v] * s[0]]
            (s1,), (t1,) = both_ways(rows, lambda i: [line("yf", i)], put("ys"), put("yt"), times, zero)
            second = lambda i: [line("ys", i) + line("yt", i)]
            (s2,), (t2,) = both_ways(rows, second, put("yv"), put("yu"), times, zero)
            ends.append((s1, t1, s2, t2))
        s1, t1, s2, t2 = zip(*ends)
        send, size = R.at("y_send", c), spec[f"y_rows{c}"]
        for k, states in enumerate((s1, t1, s2, t2)):
            for i in range(len(vs)):
                put_states(send, size, i, k, states[i])
            if c == 0:
                last = jj_n * 4 + k
                send[pl.ds(last, n_lat, stride=size), :] = jnp.zeros((n_lat, 128), F32)
                send[pl.ds(last, 1), :] = states[0][half : half + 1]
        return s2, t2

    def w_row(v, i):
        every = rows if v == 0 else 2 * rows
        return w_ref(v)[pl.ds((0 if v == 0 else (v - 1) * rows) + i, half, stride=every), :]

    def put_states(send, size, i, k, value):
        for q in range(jj_n):
            send[pl.ds((i * jj_n + q) * 4 + k, n_lat, stride=size), :] = value[q * n_lat : (q + 1) * n_lat]

    def w_states(c):
        send, size, stride = R.at("z_send", c), spec[f"y_rows{c}"], spec[f"y_stride{c}"]
        if c == 0:
            send[...] = jnp.zeros_like(send)
        for i, v in enumerate(CHUNKS[c]):
            base = y_parts(c)[i][0]

            def at(n):
                return pl.ds(pl.multiple_of(n * stride + base, 8), half)

            def put(name):
                def go(n, value):
                    R.at(name, c)[at(n), :] = value[0]

                return go

            zero = (jnp.zeros((half, 128), F32),)
            times = lambda s: [decay[v] * s[0]]
            (s1,), (t1,) = both_ways(rows, lambda n: [w_row(v, n)], put("ys"), put("yt"), times, zero)
            second = lambda n: [R.at("ys", c)[at(n), :] + R.at("yt", c)[at(n), :]]
            skip = lambda n, value: None
            (s2,), (t2,) = both_ways(rows, second, skip, skip, times, zero)
            for k, value in enumerate((s1, t1, s2, t2)):
                put_states(send, size, i, k, value)

    def local_energy(c):
        stride, out = spec[f"y_stride{c}"], []
        for i, v in enumerate(CHUNKS[c]):
            base = y_parts(c)[i][0]

            def step(n, acc):
                at = pl.ds(pl.multiple_of(n * stride + base, 8), half)
                return acc + w_row(v, n) * (R.at("yu", c)[at, :] + R.at("yv", c)[at, :])

            acc = lax.fori_loop(0, rows, step, jnp.zeros((half, 128), F32), unroll=4)
            out.append(jnp.sum(acc, axis=0, keepdims=True))
        return out

    def y_scan(c, energy):
        vs = CHUNKS[c]
        count, size = len(vs) * jj_n + (1 if c == 0 else 0), spec[f"y_rows{c}"]
        jumps = jj_n if c else count
        a_r, an_r, g1_r, g2_r = scan_coefs(vs, count, jumps, rows)
        recv, back = R.at("y_recv", c), R.at("y_back", c)

        def got(k):
            return [recv[pl.ds(e * size + k, count, stride=4), :] for e in range(n_lat)]

        def give(k, values):
            for e in range(n_lat):
                back[pl.ds(e * size + k, count, stride=4), :] = values[e]

        s_in, t_in = scan_states(n_lat, got(0), got(1), an_r, a_r)
        give(0, s_in)
        give(1, t_in)
        p2, p3 = got(2), got(3)
        s_in2, t_in2 = scan_states(
            n_lat,
            [p2[e] + g1_r * s_in[e] + g2_r * t_in[e] for e in range(n_lat)],
            [p3[e] + g1_r * t_in[e] + g2_r * s_in[e] for e in range(n_lat)],
            an_r,
            a_r,
        )
        give(2, s_in2)
        give(3, t_in2)
        w_in = R.at("z_recv", c)
        far = jnp.zeros((count, 128), F32)
        for e in range(n_lat):
            p = [w_in[pl.ds(e * size + k, count, stride=4), :] for k in range(4)]
            far = far + s_in2[e] * p[1] + t_in2[e] * p[0] + s_in[e] * p[3] + t_in[e] * p[2]
        far = a_r * far
        for i, v in enumerate(vs):
            own = jnp.sum(far[i * jj_n : (i + 1) * jj_n], axis=0, keepdims=True)
            R.e_send[pl.ds(v, 1), :] = energy[i] + own

    def y_finish(c, s2, t2):
        home, size = R.at("y_home", c), spec[f"y_rows{c}"]
        for i, v in enumerate(CHUNKS[c]):

            def entering(k):
                parts = [home[pl.ds((i * jj_n + q) * 4 + k, n_lat, stride=size), :] for q in range(jj_n)]
                if c == 0:
                    parts.append(jnp.broadcast_to(home[pl.ds(jj_n * 4 + k, 1), :], (8, 128)))
                return rows_of(parts)

            s_en, t_en, s2_en, t2_en = (entering(k) for k in range(4))
            if c == 0:
                g1v, g2v = through(0, rows)
                an = power(0, rows)
                first = s2_en + decay[0] * (t2[0] + g1v * t_en + g2v * s_en + an * t2_en)
                after = decay[0] * (s2[0] + g1v * s_en + g2v * t_en + an * s2_en) + t2_en
                edge_rows[pl.ds(0, half), :] = first[:half]
                edge_rows[pl.ds(half, half), :] = after[:half]
            base, height = y_parts(c)[i]
            stride = spec[f"y_stride{c}"]
            yt, yv, yf = R.at("yu", c), R.at("yv", c), R.at("yf", c)

            def correct(n, _):
                at = pl.ds(pl.multiple_of(n * stride + base, 8), height)
                f0 = ytab[pl.ds(v * rows + n, 1), :]
                b0 = ytab[pl.ds(v * rows + rows - 1 - n, 1), :]
                f1 = ytab[pl.ds((3 + v) * rows + n, 1), :]
                b1 = ytab[pl.ds((3 + v) * rows + rows - 1 - n, 1), :]
                value = yt[at, :] + yv[at, :] + s_en * f1 + t_en * b1
                yf[at, :] = value + s2_en * f0 + t2_en * b0
                return 0

            lax.fori_loop(0, rows, correct, 0, unroll=2)

    def mix_out(c):
        yf, stride = R.at("yf", c), spec[f"y_stride{c}"]

        def step(b, _):
            js = batch(b)
            for i, v in enumerate(CHUNKS[c]):
                parts = [yf[pl.ds(i * half + j, rows, stride=stride), :] for j in js]
                y = split_product(rows_of(parts), mats[3 + v])
                tile = sig[pl.ds(v * rows, rows), :]
                for t, j in enumerate(js):
                    z = y[t * rows : (t + 1) * rows] * spread(tile, j)
                    if v == 0:
                        put_block(temp, (j + 1) * rows, z)
                    else:
                        put_block(R.w1, w_at(v, j), z)
            return 0

        lax.fori_loop(0, half // 8, step, 0, unroll=True)

    kept = {1: x_filter(1)}
    pl.semaphore_wait(barrier, n_lat + n_lon - 2)

    up = (lax.rem(la + n_lat - 1, n_lat), lo)
    down = (lax.rem(la + 1, n_lat), lo)
    left = (la, lax.rem(lo + n_lon - 1, n_lon))
    right = (la, lax.rem(lo + 1, n_lon))
    starts = (0, msg_r, 2 * msg_r, 2 * msg_r + msg_c)
    sizes = (msg_r, msg_r, msg_c, msg_c)
    halo = []
    for q, device in enumerate((up, down, left, right)):
        here = pl.ds(starts[q], sizes[q])
        copy = pltpu.make_async_remote_copy(
            src_ref=halo_send.at[here],
            dst_ref=halo_recv.at[here],
            send_sem=R.halo_ss.at[q],
            recv_sem=R.halo_rs.at[q],
            device_id=device,
            device_id_type=MESH,
        )
        copy.start()
        halo.append(copy)
    xa1, xb1, xa0, xb0 = way("lon", 1, False), way("lon", 1, True), way("lon", 0, False), way("lon", 0, True)
    ya1, yb1, ya0, yb0 = way("lat", 1, False), way("lat", 1, True), way("lat", 0, False), way("lat", 0, True)
    za1, za0 = way("lat", 1, False, "z"), way("lat", 0, False, "z")
    exchange(*xa1)

    loads[0].wait()
    pair(0)
    edge_rows[...] = jnp.zeros_like(edge_rows)

    def close_columns(lo_edge, hi_edge):
        put_block(temp, 0, pick(lo_edge, swap(temp[pl.ds(half * rows, rows), :])))
        put_block(temp, (half + 1) * rows, pick(swap(temp[pl.ds(rows, rows), :]), hi_edge))

    zero_block = jnp.zeros((rows, 128), F32)
    close_columns(zero_block, zero_block)
    row_id = lax.broadcasted_iota(jnp.int32, (rows, 128), 0)

    def laplace(j):
        x = block(temp, (j + 1) * rows)
        above = jnp.where(row_id == 0, edge_rows[pl.ds(j, 1), :], pltpu.roll(x, 1, 0))
        below = jnp.where(row_id == rows - 1, edge_rows[pl.ds(half + j, 1), :], pltpu.roll(x, rows - 1, 0))
        return 4.0 * x - above - below - block(temp, j * rows) - block(temp, (j + 2) * rows)

    def mix_psi(b, _):
        js = batch(b)
        y = split_product(rows_of([laplace(j) for j in js]), mats[6])
        y = y + rows_of([block(R.w0, j * rows) for j in js])
        y = split_product(y, mats[0])
        for t, j in enumerate(js):
            put_block(R.w0, j * rows, y[t * rows : (t + 1) * rows] * spread(sig0, j))
        return 0

    lax.fori_loop(0, half // 8, mix_psi, 0, unroll=True)

    wide = jnp.broadcast_to(low1, (half, 128))

    def row_sigma(tile, r):
        t = jnp.concatenate([tile, jnp.zeros((128 - rows, 128), F32)], axis=0).T
        a = jnp.broadcast_to(t[:half, r : r + 1], (half, 128))
        b = jnp.broadcast_to(t[half : 2 * half, r : r + 1], (half, 128))
        return jnp.where(wide, a, b)

    lane_r = lax.broadcasted_iota(jnp.int32, (rows, 128), 1)

    def side_sigma(a, at_a, b, at_b):
        take = lambda x, at: jnp.take_along_axis(
            x, jnp.full((rows, 128), at, jnp.int32), axis=1, mode="promise_in_bounds"
        )
        return jnp.where(lane_r < 64, take(a, at_a), take(b, at_b))

    own_up, own_down = row_sigma(sig0, 0), row_sigma(sig0, rows - 1)
    own_side = side_sigma(sig0, 0, sig0, cols - 1)

    w_states(1)
    exchange(*za1)

    arrive(*xa1)
    x_scan(1)
    exchange(*xb1)

    for copy in halo:
        copy.wait()
    has_up = jnp.where(la > 0, 1.0, 0.0).astype(F32)
    has_down = jnp.where(la < n_lat - 1, 1.0, 0.0).astype(F32)
    has_left = jnp.where(lo > 0, 1.0, 0.0).astype(F32)
    has_right = jnp.where(lo < n_lon - 1, 1.0, 0.0).astype(F32)
    from_right = swap(halo_recv[pl.ds(2 * msg_r, rows), :]) * has_right
    from_left = swap(halo_recv[pl.ds(2 * msg_r + msg_c, rows), :]) * has_left
    outside = rows_of(
        [
            halo_recv[pl.ds(msg_r, half), :] * has_up,
            halo_recv[pl.ds(0, half), :] * has_down,
            pick(from_left, from_right),
        ]
    )
    outside = split_product(split_product(outside, mats[6]), mats[0])
    first_rows = pl.ds(0, half, stride=rows)
    last_rows = pl.ds(rows - 1, half, stride=rows)
    R.w0[first_rows, :] = R.w0[first_rows, :] - outside[:half] * own_up
    R.w0[last_rows, :] = R.w0[last_rows, :] - outside[half : 2 * half] * own_down
    side = outside[2 * half :] * own_side
    at_last = pl.ds((half - 1) * rows, rows)
    R.w0[pl.ds(0, rows), :] = R.w0[pl.ds(0, rows), :] - pick(side, zero_block)
    R.w0[at_last, :] = R.w0[at_last, :] - pick(zero_block, side)

    kept[0] = x_filter(0)
    exchange(*xa0)
    w_states(0)
    exchange(*za0)

    arrive(*xb1)
    arrive(*xa0)
    x_scan(0)
    exchange(*xb0)
    x_finish(1, kept[1])
    ends1 = y_filter(1)
    exchange(*ya1)
    arrive(*xb0)
    x_finish(0, kept[0])
    ends0 = y_filter(0)
    exchange(*ya0)

    up_sigma = row_sigma(halo_recv[pl.ds(msg_r + half, rows), :] * has_up, rows - 1)
    down_sigma = row_sigma(halo_recv[pl.ds(half, rows), :] * has_down, 0)
    side_out = side_sigma(
        halo_recv[pl.ds(2 * msg_r + msg_c + rows, rows), :] * has_left,
        cols - 1,
        halo_recv[pl.ds(2 * msg_r + rows, rows), :] * has_right,
        0,
    )

    R.e_send[...] = jnp.zeros_like(R.e_send)
    near1, near0 = local_energy(1), local_energy(0)

    arrive(*za1)
    arrive(*ya1)
    y_scan(1, near1)
    exchange(*yb1)
    arrive(*za0)
    arrive(*ya0)
    y_scan(0, near0)
    exchange(*yb0)
    ea = ("lat", la, n_lat, 8, R.e_send, R.e_recv, R.e_ss, R.e_rs)
    exchange(*ea, shared=True)

    def total_of(ref, n):
        total = ref[pl.ds(0, 8), :]
        for e in range(1, n):
            total = total + ref[pl.ds(e * 8, 8), :]
        return total

    arrive(*yb1)
    y_finish(1, *ends1)
    mix_out(1)
    arrive(*ea, shared=True)
    R.f_send[...] = total_of(R.e_recv, n_lat)
    fa = ("lon", lo, n_lon, 8, R.f_send, R.f_recv, R.f_ss, R.f_rs)
    exchange(*fa, shared=True)
    arrive(*yb0)
    y_finish(0, *ends0)
    mix_out(0)
    edges = split_product(
        rows_of([edge_rows[...], R.yf0[pl.ds(half, rows, stride=spec["y_stride0"]), :]]), mats[3]
    )
    edge_rows[pl.ds(0, half), :] = edges[:half] * up_sigma
    edge_rows[pl.ds(half, half), :] = edges[half : 2 * half] * down_sigma
    side = edges[2 * half :] * side_out
    close_columns(side, side)

    def unpair(v, js, values):
        for t in range(0, len(js), 2):
            even, odd = values[t], values[t + 1]
            k = lax.div(js[t], 2)
            out_ref[v, :, pl.ds(pl.multiple_of(k * 128, 128), 128)] = pick(even, swap(odd))
            out_ref[v, :, pl.ds(pl.multiple_of((k + half // 2) * 128, 128), 128)] = pick(swap(even), odd)

    def finish(b, _):
        js = batch(b)
        y = split_product(rows_of([laplace(j) for j in js]), mats[7])
        z0 = [block(temp, (j + 1) * rows) for j in js]
        unpair(0, js, z0)
        unpair(1, js, [block(R.w1, w_at(1, j)) + coupling * z for j, z in zip(js, z0)])
        unpair(2, js, [y[t * rows : (t + 1) * rows] + block(R.w1, w_at(2, j)) for t, j in enumerate(js)])
        return 0

    lax.fori_loop(0, half // 8, finish, 0, unroll=True)

    arrive(*fa, shared=True)
    total = total_of(R.f_recv, n_lon)
    total = total + swap(total)

    rank = (la * n_lon + lo).astype(F32)
    keep = lane[:1] < 64
    strict = (
        lax.broadcasted_iota(jnp.int32, (128, 128), 0) < lax.broadcasted_iota(jnp.int32, (128, 128), 1)
    ).astype(F32)
    before = jnp.zeros((1, 1), F32)
    outs = [jnp.zeros((1, 1), F32)] * 3
    scale = 1.0 / float(rows * n_lat * cols * n_lon)
    for v in range(3):
        mine = jnp.where(keep & (owners[v] == rank), 1.0, 0.0)
        slot = jnp.dot(jnp.broadcast_to(mine, (8, 128)), strict, preferred_element_type=F32)[:1] + before
        before = before + jnp.sum(mine, axis=1, keepdims=True)
        value = total[v : v + 1] * gain[v] * scale * mine
        for k in range(3):
            outs[k] = outs[k] + jnp.sum(jnp.where(slot == float(k), value, 0.0), axis=1, keepdims=True)
    for k in range(3):
        energy_ref[:, k : k + 1] = outs[k]

    for one in (xa1, xb1, xa0, xb0, za1, za0, ya1, yb1, ya0, yb0, ea, fa):
        left_for_good(*one)


def shards(state, sigma, vert, bal_temp, chi_coef, scales, classes, owner):
    dims = (lax.axis_size("lat"), lax.axis_size("lon"), state.shape[1], sigma.shape[2])
    spec, scratch = layout(*dims, scales.shape[0])
    vmem = pl.BlockSpec(memory_space=pltpu.VMEM)
    return pl.pallas_call(
        functools.partial(kernel, dims, spec, tuple(scratch)),
        out_shape=(pltpu.VMEM(state.shape, F32), pltpu.VMEM((1, 3), F32)),
        in_specs=[pl.BlockSpec(memory_space=pltpu.MemorySpace.HBM)] * 8,
        out_specs=(vmem, vmem),
        scratch_shapes=list(scratch.values()),
        compiler_params=pltpu.CompilerParams(
            collective_id=0, has_side_effects=True, vmem_limit_bytes=56 * 1024 * 1024
        ),
        name="covariance",
    )(
        state,
        sigma,
        vert,
        bal_temp,
        chi_coef.reshape(1, -1),
        scales.reshape(1, -1),
        classes.reshape(1, -1),
        owner.reshape(1, -1),
    )


def solution(mesh):
    return jax.shard_map(
        shards,
        mesh=mesh,
        in_specs=(P(None, "lat", "lon"), P(None, "lat", "lon"), P(), P(), P(), P(), P(), P()),
        out_specs=(P(None, "lat", "lon"), P(("lat", "lon"), None)),
        check_vma=False,
    )
```

```python
import functools

import jax
import jax.numpy as jnp
from jax import lax
from jax.experimental import pallas as pl
from jax.experimental.pallas import tpu as pltpu
from jax.sharding import PartitionSpec as P

F32 = jnp.float32
BF16 = jnp.bfloat16
MESH = pl.DeviceIdType.MESH


def split_product(x, w):
    hi = x.astype(BF16)
    lo = (x - hi.astype(F32)).astype(BF16)
    y = jnp.dot(jnp.concatenate([hi, lo], axis=1), w, preferred_element_type=F32)
    return y[:, :128] + y[:, 128:]


def swap(x):
    return pltpu.roll(x, 64, 1)


def rows_of(parts):
    return jnp.concatenate(parts, axis=0)


def layout(n_lat, n_lon, rows, cols, n_class):
    half = cols // 2
    jj_n = half // n_lat
    groups = rows // 8
    spec = {}
    for c, count in enumerate((1, 2)):
        spec[f"x_rows{c}"] = -(-count * groups * 2 // 8) * 8 if c else 2 * rows
        spec[f"y_rows{c}"] = -(-(count * jj_n * 4 + (4 if c == 0 else 0)) // 8) * 8
        spec[f"y_stride{c}"] = count * half + 8
    shapes = {
        "in_sem": 3,
        "small_sem": 7,
        "halo_ss": 4,
        "halo_rs": 4,
        "e_ss": 1,
        "e_rs": 1,
        "f_ss": 1,
        "f_rs": 1,
    }
    for name in shapes:
        shapes[name] = pltpu.SemaphoreType.DMA((shapes[name],))
    vm = lambda r: pltpu.VMEM((r, 128), F32)
    shapes["state"] = pltpu.VMEM((3, rows, cols * 64), F32)
    shapes["sigma"] = pltpu.VMEM((3, rows, cols), F32)
    shapes["vert"] = pltpu.VMEM((3, 64, 64), F32)
    shapes["bal"] = pltpu.VMEM((64, 64), F32)
    shapes["chi"] = pltpu.VMEM((1, 64), F32)
    shapes["scales"] = pltpu.VMEM((1, n_class), F32)
    shapes["classes"] = pltpu.VMEM((1, 192), jnp.int32)
    shapes["owner"] = pltpu.VMEM((1, 192), jnp.int32)
    shapes["mats"] = pltpu.VMEM((8, 256, 256), BF16)
    sizes = {
        "table": 8,
        "pad": 64,
        "sig": 3 * rows,
        "temp": (half + 2) * rows,
        "xtab": 6 * half,
        "ytab": 6 * rows,
        "edge_rows": 2 * half,
        "halo_send": 2 * (half + rows) + 4 * rows,
        "halo_recv": 2 * (half + rows) + 4 * rows,
        "e_send": 8,
        "e_recv": 8 * n_lat,
        "f_send": 8,
        "f_recv": 8 * n_lon,
    }
    for c, count in enumerate((1, 2)):
        for name in ("w", "xs", "xt", "xu", "xv"):
            sizes[f"{name}{c}"] = half * count * rows
        sizes[f"xe{c}"] = 4 * count * rows
        for name in ("yf", "ys", "yt", "yv", "yu"):
            sizes[f"{name}{c}"] = rows * spec[f"y_stride{c}"]
        for name in ("send", "recv", "back", "home"):
            sizes[f"x_{name}{c}"] = n_lon * spec[f"x_rows{c}"]
            if c == 0 and name == "send":
                sizes[f"x_{name}{c}"] = spec[f"x_rows{c}"]
            sizes[f"y_{name}{c}"] = n_lat * spec[f"y_rows{c}"]
        for name in ("send", "recv"):
            sizes[f"z_{name}{c}"] = n_lat * spec[f"y_rows{c}"]
        for name in ("ss", "rs", "bss", "brs"):
            shapes[f"x_{name}{c}"] = pltpu.SemaphoreType.DMA((1,))
            shapes[f"z_{name}{c}"] = pltpu.SemaphoreType.DMA((1,))
            shapes[f"y_{name}{c}"] = pltpu.SemaphoreType.DMA((1,))
    for name, size in sizes.items():
        shapes[name] = vm(size)
    return spec, shapes


CHUNKS = ((0,), (1, 2))


def far_first(n, step):
    ring = lambda d, size: min(d, size - d)
    hops = lambda o: ring(o // step, n // step) + (ring(o % step, step) if step > 2 else 0)
    return sorted(range(1, n), key=lambda o: (-hops(o), o))


class Names:
    def __init__(self, names, refs):
        for name, ref in zip(names, refs):
            setattr(self, name, ref)

    def at(self, name, c):
        return getattr(self, f"{name}{c}")


def kernel(
    dims,
    spec,
    names,
    state_hbm,
    sigma_hbm,
    vert_hbm,
    bal_hbm,
    chi_hbm,
    scales_hbm,
    class_hbm,
    owner_hbm,
    out_ref,
    energy_ref,
    *refs,
):
    n_lat, n_lon, rows, cols = dims
    half = cols // 2
    jj_n = half // n_lat
    groups = rows // 8
    R = Names(names, refs)
    state_ref, table, mats, pad, sig, temp = R.state, R.table, R.mats, R.pad, R.sig, R.temp
    xtab, ytab, edge_rows = R.xtab, R.ytab, R.edge_rows
    halo_send, halo_recv = R.halo_send, R.halo_recv
    la = lax.axis_index("lat")
    lo = lax.axis_index("lon")

    barrier = pltpu.get_barrier_semaphore()
    lat_order, lon_order = far_first(n_lat, 4), far_first(n_lon, 2)
    for o in lat_order:
        pl.semaphore_signal(barrier, inc=1, device_id=(lax.rem(la + o, n_lat), lo), device_id_type=MESH)
    for o in lon_order:
        pl.semaphore_signal(barrier, inc=1, device_id=(la, lax.rem(lo + o, n_lon)), device_id_type=MESH)

    sigma_ref, vert_ref, bal_ref = R.sigma, R.vert, R.bal
    chi_ref, scales_ref, class_ref, owner_ref = R.chi, R.scales, R.classes, R.owner
    small = []
    for i, (src, dst) in enumerate(
        (
            (class_hbm, class_ref),
            (scales_hbm, scales_ref),
            (vert_hbm, vert_ref),
            (bal_hbm, bal_ref),
            (sigma_hbm, sigma_ref),
            (chi_hbm, chi_ref),
            (owner_hbm, owner_ref),
        )
    ):
        small.append(pltpu.make_async_copy(src, dst, R.small_sem.at[i]))
        small[-1].start()
    loads = {}
    for v in (2, 1, 0):
        loads[v] = pltpu.make_async_copy(state_hbm.at[v], state_ref.at[v], R.in_sem.at[v])
        loads[v].start()

    lane = lax.broadcasted_iota(jnp.int32, (8, 128), 1)
    low1 = lane[:1] < 64

    def low(x):
        return jnp.broadcast_to(low1, x.shape)

    def pick(a, b):
        return jnp.where(low(a), a, b)

    for copy in small:
        copy.wait()

    table[...] = jnp.zeros_like(table)

    def levels(row):
        table[0:1, :] = row[:, :128]
        table[1:2, :64] = row[:, 128:]
        pair01 = table[...]
        flip01 = swap(pair01)
        first, second = pick(pair01, flip01), pick(flip01, pair01)
        return [first[0:1], second[0:1], first[1:2]]

    classes = class_ref[...]
    lengths = jnp.zeros(classes.shape, F32)
    for c in range(scales_ref.shape[1]):
        lengths = jnp.where(classes == c, scales_ref[:, c : c + 1], lengths)
    length = levels(lengths)
    owners = levels(owner_ref[...].astype(F32))
    table[0:1, :64] = chi_ref[...]
    coupling = table[...]
    coupling = pick(coupling, swap(coupling))[0:1]
    decay = [jnp.exp(-1.0 / r) for r in length]

    def power(v, k):
        return jnp.exp(-float(k) / length[v])

    def through(v, n):
        a = decay[v]
        return float(n) * power(v, n), a * (1.0 - power(v, 2 * n)) / (1.0 - a * a)

    def fill_table(ref, n):
        pos = lax.broadcasted_iota(jnp.int32, (n, 128), 0).astype(F32)
        for v in range(3):
            a, r = decay[v], length[v]
            first = jnp.exp(-(pos + 1.0) / r)
            tail = 1.0 - jnp.exp(-2.0 * (n - 1.0 - pos) / r)
            second = (pos + 1.0) * first + first * (a * a) * tail / (1.0 - a * a)
            ref[pl.ds(v * n, n), :] = first
            ref[pl.ds((3 + v) * n, n), :] = second

    fill_table(xtab, half)
    fill_table(ytab, rows)

    gain = []
    for v in range(3):
        a = decay[v]
        c = (1.0 - a) / (1.0 + a)
        gain.append(length[v] * jnp.sqrt(length[v]) * (c * c) * (c * c))

    def put_matrix(slot, m):
        pad[:, :64] = m
        top = pad[...]
        full = rows_of([top, swap(top)])
        hi = full.astype(BF16)
        low_part = (full - hi.astype(F32)).astype(BF16)
        mats[slot] = rows_of(
            [
                jnp.concatenate([hi, low_part], axis=1),
                jnp.concatenate([hi, jnp.zeros_like(hi)], axis=1),
            ]
        )

    pad[...] = jnp.zeros_like(pad)
    for v in range(3):
        put_matrix(v, vert_ref[v])
        put_matrix(3 + v, (vert_ref[v] * gain[v][:, :64]).T)
    put_matrix(6, bal_ref[...])
    put_matrix(7, bal_ref[...].T)

    for v in range(3):
        sig[pl.ds(v * rows, rows), :] = jnp.zeros((rows, 128), F32)
        sig[pl.ds(v * rows, rows), :cols] = sigma_ref[v]
    column = jnp.where(lax.broadcasted_iota(jnp.int32, (rows, 128), 1) < 64, 0, half)

    def spread(tile, j):
        return jnp.take_along_axis(tile, column + j, axis=1, mode="promise_in_bounds")

    def block(ref, at):
        return ref[pl.ds(pl.multiple_of(at, 8), rows), :]

    def put_block(ref, at, value):
        ref[pl.ds(pl.multiple_of(at, 8), rows), :] = value


    def pair(v):
        def step(k, _):
            at1 = pl.ds(pl.multiple_of(k * 128, 128), 128)
            at2 = pl.ds(pl.multiple_of((k + half // 2) * 128, 128), 128)
            n1, n2 = state_ref[v, :, at1], state_ref[v, :, at2]
            if v == 0:
                n1 = n1 + coupling * state_ref[1, :, at1]
                n2 = n2 + coupling * state_ref[1, :, at2]
            even = pick(n1, swap(n2))
            odd = pick(swap(n1), n2)
            if v == 2:
                put_block(temp, (2 * k + 1) * rows, even)
                put_block(temp, (2 * k + 2) * rows, odd)
            elif v == 1:
                put_block(R.w1, 4 * k * rows, even)
                put_block(R.w1, (4 * k + 2) * rows, odd)
            else:
                put_block(R.w0, 2 * k * rows, even)
                put_block(R.w0, (2 * k + 1) * rows, odd)
            return 0

        lax.fori_loop(0, half // 2, step, 0, unroll=4)

    def batch(b):
        return [b * 8 + t for t in range(8)]

    def w_at(v, j):
        return j * rows if v == 0 else (2 * j + v - 1) * rows

    def w_ref(v):
        return R.w0 if v == 0 else R.w1

    loads[2].wait()
    pair(2)

    sig0 = sig[pl.ds(0, rows), :]
    msg_r, msg_c = half + rows, 2 * rows
    halo_send[pl.ds(0, half), :] = temp[pl.ds(rows, half, stride=rows), :]
    halo_send[pl.ds(half, rows), :] = sig0
    halo_send[pl.ds(msg_r, half), :] = temp[pl.ds(2 * rows - 1, half, stride=rows), :]
    halo_send[pl.ds(msg_r + half, rows), :] = sig0
    halo_send[pl.ds(2 * msg_r, rows), :] = temp[pl.ds(rows, rows), :]
    halo_send[pl.ds(2 * msg_r + rows, rows), :] = sig0
    halo_send[pl.ds(2 * msg_r + msg_c, rows), :] = temp[pl.ds(half * rows, rows), :]
    halo_send[pl.ds(2 * msg_r + msg_c + rows, rows), :] = sig0

    loads[1].wait()
    pair(1)

    def mix_in(b, _):
        js = batch(b)
        chi = [block(R.w1, w_at(1, j)) for j in js]
        for v, parts in ((1, chi), (2, [block(temp, (j + 1) * rows) for j in js])):
            y = split_product(rows_of(parts), mats[v])
            tile = sig[pl.ds(v * rows, rows), :]
            for t, j in enumerate(js):
                put_block(R.w1, w_at(v, j), y[t * rows : (t + 1) * rows] * spread(tile, j))
        return 0

    lax.fori_loop(0, half // 8, mix_in, 0, unroll=True)

    def tall(per_v):
        return rows_of([jnp.broadcast_to(c, (rows, 128)) for c in per_v])

    def both_ways(n, load, put_s, put_t, times, start):
        def step(q, carry):
            s, t = carry
            r = n - 1 - q
            s = [x + p for x, p in zip(times(s), load(q))]
            put_s(q, s)
            m = times(t)
            put_t(r, m)
            t = [x + p for x, p in zip(m, load(r))]
            return tuple(s), tuple(t)

        return lax.fori_loop(0, n, step, (start, start), unroll=4)

    def x_filter(c):
        vs = CHUNKS[c]
        full = len(vs) * rows
        ax = tall([decay[v] for v in vs])

        def line(ref, j):
            return ref[pl.ds(pl.multiple_of(j * full, 8), full), :]

        def put(ref):
            def go(j, value):
                ref[pl.ds(pl.multiple_of(j * full, 8), full), :] = value[0]

            return go

        w, xs, xt, xu, xv = (R.at(n, c) for n in ("w", "xs", "xt", "xu", "xv"))
        zero = (jnp.zeros((full, 128), F32),)
        times = lambda s: [ax * s[0]]
        (s1,), (t1,) = both_ways(half, lambda j: [line(w, j)], put(xs), put(xt), times, zero)
        second = lambda j: [line(xs, j) + line(xt, j)]
        (s2,), (t2,) = both_ways(half, second, put(xu), put(xv), times, zero)

        ah = tall([power(v, half) for v in vs])
        g1 = tall([through(v, half)[0] for v in vs])
        g2 = tall([through(v, half)[1] for v in vs])
        s1r, t1r, s2r, t2r = swap(s1), swap(t1), swap(s2), swap(t2)
        q0 = pick(ah * s1 + s1r, s2 + g1 * s1r + ah * (s2r + g2 * t1))
        q1 = pick(t1 + ah * t1r, t2r + g1 * t1 + ah * (t2 + g2 * s1r))
        send = R.at("x_send", c)
        for i, q in enumerate((q0, q1)):
            if c == 0:
                send[pl.ds(i * rows, rows), :] = q
                continue
            for g in range(full // 8):
                send[pl.ds(g * 2 + i, 8, stride=spec[f"x_rows{c}"]), :] = q[g * 8 : g * 8 + 8]
        return dict(s1r=s1r, t1r=t1r, s2=s2, t2=t2, ah=ah, g1=g1, g2=g2, ax=ax)

    def remote(axis, other, src, dst, ss, rs):
        device = (other, lo) if axis == "lat" else (la, other)
        return pltpu.make_async_remote_copy(
            src_ref=src,
            dst_ref=dst,
            send_sem=ss.at[0],
            recv_sem=rs.at[0],
            device_id=device,
            device_id_type=MESH,
        )

    def part(ref, slot, size):
        return ref.at[pl.ds(pl.multiple_of(slot * size, 8), size)]

    def way(axis, c, back, k=None):
        me, n = (la, n_lat) if axis == "lat" else (lo, n_lon)
        k = k or ("y" if axis == "lat" else "x")
        size = spec[f"{k.replace('z', 'y')}_rows{c}"]
        a, b, ss, rs = ("back", "home", "bss", "brs") if back else ("send", "recv", "ss", "rs")
        return axis, me, n, size, *(R.at(f"{k}_{name}", c) for name in (a, b, ss, rs))

    def exchange(axis, me, n, size, src, dst, ss, rs, shared=False):
        for o in lat_order if axis == "lat" else lon_order:
            other = lax.rem(me + o, n)
            remote(axis, other, src if shared else part(src, other, size), part(dst, me, size), ss, rs).start()
        pltpu.make_async_copy(src if shared else part(src, me, size), part(dst, me, size), rs.at[0]).start()

    def arrive(axis, me, n, size, src, dst, ss, rs, shared=False):
        remote(axis, lax.rem(me + 1, n), dst, dst, ss, rs).wait_recv()

    def left_for_good(axis, me, n, size, src, dst, ss, rs):
        gone = dst.at[pl.ds(0, (n - 1) * size)]
        remote(axis, lax.rem(me + 1, n), gone, gone, ss, rs).wait_send()

    def by_row(count, jumps, per_v):
        r = lax.broadcasted_iota(jnp.int32, (count, 128), 0)
        out = jnp.broadcast_to(per_v[0], (count, 128))
        for v in range(1, len(per_v)):
            inside = (r >= v * jumps) & (r < (v + 1) * jumps)
            out = jnp.where(inside, jnp.broadcast_to(per_v[v], (count, 128)), out)
        return out

    def scan_states(n, s, t, an, a):
        s_in, total = [], jnp.zeros_like(s[0])
        for e in range(n):
            s_in.append(total)
            total = an * total + s[e]
        t_in, total = [None] * n, -a * total
        for e in reversed(range(n)):
            t_in[e] = total
            total = t[e] + an * total
        return s_in, t_in

    def scan_coefs(vs, count, jumps, n):
        return (
            by_row(count, jumps, [decay[v] for v in vs]),
            by_row(count, jumps, [power(v, n) for v in vs]),
            by_row(count, jumps, [through(v, n)[0] for v in vs]),
            by_row(count, jumps, [through(v, n)[1] for v in vs]),
        )

    def x_scan(c):
        vs = CHUNKS[c]
        count, size = len(vs) * groups, spec[f"x_rows{c}"]
        if c == 0:
            count = rows
            spots = [[pl.ds(e * size + i * rows, rows) for e in range(n_lon)] for i in (0, 1)]
        else:
            spots = [[pl.ds(e * size + i, count, stride=2) for e in range(n_lon)] for i in (0, 1)]
        a_r, an_r, g1_r, g2_r = scan_coefs(vs, count, groups, cols)
        recv, back = R.at("x_recv", c), R.at("x_back", c)
        p0, p1 = ([recv[at, :] for at in line] for line in spots)
        s_in, t_in = scan_states(n_lon, p0, p1, an_r, a_r)
        sr = [swap(x) for x in s_in]
        tr = [swap(x) for x in t_in]
        s_in2, t_in2 = scan_states(
            n_lon,
            [p0[e] + g1_r * sr[e] + g2_r * tr[e] for e in range(n_lon)],
            [p1[e] + g1_r * tr[e] + g2_r * sr[e] for e in range(n_lon)],
            an_r,
            a_r,
        )
        for e in range(n_lon):
            back[spots[0][e], :] = pick(s_in[e], s_in2[e])
            back[spots[1][e], :] = pick(t_in[e], t_in2[e])

    def x_finish(c, k):
        vs = CHUNKS[c]
        full = len(vs) * rows
        stride = spec[f"y_stride{c}"]
        yf, xe = R.at("yf", c), R.at("xe", c)
        xt, xv = R.at("xu", c), R.at("xv", c)

        def got(i):
            if c == 0:
                return block(R.x_back0, lo * spec["x_rows0"] + i * rows)
            home = R.x_home1
            return rows_of(
                [home[pl.ds(g * 2 + i, 8, stride=spec[f"x_rows{c}"]), :] for g in range(full // 8)]
            )

        q0, q1 = got(0), got(1)
        q0r, q1r = swap(q0), swap(q1)
        si, s2i = pick(q0, q0r), pick(q0r, q0)
        ti, t2i = pick(q1, q1r), pick(q1r, q1)
        s_en = pick(si, k["s1r"] + k["ah"] * si)
        t_en = pick(k["t1r"] + k["ah"] * ti, ti)
        s_own = k["s2"] + k["g1"] * s_en + k["g2"] * t_en
        t_own = k["t2"] + k["g1"] * t_en + k["g2"] * s_en
        s2_en = pick(s2i, swap(s_own) + k["ah"] * s2i)
        t2_en = pick(swap(t_own) + k["ah"] * t2i, t2i)
        if c == 0:
            ax = k["ax"]
            side = pick(s2i + ax * (t_own + k["ah"] * t2_en), ax * (s_own + k["ah"] * s2_en) + t2i)
            yf[pl.ds(half, rows, stride=stride), :] = side
            for z in range(1, 8):
                yf[pl.ds(half + z, rows, stride=stride), :] = jnp.zeros((rows, 128), F32)
        for i, value in enumerate((s_en, t_en, s2_en, t2_en)):
            xe[pl.ds(i * full, full), :] = value

        def correct(j, _):
            for i, v in enumerate(vs):
                f0 = xtab[pl.ds(v * half + j, 1), :]
                b0 = xtab[pl.ds(v * half + half - 1 - j, 1), :]
                f1 = xtab[pl.ds((3 + v) * half + j, 1), :]
                b1 = xtab[pl.ds((3 + v) * half + half - 1 - j, 1), :]
                at = i * rows
                value = block(xt, j * full + at) + block(xv, j * full + at)
                value = value + xe[pl.ds(at, rows), :] * f1 + xe[pl.ds(full + at, rows), :] * b1
                value = value + xe[pl.ds(2 * full + at, rows), :] * f0 + xe[pl.ds(3 * full + at, rows), :] * b0
                yf[pl.ds(i * half + j, rows, stride=stride), :] = value
            return 0

        lax.fori_loop(0, half, correct, 0, unroll=4)

    def y_parts(c):
        return [(0, half + 8)] if c == 0 else [(0, half), (half, half)]

    def y_filter(c):
        vs = CHUNKS[c]
        stride = spec[f"y_stride{c}"]
        ends = []
        for v, (base, height) in zip(vs, y_parts(c)):

            def line(name, i):
                return R.at(name, c)[pl.ds(pl.multiple_of(i * stride + base, 8), height), :]

            def put(name):
                def go(i, value):
                    R.at(name, c)[pl.ds(pl.multiple_of(i * stride + base, 8), height), :] = value[0]

                return go

            zero = (jnp.zeros((height, 128), F32),)
            times = lambda s: [decay[v] * s[0]]
            (s1,), (t1,) = both_ways(rows, lambda i: [line("yf", i)], put("ys"), put("yt"), times, zero)
            second = lambda i: [line("ys", i) + line("yt", i)]
            (s2,), (t2,) = both_ways(rows, second, put("yv"), put("yu"), times, zero)
            ends.append((s1, t1, s2, t2))
        s1, t1, s2, t2 = zip(*ends)
        send, size = R.at("y_send", c), spec[f"y_rows{c}"]
        for k, states in enumerate((s1, t1, s2, t2)):
            for i in range(len(vs)):
                put_states(send, size, i, k, states[i])
            if c == 0:
                last = jj_n * 4 + k
                send[pl.ds(last, n_lat, stride=size), :] = jnp.zeros((n_lat, 128), F32)
                send[pl.ds(last, 1), :] = states[0][half : half + 1]
        return s2, t2

    def w_row(v, i):
        every = rows if v == 0 else 2 * rows
        return w_ref(v)[pl.ds((0 if v == 0 else (v - 1) * rows) + i, half, stride=every), :]

    def put_states(send, size, i, k, value):
        for q in range(jj_n):
            send[pl.ds((i * jj_n + q) * 4 + k, n_lat, stride=size), :] = value[q * n_lat : (q + 1) * n_lat]

    def w_states(c):
        send, size, stride = R.at("z_send", c), spec[f"y_rows{c}"], spec[f"y_stride{c}"]
        if c == 0:
            send[...] = jnp.zeros_like(send)
        for i, v in enumerate(CHUNKS[c]):
            base = y_parts(c)[i][0]

            def at(n):
                return pl.ds(pl.multiple_of(n * stride + base, 8), half)

            def put(name):
                def go(n, value):
                    R.at(name, c)[at(n), :] = value[0]

                return go

            zero = (jnp.zeros((half, 128), F32),)
            times = lambda s: [decay[v] * s[0]]
            (s1,), (t1,) = both_ways(rows, lambda n: [w_row(v, n)], put("ys"), put("yt"), times, zero)
            second = lambda n: [R.at("ys", c)[at(n), :] + R.at("yt", c)[at(n), :]]
            skip = lambda n, value: None
            (s2,), (t2,) = both_ways(rows, second, skip, skip, times, zero)
            for k, value in enumerate((s1, t1, s2, t2)):
                put_states(send, size, i, k, value)

    def local_energy(c):
        stride, out = spec[f"y_stride{c}"], []
        for i, v in enumerate(CHUNKS[c]):
            base = y_parts(c)[i][0]

            def step(n, acc):
                at = pl.ds(pl.multiple_of(n * stride + base, 8), half)
                return acc + w_row(v, n) * (R.at("yu", c)[at, :] + R.at("yv", c)[at, :])

            acc = lax.fori_loop(0, rows, step, jnp.zeros((half, 128), F32), unroll=4)
            out.append(jnp.sum(acc, axis=0, keepdims=True))
        return out

    def y_scan(c, energy):
        vs = CHUNKS[c]
        count, size = len(vs) * jj_n + (1 if c == 0 else 0), spec[f"y_rows{c}"]
        jumps = jj_n if c else count
        a_r, an_r, g1_r, g2_r = scan_coefs(vs, count, jumps, rows)
        recv, back = R.at("y_recv", c), R.at("y_back", c)

        def got(k):
            return [recv[pl.ds(e * size + k, count, stride=4), :] for e in range(n_lat)]

        def give(k, values):
            for e in range(n_lat):
                back[pl.ds(e * size + k, count, stride=4), :] = values[e]

        s_in, t_in = scan_states(n_lat, got(0), got(1), an_r, a_r)
        give(0, s_in)
        give(1, t_in)
        p2, p3 = got(2), got(3)
        s_in2, t_in2 = scan_states(
            n_lat,
            [p2[e] + g1_r * s_in[e] + g2_r * t_in[e] for e in range(n_lat)],
            [p3[e] + g1_r * t_in[e] + g2_r * s_in[e] for e in range(n_lat)],
            an_r,
            a_r,
        )
        give(2, s_in2)
        give(3, t_in2)
        w_in = R.at("z_recv", c)
        far = jnp.zeros((count, 128), F32)
        for e in range(n_lat):
            p = [w_in[pl.ds(e * size + k, count, stride=4), :] for k in range(4)]
            far = far + s_in2[e] * p[1] + t_in2[e] * p[0] + s_in[e] * p[3] + t_in[e] * p[2]
        far = a_r * far
        for i, v in enumerate(vs):
            own = jnp.sum(far[i * jj_n : (i + 1) * jj_n], axis=0, keepdims=True)
            R.e_send[pl.ds(v, 1), :] = energy[i] + own

    def y_finish(c, s2, t2):
        home, size = R.at("y_home", c), spec[f"y_rows{c}"]
        for i, v in enumerate(CHUNKS[c]):

            def entering(k):
                parts = [home[pl.ds((i * jj_n + q) * 4 + k, n_lat, stride=size), :] for q in range(jj_n)]
                if c == 0:
                    parts.append(jnp.broadcast_to(home[pl.ds(jj_n * 4 + k, 1), :], (8, 128)))
                return rows_of(parts)

            s_en, t_en, s2_en, t2_en = (entering(k) for k in range(4))
            if c == 0:
                g1v, g2v = through(0, rows)
                an = power(0, rows)
                first = s2_en + decay[0] * (t2[0] + g1v * t_en + g2v * s_en + an * t2_en)
                after = decay[0] * (s2[0] + g1v * s_en + g2v * t_en + an * s2_en) + t2_en
                edge_rows[pl.ds(0, half), :] = first[:half]
                edge_rows[pl.ds(half, half), :] = after[:half]
            base, height = y_parts(c)[i]
            stride = spec[f"y_stride{c}"]
            yt, yv, yf = R.at("yu", c), R.at("yv", c), R.at("yf", c)

            def correct(n, _):
                at = pl.ds(pl.multiple_of(n * stride + base, 8), height)
                f0 = ytab[pl.ds(v * rows + n, 1), :]
                b0 = ytab[pl.ds(v * rows + rows - 1 - n, 1), :]
                f1 = ytab[pl.ds((3 + v) * rows + n, 1), :]
                b1 = ytab[pl.ds((3 + v) * rows + rows - 1 - n, 1), :]
                value = yt[at, :] + yv[at, :] + s_en * f1 + t_en * b1
                yf[at, :] = value + s2_en * f0 + t2_en * b0
                return 0

            lax.fori_loop(0, rows, correct, 0, unroll=2)

    def mix_out(c):
        yf, stride = R.at("yf", c), spec[f"y_stride{c}"]

        def step(b, _):
            js = batch(b)
            for i, v in enumerate(CHUNKS[c]):
                parts = [yf[pl.ds(i * half + j, rows, stride=stride), :] for j in js]
                y = split_product(rows_of(parts), mats[3 + v])
                tile = sig[pl.ds(v * rows, rows), :]
                for t, j in enumerate(js):
                    z = y[t * rows : (t + 1) * rows] * spread(tile, j)
                    if v == 0:
                        put_block(temp, (j + 1) * rows, z)
                    else:
                        put_block(R.w1, w_at(v, j), z)
            return 0

        lax.fori_loop(0, half // 8, step, 0, unroll=True)

    kept = {1: x_filter(1)}
    pl.semaphore_wait(barrier, n_lat + n_lon - 2)

    up = (lax.rem(la + n_lat - 1, n_lat), lo)
    down = (lax.rem(la + 1, n_lat), lo)
    left = (la, lax.rem(lo + n_lon - 1, n_lon))
    right = (la, lax.rem(lo + 1, n_lon))
    starts = (0, msg_r, 2 * msg_r, 2 * msg_r + msg_c)
    sizes = (msg_r, msg_r, msg_c, msg_c)
    halo = []
    for q, device in enumerate((up, down, left, right)):
        here = pl.ds(starts[q], sizes[q])
        copy = pltpu.make_async_remote_copy(
            src_ref=halo_send.at[here],
            dst_ref=halo_recv.at[here],
            send_sem=R.halo_ss.at[q],
            recv_sem=R.halo_rs.at[q],
            device_id=device,
            device_id_type=MESH,
        )
        copy.start()
        halo.append(copy)
    xa1, xb1, xa0 = way("lon", 1, False), way("lon", 1, True), way("lon", 0, False)
    ya1, yb1, ya0, yb0 = way("lat", 1, False), way("lat", 1, True), way("lat", 0, False), way("lat", 0, True)
    za1, za0 = way("lat", 1, False, "z"), way("lat", 0, False, "z")
    exchange(*xa1)

    loads[0].wait()
    pair(0)
    edge_rows[...] = jnp.zeros_like(edge_rows)

    def close_columns(lo_edge, hi_edge):
        put_block(temp, 0, pick(lo_edge, swap(temp[pl.ds(half * rows, rows), :])))
        put_block(temp, (half + 1) * rows, pick(swap(temp[pl.ds(rows, rows), :]), hi_edge))

    zero_block = jnp.zeros((rows, 128), F32)
    close_columns(zero_block, zero_block)
    row_id = lax.broadcasted_iota(jnp.int32, (rows, 128), 0)

    def laplace(j):
        x = block(temp, (j + 1) * rows)
        above = jnp.where(row_id == 0, edge_rows[pl.ds(j, 1), :], pltpu.roll(x, 1, 0))
        below = jnp.where(row_id == rows - 1, edge_rows[pl.ds(half + j, 1), :], pltpu.roll(x, rows - 1, 0))
        return 4.0 * x - above - below - block(temp, j * rows) - block(temp, (j + 2) * rows)

    def mix_psi(b, _):
        js = batch(b)
        y = split_product(rows_of([laplace(j) for j in js]), mats[6])
        y = y + rows_of([block(R.w0, j * rows) for j in js])
        y = split_product(y, mats[0])
        for t, j in enumerate(js):
            put_block(R.w0, j * rows, y[t * rows : (t + 1) * rows] * spread(sig0, j))
        return 0

    lax.fori_loop(0, half // 8, mix_psi, 0, unroll=True)

    wide = jnp.broadcast_to(low1, (half, 128))

    def row_sigma(tile, r):
        t = jnp.concatenate([tile, jnp.zeros((128 - rows, 128), F32)], axis=0).T
        a = jnp.broadcast_to(t[:half, r : r + 1], (half, 128))
        b = jnp.broadcast_to(t[half : 2 * half, r : r + 1], (half, 128))
        return jnp.where(wide, a, b)

    lane_r = lax.broadcasted_iota(jnp.int32, (rows, 128), 1)

    def side_sigma(a, at_a, b, at_b):
        take = lambda x, at: jnp.take_along_axis(
            x, jnp.full((rows, 128), at, jnp.int32), axis=1, mode="promise_in_bounds"
        )
        return jnp.where(lane_r < 64, take(a, at_a), take(b, at_b))

    own_up, own_down = row_sigma(sig0, 0), row_sigma(sig0, rows - 1)
    own_side = side_sigma(sig0, 0, sig0, cols - 1)

    arrive(*xa1)
    x_scan(1)
    exchange(*xb1)

    for copy in halo:
        copy.wait()
    has_up = jnp.where(la > 0, 1.0, 0.0).astype(F32)
    has_down = jnp.where(la < n_lat - 1, 1.0, 0.0).astype(F32)
    has_left = jnp.where(lo > 0, 1.0, 0.0).astype(F32)
    has_right = jnp.where(lo < n_lon - 1, 1.0, 0.0).astype(F32)
    from_right = swap(halo_recv[pl.ds(2 * msg_r, rows), :]) * has_right
    from_left = swap(halo_recv[pl.ds(2 * msg_r + msg_c, rows), :]) * has_left
    outside = rows_of(
        [
            halo_recv[pl.ds(msg_r, half), :] * has_up,
            halo_recv[pl.ds(0, half), :] * has_down,
            pick(from_left, from_right),
        ]
    )
    outside = split_product(split_product(outside, mats[6]), mats[0])
    first_rows = pl.ds(0, half, stride=rows)
    last_rows = pl.ds(rows - 1, half, stride=rows)
    R.w0[first_rows, :] = R.w0[first_rows, :] - outside[:half] * own_up
    R.w0[last_rows, :] = R.w0[last_rows, :] - outside[half : 2 * half] * own_down
    side = outside[2 * half :] * own_side
    at_last = pl.ds((half - 1) * rows, rows)
    R.w0[pl.ds(0, rows), :] = R.w0[pl.ds(0, rows), :] - pick(side, zero_block)
    R.w0[at_last, :] = R.w0[at_last, :] - pick(zero_block, side)

    kept[0] = x_filter(0)
    exchange(*xa0, shared=True)
    w_states(1)
    exchange(*za1)
    w_states(0)
    exchange(*za0)

    arrive(*xb1)
    x_finish(1, kept[1])
    ends1 = y_filter(1)
    exchange(*ya1)
    arrive(*xa0, shared=True)
    x_scan(0)
    x_finish(0, kept[0])
    ends0 = y_filter(0)
    exchange(*ya0)

    up_sigma = row_sigma(halo_recv[pl.ds(msg_r + half, rows), :] * has_up, rows - 1)
    down_sigma = row_sigma(halo_recv[pl.ds(half, rows), :] * has_down, 0)
    side_out = side_sigma(
        halo_recv[pl.ds(2 * msg_r + msg_c + rows, rows), :] * has_left,
        cols - 1,
        halo_recv[pl.ds(2 * msg_r + rows, rows), :] * has_right,
        0,
    )

    R.e_send[...] = jnp.zeros_like(R.e_send)
    near1, near0 = local_energy(1), local_energy(0)

    arrive(*za1)
    arrive(*ya1)
    y_scan(1, near1)
    exchange(*yb1)
    arrive(*za0)
    arrive(*ya0)
    y_scan(0, near0)
    ea = ("lat", la, n_lat, 8, R.e_send, R.e_recv, R.e_ss, R.e_rs)
    exchange(*ea, shared=True)
    exchange(*yb0)

    def total_of(ref, n):
        total = ref[pl.ds(0, 8), :]
        for e in range(1, n):
            total = total + ref[pl.ds(e * 8, 8), :]
        return total

    arrive(*ea, shared=True)
    R.f_send[...] = total_of(R.e_recv, n_lat)
    fa = ("lon", lo, n_lon, 8, R.f_send, R.f_recv, R.f_ss, R.f_rs)
    exchange(*fa, shared=True)
    arrive(*yb1)
    y_finish(1, *ends1)
    mix_out(1)
    arrive(*yb0)
    y_finish(0, *ends0)
    mix_out(0)
    edges = split_product(
        rows_of([edge_rows[...], R.yf0[pl.ds(half, rows, stride=spec["y_stride0"]), :]]), mats[3]
    )
    edge_rows[pl.ds(0, half), :] = edges[:half] * up_sigma
    edge_rows[pl.ds(half, half), :] = edges[half : 2 * half] * down_sigma
    side = edges[2 * half :] * side_out
    close_columns(side, side)

    def unpair(v, js, values):
        for t in range(0, len(js), 2):
            even, odd = values[t], values[t + 1]
            k = lax.div(js[t], 2)
            out_ref[v, :, pl.ds(pl.multiple_of(k * 128, 128), 128)] = pick(even, swap(odd))
            out_ref[v, :, pl.ds(pl.multiple_of((k + half // 2) * 128, 128), 128)] = pick(swap(even), odd)

    def finish(b, _):
        js = batch(b)
        y = split_product(rows_of([laplace(j) for j in js]), mats[7])
        z0 = [block(temp, (j + 1) * rows) for j in js]
        unpair(0, js, z0)
        unpair(1, js, [block(R.w1, w_at(1, j)) + coupling * z for j, z in zip(js, z0)])
        unpair(2, js, [y[t * rows : (t + 1) * rows] + block(R.w1, w_at(2, j)) for t, j in enumerate(js)])
        return 0

    lax.fori_loop(0, half // 8, finish, 0, unroll=True)

    arrive(*fa, shared=True)
    total = total_of(R.f_recv, n_lon)
    total = total + swap(total)

    rank = (la * n_lon + lo).astype(F32)
    keep = lane[:1] < 64
    strict = (
        lax.broadcasted_iota(jnp.int32, (128, 128), 0) < lax.broadcasted_iota(jnp.int32, (128, 128), 1)
    ).astype(F32)
    before = jnp.zeros((1, 1), F32)
    outs = [jnp.zeros((1, 1), F32)] * 3
    scale = 1.0 / float(rows * n_lat * cols * n_lon)
    for v in range(3):
        mine = jnp.where(keep & (owners[v] == rank), 1.0, 0.0)
        slot = jnp.dot(jnp.broadcast_to(mine, (8, 128)), strict, preferred_element_type=F32)[:1] + before
        before = before + jnp.sum(mine, axis=1, keepdims=True)
        value = total[v : v + 1] * gain[v] * scale * mine
        for k in range(3):
            outs[k] = outs[k] + jnp.sum(jnp.where(slot == float(k), value, 0.0), axis=1, keepdims=True)
    for k in range(3):
        energy_ref[:, k : k + 1] = outs[k]

    for one in (xa1, xb1, xa0, za1, za0, ya1, yb1, ya0, yb0, ea, fa):
        left_for_good(*one)


def shards(state, sigma, vert, bal_temp, chi_coef, scales, classes, owner):
    dims = (lax.axis_size("lat"), lax.axis_size("lon"), state.shape[1], sigma.shape[2])
    spec, scratch = layout(*dims, scales.shape[0])
    vmem = pl.BlockSpec(memory_space=pltpu.VMEM)
    return pl.pallas_call(
        functools.partial(kernel, dims, spec, tuple(scratch)),
        out_shape=(pltpu.VMEM(state.shape, F32), pltpu.VMEM((1, 3), F32)),
        in_specs=[pl.BlockSpec(memory_space=pltpu.MemorySpace.HBM)] * 8,
        out_specs=(vmem, vmem),
        scratch_shapes=list(scratch.values()),
        compiler_params=pltpu.CompilerParams(
            collective_id=0, has_side_effects=True, vmem_limit_bytes=56 * 1024 * 1024
        ),
        name="covariance",
    )(
        state,
        sigma,
        vert,
        bal_temp,
        chi_coef.reshape(1, -1),
        scales.reshape(1, -1),
        classes.reshape(1, -1),
        owner.reshape(1, -1),
    )


def solution(mesh):
    return jax.shard_map(
        shards,
        mesh=mesh,
        in_specs=(P(None, "lat", "lon"), P(None, "lat", "lon"), P(), P(), P(), P(), P(), P()),
        out_specs=(P(None, "lat", "lon"), P(("lat", "lon"), None)),
        check_vma=False,
    )
```

```python
import functools

import jax
import jax.numpy as jnp
from jax import lax
from jax.experimental import pallas as pl
from jax.experimental.pallas import tpu as pltpu
from jax.sharding import PartitionSpec as P

F32 = jnp.float32
BF16 = jnp.bfloat16
MESH = pl.DeviceIdType.MESH


def split_product(x, w):
    hi = x.astype(BF16)
    lo = (x - hi.astype(F32)).astype(BF16)
    y = jnp.dot(jnp.concatenate([hi, lo], axis=1), w, preferred_element_type=F32)
    return y[:, :128] + y[:, 128:]


def swap(x):
    return pltpu.roll(x, 64, 1)


def rows_of(parts):
    return jnp.concatenate(parts, axis=0)


def layout(n_lat, n_lon, rows, cols, n_class):
    half = cols // 2
    jj_n = half // n_lat
    groups = rows // 8
    spec = {}
    for c, count in enumerate((1, 2)):
        spec[f"x_rows{c}"] = -(-count * groups * 2 // 8) * 8 if c else 2 * rows
        spec[f"y_rows{c}"] = -(-(count * jj_n * 4 + (4 if c == 0 else 0)) // 8) * 8
        spec[f"y_stride{c}"] = count * half + 8
    shapes = {
        "in_sem": 3,
        "small_sem": 7,
        "halo_ss": 4,
        "halo_rs": 4,
        "e_ss": 1,
        "e_rs": 1,
        "f_ss": 1,
        "f_rs": 1,
    }
    for name in shapes:
        shapes[name] = pltpu.SemaphoreType.DMA((shapes[name],))
    vm = lambda r: pltpu.VMEM((r, 128), F32)
    shapes["state"] = pltpu.VMEM((3, rows, cols * 64), F32)
    shapes["sigma"] = pltpu.VMEM((3, rows, cols), F32)
    shapes["vert"] = pltpu.VMEM((3, 64, 64), F32)
    shapes["bal"] = pltpu.VMEM((64, 64), F32)
    shapes["chi"] = pltpu.VMEM((1, 64), F32)
    shapes["scales"] = pltpu.VMEM((1, n_class), F32)
    shapes["classes"] = pltpu.VMEM((1, 192), jnp.int32)
    shapes["owner"] = pltpu.VMEM((1, 192), jnp.int32)
    shapes["mats"] = pltpu.VMEM((8, 256, 256), BF16)
    sizes = {
        "table": 8,
        "pad": 64,
        "sig": 3 * rows,
        "temp": (half + 2) * rows,
        "xtab": 6 * half,
        "ytab": 6 * rows,
        "edge_rows": 2 * half,
        "halo_send": 2 * (half + rows) + 4 * rows,
        "halo_recv": 2 * (half + rows) + 4 * rows,
        "e_send": 8,
        "e_recv": 8 * n_lat,
        "f_send": 8,
        "f_recv": 8 * n_lon,
    }
    for c, count in enumerate((1, 2)):
        for name in ("w", "xs", "xt", "xu", "xv"):
            sizes[f"{name}{c}"] = half * count * rows
        sizes[f"xe{c}"] = 4 * count * rows
        for name in ("yf", "ys", "yt", "yv", "yu"):
            sizes[f"{name}{c}"] = rows * spec[f"y_stride{c}"]
        for name in ("send", "recv", "back", "home"):
            sizes[f"x_{name}{c}"] = n_lon * spec[f"x_rows{c}"]
            if c == 0 and name == "send":
                sizes[f"x_{name}{c}"] = spec[f"x_rows{c}"]
            sizes[f"y_{name}{c}"] = n_lat * spec[f"y_rows{c}"]
        for name in ("send", "recv"):
            sizes[f"z_{name}{c}"] = n_lat * spec[f"y_rows{c}"]
        for name in ("ss", "rs", "bss", "brs"):
            shapes[f"x_{name}{c}"] = pltpu.SemaphoreType.DMA((1,))
            shapes[f"z_{name}{c}"] = pltpu.SemaphoreType.DMA((1,))
            shapes[f"y_{name}{c}"] = pltpu.SemaphoreType.DMA((1,))
    for name, size in sizes.items():
        shapes[name] = vm(size)
    return spec, shapes


CHUNKS = ((0,), (1, 2))


def far_first(n, step):
    ring = lambda d, size: min(d, size - d)
    hops = lambda o: ring(o // step, n // step) + (ring(o % step, step) if step > 2 else 0)
    return sorted(range(1, n), key=lambda o: (-hops(o), o))


class Names:
    def __init__(self, names, refs):
        for name, ref in zip(names, refs):
            setattr(self, name, ref)

    def at(self, name, c):
        return getattr(self, f"{name}{c}")


def kernel(
    dims,
    spec,
    names,
    state_hbm,
    sigma_hbm,
    vert_hbm,
    bal_hbm,
    chi_hbm,
    scales_hbm,
    class_hbm,
    owner_hbm,
    out_ref,
    energy_ref,
    *refs,
):
    n_lat, n_lon, rows, cols = dims
    half = cols // 2
    jj_n = half // n_lat
    groups = rows // 8
    R = Names(names, refs)
    state_ref, table, mats, pad, sig, temp = R.state, R.table, R.mats, R.pad, R.sig, R.temp
    xtab, ytab, edge_rows = R.xtab, R.ytab, R.edge_rows
    halo_send, halo_recv = R.halo_send, R.halo_recv
    la = lax.axis_index("lat")
    lo = lax.axis_index("lon")

    barrier = pltpu.get_barrier_semaphore()
    lat_order, lon_order = far_first(n_lat, 4), far_first(n_lon, 2)
    for o in lat_order:
        pl.semaphore_signal(barrier, inc=1, device_id=(lax.rem(la + o, n_lat), lo), device_id_type=MESH)
    for o in lon_order:
        pl.semaphore_signal(barrier, inc=1, device_id=(la, lax.rem(lo + o, n_lon)), device_id_type=MESH)

    sigma_ref, vert_ref, bal_ref = R.sigma, R.vert, R.bal
    chi_ref, scales_ref, class_ref, owner_ref = R.chi, R.scales, R.classes, R.owner
    small = []
    for i, (src, dst) in enumerate(
        (
            (class_hbm, class_ref),
            (scales_hbm, scales_ref),
            (vert_hbm, vert_ref),
            (bal_hbm, bal_ref),
            (sigma_hbm, sigma_ref),
            (chi_hbm, chi_ref),
            (owner_hbm, owner_ref),
        )
    ):
        small.append(pltpu.make_async_copy(src, dst, R.small_sem.at[i]))
        small[-1].start()
    loads = {}
    for v in (2, 1, 0):
        loads[v] = pltpu.make_async_copy(state_hbm.at[v], state_ref.at[v], R.in_sem.at[v])
        loads[v].start()

    lane = lax.broadcasted_iota(jnp.int32, (8, 128), 1)
    low1 = lane[:1] < 64

    def low(x):
        return jnp.broadcast_to(low1, x.shape)

    def pick(a, b):
        return jnp.where(low(a), a, b)

    for copy in small:
        copy.wait()

    table[...] = jnp.zeros_like(table)

    def levels(row):
        table[0:1, :] = row[:, :128]
        table[1:2, :64] = row[:, 128:]
        pair01 = table[...]
        flip01 = swap(pair01)
        first, second = pick(pair01, flip01), pick(flip01, pair01)
        return [first[0:1], second[0:1], first[1:2]]

    classes = class_ref[...]
    lengths = jnp.zeros(classes.shape, F32)
    for c in range(scales_ref.shape[1]):
        lengths = jnp.where(classes == c, scales_ref[:, c : c + 1], lengths)
    length = levels(lengths)
    owners = levels(owner_ref[...].astype(F32))
    table[0:1, :64] = chi_ref[...]
    coupling = table[...]
    coupling = pick(coupling, swap(coupling))[0:1]
    decay = [jnp.exp(-1.0 / r) for r in length]

    def power(v, k):
        return jnp.exp(-float(k) / length[v])

    def through(v, n):
        a = decay[v]
        return float(n) * power(v, n), a * (1.0 - power(v, 2 * n)) / (1.0 - a * a)

    def fill_table(ref, n):
        pos = lax.broadcasted_iota(jnp.int32, (n, 128), 0).astype(F32)
        for v in range(3):
            a, r = decay[v], length[v]
            first = jnp.exp(-(pos + 1.0) / r)
            tail = 1.0 - jnp.exp(-2.0 * (n - 1.0 - pos) / r)
            second = (pos + 1.0) * first + first * (a * a) * tail / (1.0 - a * a)
            ref[pl.ds(v * n, n), :] = first
            ref[pl.ds((3 + v) * n, n), :] = second

    fill_table(xtab, half)
    fill_table(ytab, rows)

    gain = []
    for v in range(3):
        a = decay[v]
        c = (1.0 - a) / (1.0 + a)
        gain.append(length[v] * jnp.sqrt(length[v]) * (c * c) * (c * c))

    def put_matrix(slot, m):
        pad[:, :64] = m
        top = pad[...]
        full = rows_of([top, swap(top)])
        hi = full.astype(BF16)
        low_part = (full - hi.astype(F32)).astype(BF16)
        mats[slot] = rows_of(
            [
                jnp.concatenate([hi, low_part], axis=1),
                jnp.concatenate([hi, jnp.zeros_like(hi)], axis=1),
            ]
        )

    pad[...] = jnp.zeros_like(pad)
    for v in range(3):
        put_matrix(v, vert_ref[v])
        put_matrix(3 + v, (vert_ref[v] * gain[v][:, :64]).T)
    put_matrix(6, bal_ref[...])
    put_matrix(7, bal_ref[...].T)

    for v in range(3):
        sig[pl.ds(v * rows, rows), :] = jnp.zeros((rows, 128), F32)
        sig[pl.ds(v * rows, rows), :cols] = sigma_ref[v]
    column = jnp.where(lax.broadcasted_iota(jnp.int32, (rows, 128), 1) < 64, 0, half)

    def spread(tile, j):
        return jnp.take_along_axis(tile, column + j, axis=1, mode="promise_in_bounds")

    def block(ref, at):
        return ref[pl.ds(pl.multiple_of(at, 8), rows), :]

    def put_block(ref, at, value):
        ref[pl.ds(pl.multiple_of(at, 8), rows), :] = value


    def pair(v):
        def step(k, _):
            at1 = pl.ds(pl.multiple_of(k * 128, 128), 128)
            at2 = pl.ds(pl.multiple_of((k + half // 2) * 128, 128), 128)
            n1, n2 = state_ref[v, :, at1], state_ref[v, :, at2]
            if v == 0:
                n1 = n1 + coupling * state_ref[1, :, at1]
                n2 = n2 + coupling * state_ref[1, :, at2]
            even = pick(n1, swap(n2))
            odd = pick(swap(n1), n2)
            if v == 2:
                put_block(temp, (2 * k + 1) * rows, even)
                put_block(temp, (2 * k + 2) * rows, odd)
            elif v == 1:
                put_block(R.w1, 4 * k * rows, even)
                put_block(R.w1, (4 * k + 2) * rows, odd)
            else:
                put_block(R.w0, 2 * k * rows, even)
                put_block(R.w0, (2 * k + 1) * rows, odd)
            return 0

        lax.fori_loop(0, half // 2, step, 0, unroll=4)

    def batch(b):
        return [b * 8 + t for t in range(8)]

    def w_at(v, j):
        return j * rows if v == 0 else (2 * j + v - 1) * rows

    def w_ref(v):
        return R.w0 if v == 0 else R.w1

    loads[2].wait()
    pair(2)

    sig0 = sig[pl.ds(0, rows), :]
    msg_r, msg_c = half + rows, 2 * rows
    halo_send[pl.ds(0, half), :] = temp[pl.ds(rows, half, stride=rows), :]
    halo_send[pl.ds(half, rows), :] = sig0
    halo_send[pl.ds(msg_r, half), :] = temp[pl.ds(2 * rows - 1, half, stride=rows), :]
    halo_send[pl.ds(msg_r + half, rows), :] = sig0
    halo_send[pl.ds(2 * msg_r, rows), :] = temp[pl.ds(rows, rows), :]
    halo_send[pl.ds(2 * msg_r + rows, rows), :] = sig0
    halo_send[pl.ds(2 * msg_r + msg_c, rows), :] = temp[pl.ds(half * rows, rows), :]
    halo_send[pl.ds(2 * msg_r + msg_c + rows, rows), :] = sig0

    loads[1].wait()
    pair(1)

    def mix_in(b, _):
        js = batch(b)
        chi = [block(R.w1, w_at(1, j)) for j in js]
        for v, parts in ((1, chi), (2, [block(temp, (j + 1) * rows) for j in js])):
            y = split_product(rows_of(parts), mats[v])
            tile = sig[pl.ds(v * rows, rows), :]
            for t, j in enumerate(js):
                put_block(R.w1, w_at(v, j), y[t * rows : (t + 1) * rows] * spread(tile, j))
        return 0

    lax.fori_loop(0, half // 8, mix_in, 0, unroll=True)

    def tall(per_v):
        return rows_of([jnp.broadcast_to(c, (rows, 128)) for c in per_v])

    def both_ways(n, load, put_s, put_t, times, start):
        def step(q, carry):
            s, t = carry
            r = n - 1 - q
            s = [x + p for x, p in zip(times(s), load(q))]
            put_s(q, s)
            m = times(t)
            put_t(r, m)
            t = [x + p for x, p in zip(m, load(r))]
            return tuple(s), tuple(t)

        return lax.fori_loop(0, n, step, (start, start), unroll=4)

    def x_filter(c):
        vs = CHUNKS[c]
        full = len(vs) * rows
        ax = tall([decay[v] for v in vs])

        def line(ref, j):
            return ref[pl.ds(pl.multiple_of(j * full, 8), full), :]

        def put(ref):
            def go(j, value):
                ref[pl.ds(pl.multiple_of(j * full, 8), full), :] = value[0]

            return go

        w, xs, xt, xu, xv = (R.at(n, c) for n in ("w", "xs", "xt", "xu", "xv"))
        zero = (jnp.zeros((full, 128), F32),)
        times = lambda s: [ax * s[0]]
        (s1,), (t1,) = both_ways(half, lambda j: [line(w, j)], put(xs), put(xt), times, zero)
        second = lambda j: [line(xs, j) + line(xt, j)]
        (s2,), (t2,) = both_ways(half, second, put(xu), put(xv), times, zero)

        ah = tall([power(v, half) for v in vs])
        g1 = tall([through(v, half)[0] for v in vs])
        g2 = tall([through(v, half)[1] for v in vs])
        s1r, t1r, s2r, t2r = swap(s1), swap(t1), swap(s2), swap(t2)
        q0 = pick(ah * s1 + s1r, s2 + g1 * s1r + ah * (s2r + g2 * t1))
        q1 = pick(t1 + ah * t1r, t2r + g1 * t1 + ah * (t2 + g2 * s1r))
        send = R.at("x_send", c)
        for i, q in enumerate((q0, q1)):
            if c == 0:
                send[pl.ds(i * rows, rows), :] = q
                continue
            for g in range(full // 8):
                send[pl.ds(g * 2 + i, 8, stride=spec[f"x_rows{c}"]), :] = q[g * 8 : g * 8 + 8]
        return dict(s1r=s1r, t1r=t1r, s2=s2, t2=t2, ah=ah, g1=g1, g2=g2, ax=ax)

    def remote(axis, other, src, dst, ss, rs):
        device = (other, lo) if axis == "lat" else (la, other)
        return pltpu.make_async_remote_copy(
            src_ref=src,
            dst_ref=dst,
            send_sem=ss.at[0],
            recv_sem=rs.at[0],
            device_id=device,
            device_id_type=MESH,
        )

    def part(ref, slot, size):
        return ref.at[pl.ds(pl.multiple_of(slot * size, 8), size)]

    def way(axis, c, back, k=None):
        me, n = (la, n_lat) if axis == "lat" else (lo, n_lon)
        k = k or ("y" if axis == "lat" else "x")
        size = spec[f"{k.replace('z', 'y')}_rows{c}"]
        a, b, ss, rs = ("back", "home", "bss", "brs") if back else ("send", "recv", "ss", "rs")
        return axis, me, n, size, *(R.at(f"{k}_{name}", c) for name in (a, b, ss, rs))

    def exchange(axis, me, n, size, src, dst, ss, rs, shared=False):
        for o in lat_order if axis == "lat" else lon_order:
            other = lax.rem(me + o, n)
            remote(axis, other, src if shared else part(src, other, size), part(dst, me, size), ss, rs).start()
        pltpu.make_async_copy(src if shared else part(src, me, size), part(dst, me, size), rs.at[0]).start()

    def arrive(axis, me, n, size, src, dst, ss, rs, shared=False):
        remote(axis, lax.rem(me + 1, n), dst, dst, ss, rs).wait_recv()

    def left_for_good(axis, me, n, size, src, dst, ss, rs):
        gone = dst.at[pl.ds(0, (n - 1) * size)]
        remote(axis, lax.rem(me + 1, n), gone, gone, ss, rs).wait_send()

    def by_row(count, jumps, per_v):
        r = lax.broadcasted_iota(jnp.int32, (count, 128), 0)
        out = jnp.broadcast_to(per_v[0], (count, 128))
        for v in range(1, len(per_v)):
            inside = (r >= v * jumps) & (r < (v + 1) * jumps)
            out = jnp.where(inside, jnp.broadcast_to(per_v[v], (count, 128)), out)
        return out

    def scan_states(n, s, t, an, a):
        s_in, total = [], jnp.zeros_like(s[0])
        for e in range(n):
            s_in.append(total)
            total = an * total + s[e]
        t_in, total = [None] * n, -a * total
        for e in reversed(range(n)):
            t_in[e] = total
            total = t[e] + an * total
        return s_in, t_in

    def scan_coefs(vs, count, jumps, n):
        return (
            by_row(count, jumps, [decay[v] for v in vs]),
            by_row(count, jumps, [power(v, n) for v in vs]),
            by_row(count, jumps, [through(v, n)[0] for v in vs]),
            by_row(count, jumps, [through(v, n)[1] for v in vs]),
        )

    def x_scan(c):
        vs = CHUNKS[c]
        count, size = len(vs) * groups, spec[f"x_rows{c}"]
        if c == 0:
            count = rows
            spots = [[pl.ds(e * size + i * rows, rows) for e in range(n_lon)] for i in (0, 1)]
        else:
            spots = [[pl.ds(e * size + i, count, stride=2) for e in range(n_lon)] for i in (0, 1)]
        a_r, an_r, g1_r, g2_r = scan_coefs(vs, count, groups, cols)
        recv, back = R.at("x_recv", c), R.at("x_back", c)
        p0, p1 = ([recv[at, :] for at in line] for line in spots)
        s_in, t_in = scan_states(n_lon, p0, p1, an_r, a_r)
        sr = [swap(x) for x in s_in]
        tr = [swap(x) for x in t_in]
        s_in2, t_in2 = scan_states(
            n_lon,
            [p0[e] + g1_r * sr[e] + g2_r * tr[e] for e in range(n_lon)],
            [p1[e] + g1_r * tr[e] + g2_r * sr[e] for e in range(n_lon)],
            an_r,
            a_r,
        )
        for e in range(n_lon):
            back[spots[0][e], :] = pick(s_in[e], s_in2[e])
            back[spots[1][e], :] = pick(t_in[e], t_in2[e])

    def x_finish(c, k):
        vs = CHUNKS[c]
        full = len(vs) * rows
        stride = spec[f"y_stride{c}"]
        yf, xe = R.at("yf", c), R.at("xe", c)
        xt, xv = R.at("xu", c), R.at("xv", c)

        def got(i):
            if c == 0:
                return block(R.x_back0, lo * spec["x_rows0"] + i * rows)
            home = R.x_home1
            return rows_of(
                [home[pl.ds(g * 2 + i, 8, stride=spec[f"x_rows{c}"]), :] for g in range(full // 8)]
            )

        q0, q1 = got(0), got(1)
        q0r, q1r = swap(q0), swap(q1)
        si, s2i = pick(q0, q0r), pick(q0r, q0)
        ti, t2i = pick(q1, q1r), pick(q1r, q1)
        s_en = pick(si, k["s1r"] + k["ah"] * si)
        t_en = pick(k["t1r"] + k["ah"] * ti, ti)
        s_own = k["s2"] + k["g1"] * s_en + k["g2"] * t_en
        t_own = k["t2"] + k["g1"] * t_en + k["g2"] * s_en
        s2_en = pick(s2i, swap(s_own) + k["ah"] * s2i)
        t2_en = pick(swap(t_own) + k["ah"] * t2i, t2i)
        if c == 0:
            ax = k["ax"]
            side = pick(s2i + ax * (t_own + k["ah"] * t2_en), ax * (s_own + k["ah"] * s2_en) + t2i)
            yf[pl.ds(half, rows, stride=stride), :] = side
            for z in range(1, 8):
                yf[pl.ds(half + z, rows, stride=stride), :] = jnp.zeros((rows, 128), F32)
        for i, value in enumerate((s_en, t_en, s2_en, t2_en)):
            xe[pl.ds(i * full, full), :] = value

        def correct(j, _):
            for i, v in enumerate(vs):
                f0 = xtab[pl.ds(v * half + j, 1), :]
                b0 = xtab[pl.ds(v * half + half - 1 - j, 1), :]
                f1 = xtab[pl.ds((3 + v) * half + j, 1), :]
                b1 = xtab[pl.ds((3 + v) * half + half - 1 - j, 1), :]
                at = i * rows
                value = block(xt, j * full + at) + block(xv, j * full + at)
                value = value + xe[pl.ds(at, rows), :] * f1 + xe[pl.ds(full + at, rows), :] * b1
                value = value + xe[pl.ds(2 * full + at, rows), :] * f0 + xe[pl.ds(3 * full + at, rows), :] * b0
                yf[pl.ds(i * half + j, rows, stride=stride), :] = value
            return 0

        lax.fori_loop(0, half, correct, 0, unroll=4)

    def y_parts(c):
        return [(0, half + 8)] if c == 0 else [(0, half), (half, half)]

    def y_filter(c):
        vs = CHUNKS[c]
        stride = spec[f"y_stride{c}"]
        ends = []
        for v, (base, height) in zip(vs, y_parts(c)):

            def line(name, i):
                return R.at(name, c)[pl.ds(pl.multiple_of(i * stride + base, 8), height), :]

            def put(name):
                def go(i, value):
                    R.at(name, c)[pl.ds(pl.multiple_of(i * stride + base, 8), height), :] = value[0]

                return go

            zero = (jnp.zeros((height, 128), F32),)
            times = lambda s: [decay[v] * s[0]]
            (s1,), (t1,) = both_ways(rows, lambda i: [line("yf", i)], put("ys"), put("yt"), times, zero)
            second = lambda i: [line("ys", i) + line("yt", i)]
            (s2,), (t2,) = both_ways(rows, second, put("yv"), put("yu"), times, zero)
            ends.append((s1, t1, s2, t2))
        s1, t1, s2, t2 = zip(*ends)
        send, size = R.at("y_send", c), spec[f"y_rows{c}"]
        for k, states in enumerate((s1, t1, s2, t2)):
            for i in range(len(vs)):
                put_states(send, size, i, k, states[i])
            if c == 0:
                last = jj_n * 4 + k
                send[pl.ds(last, n_lat, stride=size), :] = jnp.zeros((n_lat, 128), F32)
                send[pl.ds(last, 1), :] = states[0][half : half + 1]
        return s2, t2

    def w_row(v, i):
        every = rows if v == 0 else 2 * rows
        return w_ref(v)[pl.ds((0 if v == 0 else (v - 1) * rows) + i, half, stride=every), :]

    def put_states(send, size, i, k, value):
        for q in range(jj_n):
            send[pl.ds((i * jj_n + q) * 4 + k, n_lat, stride=size), :] = value[q * n_lat : (q + 1) * n_lat]

    def w_states(c):
        send, size, stride = R.at("z_send", c), spec[f"y_rows{c}"], spec[f"y_stride{c}"]
        if c == 0:
            send[...] = jnp.zeros_like(send)
        for i, v in enumerate(CHUNKS[c]):
            base = y_parts(c)[i][0]

            def at(n):
                return pl.ds(pl.multiple_of(n * stride + base, 8), half)

            def put(name):
                def go(n, value):
                    R.at(name, c)[at(n), :] = value[0]

                return go

            zero = (jnp.zeros((half, 128), F32),)
            times = lambda s: [decay[v] * s[0]]
            (s1,), (t1,) = both_ways(rows, lambda n: [w_row(v, n)], put("ys"), put("yt"), times, zero)
            second = lambda n: [R.at("ys", c)[at(n), :] + R.at("yt", c)[at(n), :]]
            skip = lambda n, value: None
            (s2,), (t2,) = both_ways(rows, second, skip, skip, times, zero)
            for k, value in enumerate((s1, t1, s2, t2)):
                put_states(send, size, i, k, value)

    def local_energy(c):
        stride, out = spec[f"y_stride{c}"], []
        for i, v in enumerate(CHUNKS[c]):
            base = y_parts(c)[i][0]

            def step(n, acc):
                at = pl.ds(pl.multiple_of(n * stride + base, 8), half)
                return acc + w_row(v, n) * (R.at("yu", c)[at, :] + R.at("yv", c)[at, :])

            acc = lax.fori_loop(0, rows, step, jnp.zeros((half, 128), F32), unroll=4)
            out.append(jnp.sum(acc, axis=0, keepdims=True))
        return out

    def y_scan(c, energy):
        vs = CHUNKS[c]
        count, size = len(vs) * jj_n + (1 if c == 0 else 0), spec[f"y_rows{c}"]
        jumps = jj_n if c else count
        a_r, an_r, g1_r, g2_r = scan_coefs(vs, count, jumps, rows)
        recv, back = R.at("y_recv", c), R.at("y_back", c)

        def got(k):
            return [recv[pl.ds(e * size + k, count, stride=4), :] for e in range(n_lat)]

        def give(k, values):
            for e in range(n_lat):
                back[pl.ds(e * size + k, count, stride=4), :] = values[e]

        s_in, t_in = scan_states(n_lat, got(0), got(1), an_r, a_r)
        give(0, s_in)
        give(1, t_in)
        p2, p3 = got(2), got(3)
        s_in2, t_in2 = scan_states(
            n_lat,
            [p2[e] + g1_r * s_in[e] + g2_r * t_in[e] for e in range(n_lat)],
            [p3[e] + g1_r * t_in[e] + g2_r * s_in[e] for e in range(n_lat)],
            an_r,
            a_r,
        )
        give(2, s_in2)
        give(3, t_in2)
        w_in = R.at("z_recv", c)
        far = jnp.zeros((count, 128), F32)
        for e in range(n_lat):
            p = [w_in[pl.ds(e * size + k, count, stride=4), :] for k in range(4)]
            far = far + s_in2[e] * p[1] + t_in2[e] * p[0] + s_in[e] * p[3] + t_in[e] * p[2]
        far = a_r * far
        for i, v in enumerate(vs):
            own = jnp.sum(far[i * jj_n : (i + 1) * jj_n], axis=0, keepdims=True)
            R.e_send[pl.ds(v, 1), :] = energy[i] + own

    def y_finish(c, s2, t2):
        home, size = R.at("y_home", c), spec[f"y_rows{c}"]
        for i, v in enumerate(CHUNKS[c]):

            def entering(k):
                parts = [home[pl.ds((i * jj_n + q) * 4 + k, n_lat, stride=size), :] for q in range(jj_n)]
                if c == 0:
                    parts.append(jnp.broadcast_to(home[pl.ds(jj_n * 4 + k, 1), :], (8, 128)))
                return rows_of(parts)

            s_en, t_en, s2_en, t2_en = (entering(k) for k in range(4))
            if c == 0:
                g1v, g2v = through(0, rows)
                an = power(0, rows)
                first = s2_en + decay[0] * (t2[0] + g1v * t_en + g2v * s_en + an * t2_en)
                after = decay[0] * (s2[0] + g1v * s_en + g2v * t_en + an * s2_en) + t2_en
                edge_rows[pl.ds(0, half), :] = first[:half]
                edge_rows[pl.ds(half, half), :] = after[:half]
            base, height = y_parts(c)[i]
            stride = spec[f"y_stride{c}"]
            yt, yv, yf = R.at("yu", c), R.at("yv", c), R.at("yf", c)

            def correct(n, _):
                at = pl.ds(pl.multiple_of(n * stride + base, 8), height)
                f0 = ytab[pl.ds(v * rows + n, 1), :]
                b0 = ytab[pl.ds(v * rows + rows - 1 - n, 1), :]
                f1 = ytab[pl.ds((3 + v) * rows + n, 1), :]
                b1 = ytab[pl.ds((3 + v) * rows + rows - 1 - n, 1), :]
                value = yt[at, :] + yv[at, :] + s_en * f1 + t_en * b1
                yf[at, :] = value + s2_en * f0 + t2_en * b0
                return 0

            lax.fori_loop(0, rows, correct, 0, unroll=2)

    def mix_out(c):
        yf, stride = R.at("yf", c), spec[f"y_stride{c}"]

        def step(b, _):
            js = batch(b)
            for i, v in enumerate(CHUNKS[c]):
                parts = [yf[pl.ds(i * half + j, rows, stride=stride), :] for j in js]
                y = split_product(rows_of(parts), mats[3 + v])
                tile = sig[pl.ds(v * rows, rows), :]
                for t, j in enumerate(js):
                    z = y[t * rows : (t + 1) * rows] * spread(tile, j)
                    if v == 0:
                        put_block(temp, (j + 1) * rows, z)
                    else:
                        put_block(R.w1, w_at(v, j), z)
            return 0

        lax.fori_loop(0, half // 8, step, 0, unroll=True)

    kept = {1: x_filter(1)}
    pl.semaphore_wait(barrier, n_lat + n_lon - 2)

    up = (lax.rem(la + n_lat - 1, n_lat), lo)
    down = (lax.rem(la + 1, n_lat), lo)
    left = (la, lax.rem(lo + n_lon - 1, n_lon))
    right = (la, lax.rem(lo + 1, n_lon))
    starts = (0, msg_r, 2 * msg_r, 2 * msg_r + msg_c)
    sizes = (msg_r, msg_r, msg_c, msg_c)
    halo = []
    for q, device in enumerate((up, down, left, right)):
        here = pl.ds(starts[q], sizes[q])
        copy = pltpu.make_async_remote_copy(
            src_ref=halo_send.at[here],
            dst_ref=halo_recv.at[here],
            send_sem=R.halo_ss.at[q],
            recv_sem=R.halo_rs.at[q],
            device_id=device,
            device_id_type=MESH,
        )
        copy.start()
        halo.append(copy)
    xa1, xb1, xa0 = way("lon", 1, False), way("lon", 1, True), way("lon", 0, False)
    ya1, yb1, ya0, yb0 = way("lat", 1, False), way("lat", 1, True), way("lat", 0, False), way("lat", 0, True)
    za1, za0 = way("lat", 1, False, "z"), way("lat", 0, False, "z")
    exchange(*xa1)

    loads[0].wait()
    pair(0)
    edge_rows[...] = jnp.zeros_like(edge_rows)

    def close_columns(lo_edge, hi_edge):
        put_block(temp, 0, pick(lo_edge, swap(temp[pl.ds(half * rows, rows), :])))
        put_block(temp, (half + 1) * rows, pick(swap(temp[pl.ds(rows, rows), :]), hi_edge))

    zero_block = jnp.zeros((rows, 128), F32)
    close_columns(zero_block, zero_block)
    row_id = lax.broadcasted_iota(jnp.int32, (rows, 128), 0)

    def laplace(j):
        x = block(temp, (j + 1) * rows)
        above = jnp.where(row_id == 0, edge_rows[pl.ds(j, 1), :], pltpu.roll(x, 1, 0))
        below = jnp.where(row_id == rows - 1, edge_rows[pl.ds(half + j, 1), :], pltpu.roll(x, rows - 1, 0))
        return 4.0 * x - above - below - block(temp, j * rows) - block(temp, (j + 2) * rows)

    def mix_psi(b, _):
        js = batch(b)
        y = split_product(rows_of([laplace(j) for j in js]), mats[6])
        y = y + rows_of([block(R.w0, j * rows) for j in js])
        y = split_product(y, mats[0])
        for t, j in enumerate(js):
            put_block(R.w0, j * rows, y[t * rows : (t + 1) * rows] * spread(sig0, j))
        return 0

    lax.fori_loop(0, half // 8, mix_psi, 0, unroll=True)

    wide = jnp.broadcast_to(low1, (half, 128))

    def row_sigma(tile, r):
        t = jnp.concatenate([tile, jnp.zeros((128 - rows, 128), F32)], axis=0).T
        a = jnp.broadcast_to(t[:half, r : r + 1], (half, 128))
        b = jnp.broadcast_to(t[half : 2 * half, r : r + 1], (half, 128))
        return jnp.where(wide, a, b)

    lane_r = lax.broadcasted_iota(jnp.int32, (rows, 128), 1)

    def side_sigma(a, at_a, b, at_b):
        take = lambda x, at: jnp.take_along_axis(
            x, jnp.full((rows, 128), at, jnp.int32), axis=1, mode="promise_in_bounds"
        )
        return jnp.where(lane_r < 64, take(a, at_a), take(b, at_b))

    own_up, own_down = row_sigma(sig0, 0), row_sigma(sig0, rows - 1)
    own_side = side_sigma(sig0, 0, sig0, cols - 1)

    arrive(*xa1)
    x_scan(1)
    exchange(*xb1)

    for copy in halo:
        copy.wait()
    has_up = jnp.where(la > 0, 1.0, 0.0).astype(F32)
    has_down = jnp.where(la < n_lat - 1, 1.0, 0.0).astype(F32)
    has_left = jnp.where(lo > 0, 1.0, 0.0).astype(F32)
    has_right = jnp.where(lo < n_lon - 1, 1.0, 0.0).astype(F32)
    from_right = swap(halo_recv[pl.ds(2 * msg_r, rows), :]) * has_right
    from_left = swap(halo_recv[pl.ds(2 * msg_r + msg_c, rows), :]) * has_left
    outside = rows_of(
        [
            halo_recv[pl.ds(msg_r, half), :] * has_up,
            halo_recv[pl.ds(0, half), :] * has_down,
            pick(from_left, from_right),
        ]
    )
    outside = split_product(split_product(outside, mats[6]), mats[0])
    first_rows = pl.ds(0, half, stride=rows)
    last_rows = pl.ds(rows - 1, half, stride=rows)
    R.w0[first_rows, :] = R.w0[first_rows, :] - outside[:half] * own_up
    R.w0[last_rows, :] = R.w0[last_rows, :] - outside[half : 2 * half] * own_down
    side = outside[2 * half :] * own_side
    at_last = pl.ds((half - 1) * rows, rows)
    R.w0[pl.ds(0, rows), :] = R.w0[pl.ds(0, rows), :] - pick(side, zero_block)
    R.w0[at_last, :] = R.w0[at_last, :] - pick(zero_block, side)

    kept[0] = x_filter(0)
    exchange(*xa0, shared=True)
    w_states(1)
    exchange(*za1)
    w_states(0)
    exchange(*za0)

    arrive(*xb1)
    x_finish(1, kept[1])
    ends1 = y_filter(1)
    exchange(*ya1)
    arrive(*xa0, shared=True)
    x_scan(0)
    x_finish(0, kept[0])
    ends0 = y_filter(0)
    exchange(*ya0)

    up_sigma = row_sigma(halo_recv[pl.ds(msg_r + half, rows), :] * has_up, rows - 1)
    down_sigma = row_sigma(halo_recv[pl.ds(half, rows), :] * has_down, 0)
    side_out = side_sigma(
        halo_recv[pl.ds(2 * msg_r + msg_c + rows, rows), :] * has_left,
        cols - 1,
        halo_recv[pl.ds(2 * msg_r + rows, rows), :] * has_right,
        0,
    )

    R.e_send[...] = jnp.zeros_like(R.e_send)
    near1, near0 = local_energy(1), local_energy(0)

    arrive(*za1)
    arrive(*ya1)
    y_scan(1, near1)
    arrive(*za0)
    arrive(*ya0)
    y_scan(0, near0)
    ea = ("lat", la, n_lat, 8, R.e_send, R.e_recv, R.e_ss, R.e_rs)
    exchange(*ea, shared=True)
    exchange(*yb1)
    exchange(*yb0)

    def total_of(ref, n):
        total = ref[pl.ds(0, 8), :]
        for e in range(1, n):
            total = total + ref[pl.ds(e * 8, 8), :]
        return total

    arrive(*ea, shared=True)
    R.f_send[...] = total_of(R.e_recv, n_lat)
    fa = ("lon", lo, n_lon, 8, R.f_send, R.f_recv, R.f_ss, R.f_rs)
    exchange(*fa, shared=True)
    arrive(*yb1)
    y_finish(1, *ends1)
    mix_out(1)
    arrive(*yb0)
    y_finish(0, *ends0)
    mix_out(0)
    edges = split_product(
        rows_of([edge_rows[...], R.yf0[pl.ds(half, rows, stride=spec["y_stride0"]), :]]), mats[3]
    )
    edge_rows[pl.ds(0, half), :] = edges[:half] * up_sigma
    edge_rows[pl.ds(half, half), :] = edges[half : 2 * half] * down_sigma
    side = edges[2 * half :] * side_out
    close_columns(side, side)

    def unpair(v, js, values):
        for t in range(0, len(js), 2):
            even, odd = values[t], values[t + 1]
            k = lax.div(js[t], 2)
            out_ref[v, :, pl.ds(pl.multiple_of(k * 128, 128), 128)] = pick(even, swap(odd))
            out_ref[v, :, pl.ds(pl.multiple_of((k + half // 2) * 128, 128), 128)] = pick(swap(even), odd)

    def finish(b, _):
        js = batch(b)
        y = split_product(rows_of([laplace(j) for j in js]), mats[7])
        z0 = [block(temp, (j + 1) * rows) for j in js]
        unpair(0, js, z0)
        unpair(1, js, [block(R.w1, w_at(1, j)) + coupling * z for j, z in zip(js, z0)])
        unpair(2, js, [y[t * rows : (t + 1) * rows] + block(R.w1, w_at(2, j)) for t, j in enumerate(js)])
        return 0

    lax.fori_loop(0, half // 8, finish, 0, unroll=True)

    rank = (la * n_lon + lo).astype(F32)
    strict = (
        lax.broadcasted_iota(jnp.int32, (128, 128), 0) < lax.broadcasted_iota(jnp.int32, (128, 128), 1)
    ).astype(F32)
    before = jnp.zeros((1, 1), F32)
    weights = [[], [], []]
    scale = 1.0 / float(rows * n_lat * cols * n_lon)
    for v in range(3):
        mine = jnp.where(low1 & (owners[v] == rank), 1.0, 0.0)
        slot = jnp.dot(jnp.broadcast_to(mine, (8, 128)), strict, preferred_element_type=F32)[:1] + before
        before = before + jnp.sum(mine, axis=1, keepdims=True)
        for k in range(3):
            weights[k].append(jnp.where(slot == float(k), gain[v] * scale * mine, 0.0))
    zeros = jnp.zeros((5, 128), F32)
    weights = [rows_of(line + [zeros]) for line in weights]

    arrive(*fa, shared=True)
    total = total_of(R.f_recv, n_lon)
    total = total + swap(total)
    for k in range(3):
        share = jnp.sum(total * weights[k], axis=0, keepdims=True)
        energy_ref[:, k : k + 1] = jnp.sum(share, axis=1, keepdims=True)

    for one in (xa1, xb1, xa0, za1, za0, ya1, yb1, ya0, yb0, ea, fa):
        left_for_good(*one)


def shards(state, sigma, vert, bal_temp, chi_coef, scales, classes, owner):
    dims = (lax.axis_size("lat"), lax.axis_size("lon"), state.shape[1], sigma.shape[2])
    spec, scratch = layout(*dims, scales.shape[0])
    vmem = pl.BlockSpec(memory_space=pltpu.VMEM)
    return pl.pallas_call(
        functools.partial(kernel, dims, spec, tuple(scratch)),
        out_shape=(pltpu.VMEM(state.shape, F32), pltpu.VMEM((1, 3), F32)),
        in_specs=[pl.BlockSpec(memory_space=pltpu.MemorySpace.HBM)] * 8,
        out_specs=(vmem, vmem),
        scratch_shapes=list(scratch.values()),
        compiler_params=pltpu.CompilerParams(
            collective_id=0, has_side_effects=True, vmem_limit_bytes=56 * 1024 * 1024
        ),
        name="covariance",
    )(
        state,
        sigma,
        vert,
        bal_temp,
        chi_coef.reshape(1, -1),
        scales.reshape(1, -1),
        classes.reshape(1, -1),
        owner.reshape(1, -1),
    )


def solution(mesh):
    return jax.shard_map(
        shards,
        mesh=mesh,
        in_specs=(P(None, "lat", "lon"), P(None, "lat", "lon"), P(), P(), P(), P(), P(), P()),
        out_specs=(P(None, "lat", "lon"), P(("lat", "lon"), None)),
        check_vma=False,
    )
```

```python
import functools

import jax
import jax.numpy as jnp
from jax import lax
from jax.experimental import pallas as pl
from jax.experimental.pallas import tpu as pltpu
from jax.sharding import PartitionSpec as P

F32 = jnp.float32
BF16 = jnp.bfloat16
MESH = pl.DeviceIdType.MESH


def split_product(x, w):
    hi = x.astype(BF16)
    lo = (x - hi.astype(F32)).astype(BF16)
    y = jnp.dot(jnp.concatenate([hi, lo], axis=1), w, preferred_element_type=F32)
    return y[:, :128] + y[:, 128:]


def swap(x):
    return pltpu.roll(x, 64, 1)


def rows_of(parts):
    return jnp.concatenate(parts, axis=0)


def layout(n_lat, n_lon, rows, cols, n_class):
    half = cols // 2
    jj_n = half // n_lat
    groups = rows // 8
    spec = {}
    for c, count in enumerate((1, 2)):
        spec[f"x_rows{c}"] = -(-count * groups * 2 // 8) * 8 if c else 2 * rows
        spec[f"y_rows{c}"] = -(-(count * jj_n * 4 + (4 if c == 0 else 0)) // 8) * 8
        spec[f"y_stride{c}"] = count * half + 8
    shapes = {
        "in_sem": 3,
        "small_sem": 7,
        "halo_ss": 4,
        "halo_rs": 4,
        "e_ss": 1,
        "e_rs": 1,
        "f_ss": 1,
        "f_rs": 1,
    }
    for name in shapes:
        shapes[name] = pltpu.SemaphoreType.DMA((shapes[name],))
    vm = lambda r: pltpu.VMEM((r, 128), F32)
    shapes["state"] = pltpu.VMEM((3, rows, cols * 64), F32)
    shapes["sigma"] = pltpu.VMEM((3, rows, cols), F32)
    shapes["vert"] = pltpu.VMEM((3, 64, 64), F32)
    shapes["bal"] = pltpu.VMEM((64, 64), F32)
    shapes["chi"] = pltpu.VMEM((1, 64), F32)
    shapes["scales"] = pltpu.VMEM((1, n_class), F32)
    shapes["classes"] = pltpu.VMEM((1, 192), jnp.int32)
    shapes["owner"] = pltpu.VMEM((1, 192), jnp.int32)
    shapes["mats"] = pltpu.VMEM((8, 256, 256), BF16)
    sizes = {
        "table": 8,
        "pad": 64,
        "sig": 3 * rows,
        "temp": (half + 2) * rows,
        "xtab": 6 * half,
        "ytab": 6 * rows,
        "edge_rows": 2 * half,
        "halo_send": 2 * (half + rows) + 4 * rows,
        "halo_recv": 2 * (half + rows) + 4 * rows,
        "e_send": 8,
        "e_recv": 8 * n_lon,
        "f_send": 8,
        "f_recv": 8 * n_lat,
    }
    for c, count in enumerate((1, 2)):
        for name in ("w", "xs", "xt", "xu", "xv"):
            sizes[f"{name}{c}"] = half * count * rows
        sizes[f"xe{c}"] = 4 * count * rows
        for name in ("yf", "ys", "yt", "yv", "yu"):
            sizes[f"{name}{c}"] = rows * spec[f"y_stride{c}"]
        for name in ("send", "recv", "back", "home"):
            sizes[f"x_{name}{c}"] = n_lon * spec[f"x_rows{c}"]
            if c == 0 and name == "send":
                sizes[f"x_{name}{c}"] = spec[f"x_rows{c}"]
            sizes[f"y_{name}{c}"] = n_lat * spec[f"y_rows{c}"]
        for name in ("send", "recv"):
            sizes[f"z_{name}{c}"] = n_lat * spec[f"y_rows{c}"]
        for name in ("ss", "rs", "bss", "brs"):
            shapes[f"x_{name}{c}"] = pltpu.SemaphoreType.DMA((1,))
            shapes[f"z_{name}{c}"] = pltpu.SemaphoreType.DMA((1,))
            shapes[f"y_{name}{c}"] = pltpu.SemaphoreType.DMA((1,))
    for name, size in sizes.items():
        shapes[name] = vm(size)
    return spec, shapes


CHUNKS = ((0,), (1, 2))


def far_first(n, step):
    ring = lambda d, size: min(d, size - d)
    hops = lambda o: ring(o // step, n // step) + (ring(o % step, step) if step > 2 else 0)
    return sorted(range(1, n), key=lambda o: (-hops(o), o))


class Names:
    def __init__(self, names, refs):
        for name, ref in zip(names, refs):
            setattr(self, name, ref)

    def at(self, name, c):
        return getattr(self, f"{name}{c}")


def kernel(
    dims,
    spec,
    names,
    state_hbm,
    sigma_hbm,
    vert_hbm,
    bal_hbm,
    chi_hbm,
    scales_hbm,
    class_hbm,
    owner_hbm,
    out_ref,
    energy_ref,
    *refs,
):
    n_lat, n_lon, rows, cols = dims
    half = cols // 2
    jj_n = half // n_lat
    groups = rows // 8
    R = Names(names, refs)
    state_ref, table, mats, pad, sig, temp = R.state, R.table, R.mats, R.pad, R.sig, R.temp
    xtab, ytab, edge_rows = R.xtab, R.ytab, R.edge_rows
    halo_send, halo_recv = R.halo_send, R.halo_recv
    la = lax.axis_index("lat")
    lo = lax.axis_index("lon")

    barrier = pltpu.get_barrier_semaphore()
    lat_order, lon_order = far_first(n_lat, 4), far_first(n_lon, 2)
    for o in lat_order:
        pl.semaphore_signal(barrier, inc=1, device_id=(lax.rem(la + o, n_lat), lo), device_id_type=MESH)
    for o in lon_order:
        pl.semaphore_signal(barrier, inc=1, device_id=(la, lax.rem(lo + o, n_lon)), device_id_type=MESH)

    sigma_ref, vert_ref, bal_ref = R.sigma, R.vert, R.bal
    chi_ref, scales_ref, class_ref, owner_ref = R.chi, R.scales, R.classes, R.owner
    small = []
    for i, (src, dst) in enumerate(
        (
            (class_hbm, class_ref),
            (scales_hbm, scales_ref),
            (vert_hbm, vert_ref),
            (bal_hbm, bal_ref),
            (sigma_hbm, sigma_ref),
            (chi_hbm, chi_ref),
            (owner_hbm, owner_ref),
        )
    ):
        small.append(pltpu.make_async_copy(src, dst, R.small_sem.at[i]))
        small[-1].start()
    loads = {}
    for v in (2, 1, 0):
        loads[v] = pltpu.make_async_copy(state_hbm.at[v], state_ref.at[v], R.in_sem.at[v])
        loads[v].start()

    lane = lax.broadcasted_iota(jnp.int32, (8, 128), 1)
    low1 = lane[:1] < 64

    def low(x):
        return jnp.broadcast_to(low1, x.shape)

    def pick(a, b):
        return jnp.where(low(a), a, b)

    for copy in small:
        copy.wait()

    table[...] = jnp.zeros_like(table)

    def levels(row):
        table[0:1, :] = row[:, :128]
        table[1:2, :64] = row[:, 128:]
        pair01 = table[...]
        flip01 = swap(pair01)
        first, second = pick(pair01, flip01), pick(flip01, pair01)
        return [first[0:1], second[0:1], first[1:2]]

    classes = class_ref[...]
    lengths = jnp.zeros(classes.shape, F32)
    for c in range(scales_ref.shape[1]):
        lengths = jnp.where(classes == c, scales_ref[:, c : c + 1], lengths)
    length = levels(lengths)
    owners = levels(owner_ref[...].astype(F32))
    table[0:1, :64] = chi_ref[...]
    coupling = table[...]
    coupling = pick(coupling, swap(coupling))[0:1]
    decay = [jnp.exp(-1.0 / r) for r in length]

    def power(v, k):
        return jnp.exp(-float(k) / length[v])

    def through(v, n):
        a = decay[v]
        return float(n) * power(v, n), a * (1.0 - power(v, 2 * n)) / (1.0 - a * a)

    def fill_table(ref, n):
        pos = lax.broadcasted_iota(jnp.int32, (n, 128), 0).astype(F32)
        for v in range(3):
            a, r = decay[v], length[v]
            first = jnp.exp(-(pos + 1.0) / r)
            tail = 1.0 - jnp.exp(-2.0 * (n - 1.0 - pos) / r)
            second = (pos + 1.0) * first + first * (a * a) * tail / (1.0 - a * a)
            ref[pl.ds(v * n, n), :] = first
            ref[pl.ds((3 + v) * n, n), :] = second

    fill_table(xtab, half)
    fill_table(ytab, rows)

    gain = []
    for v in range(3):
        a = decay[v]
        c = (1.0 - a) / (1.0 + a)
        gain.append(length[v] * jnp.sqrt(length[v]) * (c * c) * (c * c))

    def put_matrix(slot, m):
        pad[:, :64] = m
        top = pad[...]
        full = rows_of([top, swap(top)])
        hi = full.astype(BF16)
        low_part = (full - hi.astype(F32)).astype(BF16)
        mats[slot] = rows_of(
            [
                jnp.concatenate([hi, low_part], axis=1),
                jnp.concatenate([hi, jnp.zeros_like(hi)], axis=1),
            ]
        )

    pad[...] = jnp.zeros_like(pad)
    for v in range(3):
        put_matrix(v, vert_ref[v])
        put_matrix(3 + v, (vert_ref[v] * gain[v][:, :64]).T)
    put_matrix(6, bal_ref[...])
    put_matrix(7, bal_ref[...].T)

    for v in range(3):
        sig[pl.ds(v * rows, rows), :] = jnp.zeros((rows, 128), F32)
        sig[pl.ds(v * rows, rows), :cols] = sigma_ref[v]
    column = jnp.where(lax.broadcasted_iota(jnp.int32, (rows, 128), 1) < 64, 0, half)

    def spread(tile, j):
        return jnp.take_along_axis(tile, column + j, axis=1, mode="promise_in_bounds")

    def block(ref, at):
        return ref[pl.ds(pl.multiple_of(at, 8), rows), :]

    def put_block(ref, at, value):
        ref[pl.ds(pl.multiple_of(at, 8), rows), :] = value


    def pair(v):
        def step(k, _):
            at1 = pl.ds(pl.multiple_of(k * 128, 128), 128)
            at2 = pl.ds(pl.multiple_of((k + half // 2) * 128, 128), 128)
            n1, n2 = state_ref[v, :, at1], state_ref[v, :, at2]
            if v == 0:
                n1 = n1 + coupling * state_ref[1, :, at1]
                n2 = n2 + coupling * state_ref[1, :, at2]
            even = pick(n1, swap(n2))
            odd = pick(swap(n1), n2)
            if v == 2:
                put_block(temp, (2 * k + 1) * rows, even)
                put_block(temp, (2 * k + 2) * rows, odd)
            elif v == 1:
                put_block(R.w1, 4 * k * rows, even)
                put_block(R.w1, (4 * k + 2) * rows, odd)
            else:
                put_block(R.w0, 2 * k * rows, even)
                put_block(R.w0, (2 * k + 1) * rows, odd)
            return 0

        lax.fori_loop(0, half // 2, step, 0, unroll=4)

    def batch(b):
        return [b * 8 + t for t in range(8)]

    def w_at(v, j):
        return j * rows if v == 0 else (2 * j + v - 1) * rows

    def w_ref(v):
        return R.w0 if v == 0 else R.w1

    loads[2].wait()
    pair(2)

    sig0 = sig[pl.ds(0, rows), :]
    msg_r, msg_c = half + rows, 2 * rows
    halo_send[pl.ds(0, half), :] = temp[pl.ds(rows, half, stride=rows), :]
    halo_send[pl.ds(half, rows), :] = sig0
    halo_send[pl.ds(msg_r, half), :] = temp[pl.ds(2 * rows - 1, half, stride=rows), :]
    halo_send[pl.ds(msg_r + half, rows), :] = sig0
    halo_send[pl.ds(2 * msg_r, rows), :] = temp[pl.ds(rows, rows), :]
    halo_send[pl.ds(2 * msg_r + rows, rows), :] = sig0
    halo_send[pl.ds(2 * msg_r + msg_c, rows), :] = temp[pl.ds(half * rows, rows), :]
    halo_send[pl.ds(2 * msg_r + msg_c + rows, rows), :] = sig0

    loads[1].wait()
    pair(1)

    def mix_in(b, _):
        js = batch(b)
        chi = [block(R.w1, w_at(1, j)) for j in js]
        for v, parts in ((1, chi), (2, [block(temp, (j + 1) * rows) for j in js])):
            y = split_product(rows_of(parts), mats[v])
            tile = sig[pl.ds(v * rows, rows), :]
            for t, j in enumerate(js):
                put_block(R.w1, w_at(v, j), y[t * rows : (t + 1) * rows] * spread(tile, j))
        return 0

    lax.fori_loop(0, half // 8, mix_in, 0, unroll=True)

    def tall(per_v):
        return rows_of([jnp.broadcast_to(c, (rows, 128)) for c in per_v])

    def both_ways(n, load, put_s, put_t, times, start):
        def step(q, carry):
            s, t = carry
            r = n - 1 - q
            s = [x + p for x, p in zip(times(s), load(q))]
            put_s(q, s)
            m = times(t)
            put_t(r, m)
            t = [x + p for x, p in zip(m, load(r))]
            return tuple(s), tuple(t)

        return lax.fori_loop(0, n, step, (start, start), unroll=4)

    def x_filter(c):
        vs = CHUNKS[c]
        full = len(vs) * rows
        ax = tall([decay[v] for v in vs])

        def line(ref, j):
            return ref[pl.ds(pl.multiple_of(j * full, 8), full), :]

        def put(ref):
            def go(j, value):
                ref[pl.ds(pl.multiple_of(j * full, 8), full), :] = value[0]

            return go

        w, xs, xt, xu, xv = (R.at(n, c) for n in ("w", "xs", "xt", "xu", "xv"))
        zero = (jnp.zeros((full, 128), F32),)
        times = lambda s: [ax * s[0]]
        (s1,), (t1,) = both_ways(half, lambda j: [line(w, j)], put(xs), put(xt), times, zero)
        second = lambda j: [line(xs, j) + line(xt, j)]
        (s2,), (t2,) = both_ways(half, second, put(xu), put(xv), times, zero)

        ah = tall([power(v, half) for v in vs])
        g1 = tall([through(v, half)[0] for v in vs])
        g2 = tall([through(v, half)[1] for v in vs])
        s1r, t1r, s2r, t2r = swap(s1), swap(t1), swap(s2), swap(t2)
        q0 = pick(ah * s1 + s1r, s2 + g1 * s1r + ah * (s2r + g2 * t1))
        q1 = pick(t1 + ah * t1r, t2r + g1 * t1 + ah * (t2 + g2 * s1r))
        send = R.at("x_send", c)
        for i, q in enumerate((q0, q1)):
            if c == 0:
                send[pl.ds(i * rows, rows), :] = q
                continue
            for g in range(full // 8):
                send[pl.ds(g * 2 + i, 8, stride=spec[f"x_rows{c}"]), :] = q[g * 8 : g * 8 + 8]
        return dict(s1r=s1r, t1r=t1r, s2=s2, t2=t2, ah=ah, g1=g1, g2=g2, ax=ax)

    def remote(axis, other, src, dst, ss, rs):
        device = (other, lo) if axis == "lat" else (la, other)
        return pltpu.make_async_remote_copy(
            src_ref=src,
            dst_ref=dst,
            send_sem=ss.at[0],
            recv_sem=rs.at[0],
            device_id=device,
            device_id_type=MESH,
        )

    def part(ref, slot, size):
        return ref.at[pl.ds(pl.multiple_of(slot * size, 8), size)]

    def way(axis, c, back, k=None):
        me, n = (la, n_lat) if axis == "lat" else (lo, n_lon)
        k = k or ("y" if axis == "lat" else "x")
        size = spec[f"{k.replace('z', 'y')}_rows{c}"]
        a, b, ss, rs = ("back", "home", "bss", "brs") if back else ("send", "recv", "ss", "rs")
        return axis, me, n, size, *(R.at(f"{k}_{name}", c) for name in (a, b, ss, rs))

    def exchange(axis, me, n, size, src, dst, ss, rs, shared=False):
        for o in lat_order if axis == "lat" else lon_order:
            other = lax.rem(me + o, n)
            remote(axis, other, src if shared else part(src, other, size), part(dst, me, size), ss, rs).start()
        pltpu.make_async_copy(src if shared else part(src, me, size), part(dst, me, size), rs.at[0]).start()

    def arrive(axis, me, n, size, src, dst, ss, rs, shared=False):
        remote(axis, lax.rem(me + 1, n), dst, dst, ss, rs).wait_recv()

    def left_for_good(axis, me, n, size, src, dst, ss, rs):
        gone = dst.at[pl.ds(0, (n - 1) * size)]
        remote(axis, lax.rem(me + 1, n), gone, gone, ss, rs).wait_send()

    def by_row(count, jumps, per_v):
        r = lax.broadcasted_iota(jnp.int32, (count, 128), 0)
        out = jnp.broadcast_to(per_v[0], (count, 128))
        for v in range(1, len(per_v)):
            inside = (r >= v * jumps) & (r < (v + 1) * jumps)
            out = jnp.where(inside, jnp.broadcast_to(per_v[v], (count, 128)), out)
        return out

    def scan_states(n, s, t, an, a):
        s_in, total = [], jnp.zeros_like(s[0])
        for e in range(n):
            s_in.append(total)
            total = an * total + s[e]
        t_in, total = [None] * n, -a * total
        for e in reversed(range(n)):
            t_in[e] = total
            total = t[e] + an * total
        return s_in, t_in

    def scan_coefs(vs, count, jumps, n):
        return (
            by_row(count, jumps, [decay[v] for v in vs]),
            by_row(count, jumps, [power(v, n) for v in vs]),
            by_row(count, jumps, [through(v, n)[0] for v in vs]),
            by_row(count, jumps, [through(v, n)[1] for v in vs]),
        )

    def x_scan(c):
        vs = CHUNKS[c]
        count, size = len(vs) * groups, spec[f"x_rows{c}"]
        if c == 0:
            count = rows
            spots = [[pl.ds(e * size + i * rows, rows) for e in range(n_lon)] for i in (0, 1)]
        else:
            spots = [[pl.ds(e * size + i, count, stride=2) for e in range(n_lon)] for i in (0, 1)]
        a_r, an_r, g1_r, g2_r = scan_coefs(vs, count, groups, cols)
        recv, back = R.at("x_recv", c), R.at("x_back", c)
        p0, p1 = ([recv[at, :] for at in line] for line in spots)
        s_in, t_in = scan_states(n_lon, p0, p1, an_r, a_r)
        sr = [swap(x) for x in s_in]
        tr = [swap(x) for x in t_in]
        s_in2, t_in2 = scan_states(
            n_lon,
            [p0[e] + g1_r * sr[e] + g2_r * tr[e] for e in range(n_lon)],
            [p1[e] + g1_r * tr[e] + g2_r * sr[e] for e in range(n_lon)],
            an_r,
            a_r,
        )
        for e in range(n_lon):
            back[spots[0][e], :] = pick(s_in[e], s_in2[e])
            back[spots[1][e], :] = pick(t_in[e], t_in2[e])

    def x_finish(c, k):
        vs = CHUNKS[c]
        full = len(vs) * rows
        stride = spec[f"y_stride{c}"]
        yf, xe = R.at("yf", c), R.at("xe", c)
        xt, xv = R.at("xu", c), R.at("xv", c)

        def got(i):
            if c == 0:
                return block(R.x_back0, lo * spec["x_rows0"] + i * rows)
            home = R.x_home1
            return rows_of(
                [home[pl.ds(g * 2 + i, 8, stride=spec[f"x_rows{c}"]), :] for g in range(full // 8)]
            )

        q0, q1 = got(0), got(1)
        q0r, q1r = swap(q0), swap(q1)
        si, s2i = pick(q0, q0r), pick(q0r, q0)
        ti, t2i = pick(q1, q1r), pick(q1r, q1)
        s_en = pick(si, k["s1r"] + k["ah"] * si)
        t_en = pick(k["t1r"] + k["ah"] * ti, ti)
        s_own = k["s2"] + k["g1"] * s_en + k["g2"] * t_en
        t_own = k["t2"] + k["g1"] * t_en + k["g2"] * s_en
        s2_en = pick(s2i, swap(s_own) + k["ah"] * s2i)
        t2_en = pick(swap(t_own) + k["ah"] * t2i, t2i)
        if c == 0:
            ax = k["ax"]
            side = pick(s2i + ax * (t_own + k["ah"] * t2_en), ax * (s_own + k["ah"] * s2_en) + t2i)
            yf[pl.ds(half, rows, stride=stride), :] = side
            for z in range(1, 8):
                yf[pl.ds(half + z, rows, stride=stride), :] = jnp.zeros((rows, 128), F32)
        for i, value in enumerate((s_en, t_en, s2_en, t2_en)):
            xe[pl.ds(i * full, full), :] = value

        def correct(j, _):
            for i, v in enumerate(vs):
                f0 = xtab[pl.ds(v * half + j, 1), :]
                b0 = xtab[pl.ds(v * half + half - 1 - j, 1), :]
                f1 = xtab[pl.ds((3 + v) * half + j, 1), :]
                b1 = xtab[pl.ds((3 + v) * half + half - 1 - j, 1), :]
                at = i * rows
                value = block(xt, j * full + at) + block(xv, j * full + at)
                value = value + xe[pl.ds(at, rows), :] * f1 + xe[pl.ds(full + at, rows), :] * b1
                value = value + xe[pl.ds(2 * full + at, rows), :] * f0 + xe[pl.ds(3 * full + at, rows), :] * b0
                yf[pl.ds(i * half + j, rows, stride=stride), :] = value
            return 0

        lax.fori_loop(0, half, correct, 0, unroll=4)

    def y_parts(c):
        return [(0, half + 8)] if c == 0 else [(0, half), (half, half)]

    def y_filter(c):
        vs = CHUNKS[c]
        stride = spec[f"y_stride{c}"]
        ends = []
        for v, (base, height) in zip(vs, y_parts(c)):

            def line(name, i):
                return R.at(name, c)[pl.ds(pl.multiple_of(i * stride + base, 8), height), :]

            def put(name):
                def go(i, value):
                    R.at(name, c)[pl.ds(pl.multiple_of(i * stride + base, 8), height), :] = value[0]

                return go

            zero = (jnp.zeros((height, 128), F32),)
            times = lambda s: [decay[v] * s[0]]
            (s1,), (t1,) = both_ways(rows, lambda i: [line("yf", i)], put("ys"), put("yt"), times, zero)
            second = lambda i: [line("ys", i) + line("yt", i)]
            (s2,), (t2,) = both_ways(rows, second, put("yv"), put("yu"), times, zero)
            ends.append((s1, t1, s2, t2))
        s1, t1, s2, t2 = zip(*ends)
        send, size = R.at("y_send", c), spec[f"y_rows{c}"]
        for k, states in enumerate((s1, t1, s2, t2)):
            for i in range(len(vs)):
                put_states(send, size, i, k, states[i])
            if c == 0:
                last = jj_n * 4 + k
                send[pl.ds(last, n_lat, stride=size), :] = jnp.zeros((n_lat, 128), F32)
                send[pl.ds(last, 1), :] = states[0][half : half + 1]
        return s2, t2

    def w_row(v, i):
        every = rows if v == 0 else 2 * rows
        return w_ref(v)[pl.ds((0 if v == 0 else (v - 1) * rows) + i, half, stride=every), :]

    def put_states(send, size, i, k, value):
        for q in range(jj_n):
            send[pl.ds((i * jj_n + q) * 4 + k, n_lat, stride=size), :] = value[q * n_lat : (q + 1) * n_lat]

    def w_states(c):
        send, size, stride = R.at("z_send", c), spec[f"y_rows{c}"], spec[f"y_stride{c}"]
        if c == 0:
            send[...] = jnp.zeros_like(send)
        for i, v in enumerate(CHUNKS[c]):
            base = y_parts(c)[i][0]

            def at(n):
                return pl.ds(pl.multiple_of(n * stride + base, 8), half)

            def put(name):
                def go(n, value):
                    R.at(name, c)[at(n), :] = value[0]

                return go

            zero = (jnp.zeros((half, 128), F32),)
            times = lambda s: [decay[v] * s[0]]
            (s1,), (t1,) = both_ways(rows, lambda n: [w_row(v, n)], put("ys"), put("yt"), times, zero)
            second = lambda n: [R.at("ys", c)[at(n), :] + R.at("yt", c)[at(n), :]]
            skip = lambda n, value: None
            (s2,), (t2,) = both_ways(rows, second, skip, skip, times, zero)
            for k, value in enumerate((s1, t1, s2, t2)):
                put_states(send, size, i, k, value)

    def local_energy(c):
        stride, out = spec[f"y_stride{c}"], []
        for i, v in enumerate(CHUNKS[c]):
            base = y_parts(c)[i][0]

            def step(n, acc):
                at = pl.ds(pl.multiple_of(n * stride + base, 8), half)
                return acc + w_row(v, n) * (R.at("yu", c)[at, :] + R.at("yv", c)[at, :])

            acc = lax.fori_loop(0, rows, step, jnp.zeros((half, 128), F32), unroll=4)
            out.append(jnp.sum(acc, axis=0, keepdims=True))
        return out

    def y_scan(c, energy):
        vs = CHUNKS[c]
        count, size = len(vs) * jj_n + (1 if c == 0 else 0), spec[f"y_rows{c}"]
        jumps = jj_n if c else count
        a_r, an_r, g1_r, g2_r = scan_coefs(vs, count, jumps, rows)
        recv, back = R.at("y_recv", c), R.at("y_back", c)

        def got(k):
            return [recv[pl.ds(e * size + k, count, stride=4), :] for e in range(n_lat)]

        def give(k, values):
            for e in range(n_lat):
                back[pl.ds(e * size + k, count, stride=4), :] = values[e]

        s_in, t_in = scan_states(n_lat, got(0), got(1), an_r, a_r)
        give(0, s_in)
        give(1, t_in)
        p2, p3 = got(2), got(3)
        s_in2, t_in2 = scan_states(
            n_lat,
            [p2[e] + g1_r * s_in[e] + g2_r * t_in[e] for e in range(n_lat)],
            [p3[e] + g1_r * t_in[e] + g2_r * s_in[e] for e in range(n_lat)],
            an_r,
            a_r,
        )
        give(2, s_in2)
        give(3, t_in2)
        w_in = R.at("z_recv", c)
        far = jnp.zeros((count, 128), F32)
        for e in range(n_lat):
            p = [w_in[pl.ds(e * size + k, count, stride=4), :] for k in range(4)]
            far = far + s_in2[e] * p[1] + t_in2[e] * p[0] + s_in[e] * p[3] + t_in[e] * p[2]
        far = a_r * far
        for i, v in enumerate(vs):
            own = jnp.sum(far[i * jj_n : (i + 1) * jj_n], axis=0, keepdims=True)
            R.e_send[pl.ds(v, 1), :] = energy[i] + own

    def y_finish(c, s2, t2):
        home, size = R.at("y_home", c), spec[f"y_rows{c}"]
        for i, v in enumerate(CHUNKS[c]):

            def entering(k):
                parts = [home[pl.ds((i * jj_n + q) * 4 + k, n_lat, stride=size), :] for q in range(jj_n)]
                if c == 0:
                    parts.append(jnp.broadcast_to(home[pl.ds(jj_n * 4 + k, 1), :], (8, 128)))
                return rows_of(parts)

            s_en, t_en, s2_en, t2_en = (entering(k) for k in range(4))
            if c == 0:
                g1v, g2v = through(0, rows)
                an = power(0, rows)
                first = s2_en + decay[0] * (t2[0] + g1v * t_en + g2v * s_en + an * t2_en)
                after = decay[0] * (s2[0] + g1v * s_en + g2v * t_en + an * s2_en) + t2_en
                edge_rows[pl.ds(0, half), :] = first[:half]
                edge_rows[pl.ds(half, half), :] = after[:half]
            base, height = y_parts(c)[i]
            stride = spec[f"y_stride{c}"]
            yt, yv, yf = R.at("yu", c), R.at("yv", c), R.at("yf", c)

            def correct(n, _):
                at = pl.ds(pl.multiple_of(n * stride + base, 8), height)
                f0 = ytab[pl.ds(v * rows + n, 1), :]
                b0 = ytab[pl.ds(v * rows + rows - 1 - n, 1), :]
                f1 = ytab[pl.ds((3 + v) * rows + n, 1), :]
                b1 = ytab[pl.ds((3 + v) * rows + rows - 1 - n, 1), :]
                value = yt[at, :] + yv[at, :] + s_en * f1 + t_en * b1
                yf[at, :] = value + s2_en * f0 + t2_en * b0
                return 0

            lax.fori_loop(0, rows, correct, 0, unroll=2)

    def mix_out(c):
        yf, stride = R.at("yf", c), spec[f"y_stride{c}"]

        def step(b, _):
            js = batch(b)
            for i, v in enumerate(CHUNKS[c]):
                parts = [yf[pl.ds(i * half + j, rows, stride=stride), :] for j in js]
                y = split_product(rows_of(parts), mats[3 + v])
                tile = sig[pl.ds(v * rows, rows), :]
                for t, j in enumerate(js):
                    z = y[t * rows : (t + 1) * rows] * spread(tile, j)
                    if v == 0:
                        put_block(temp, (j + 1) * rows, z)
                    else:
                        put_block(R.w1, w_at(v, j), z)
            return 0

        lax.fori_loop(0, half // 8, step, 0, unroll=True)

    kept = {1: x_filter(1)}
    pl.semaphore_wait(barrier, n_lat + n_lon - 2)

    up = (lax.rem(la + n_lat - 1, n_lat), lo)
    down = (lax.rem(la + 1, n_lat), lo)
    left = (la, lax.rem(lo + n_lon - 1, n_lon))
    right = (la, lax.rem(lo + 1, n_lon))
    starts = (0, msg_r, 2 * msg_r, 2 * msg_r + msg_c)
    sizes = (msg_r, msg_r, msg_c, msg_c)
    halo = []
    for q, device in enumerate((up, down, left, right)):
        here = pl.ds(starts[q], sizes[q])
        copy = pltpu.make_async_remote_copy(
            src_ref=halo_send.at[here],
            dst_ref=halo_recv.at[here],
            send_sem=R.halo_ss.at[q],
            recv_sem=R.halo_rs.at[q],
            device_id=device,
            device_id_type=MESH,
        )
        copy.start()
        halo.append(copy)
    xa1, xb1, xa0 = way("lon", 1, False), way("lon", 1, True), way("lon", 0, False)
    ya1, yb1, ya0, yb0 = way("lat", 1, False), way("lat", 1, True), way("lat", 0, False), way("lat", 0, True)
    za1, za0 = way("lat", 1, False, "z"), way("lat", 0, False, "z")
    exchange(*xa1)

    loads[0].wait()
    pair(0)
    edge_rows[...] = jnp.zeros_like(edge_rows)

    def close_columns(lo_edge, hi_edge):
        put_block(temp, 0, pick(lo_edge, swap(temp[pl.ds(half * rows, rows), :])))
        put_block(temp, (half + 1) * rows, pick(swap(temp[pl.ds(rows, rows), :]), hi_edge))

    zero_block = jnp.zeros((rows, 128), F32)
    close_columns(zero_block, zero_block)
    row_id = lax.broadcasted_iota(jnp.int32, (rows, 128), 0)

    def laplace(j):
        x = block(temp, (j + 1) * rows)
        above = jnp.where(row_id == 0, edge_rows[pl.ds(j, 1), :], pltpu.roll(x, 1, 0))
        below = jnp.where(row_id == rows - 1, edge_rows[pl.ds(half + j, 1), :], pltpu.roll(x, rows - 1, 0))
        return 4.0 * x - above - below - block(temp, j * rows) - block(temp, (j + 2) * rows)

    def mix_psi(b, _):
        js = batch(b)
        y = split_product(rows_of([laplace(j) for j in js]), mats[6])
        y = y + rows_of([block(R.w0, j * rows) for j in js])
        y = split_product(y, mats[0])
        for t, j in enumerate(js):
            put_block(R.w0, j * rows, y[t * rows : (t + 1) * rows] * spread(sig0, j))
        return 0

    lax.fori_loop(0, half // 8, mix_psi, 0, unroll=True)

    wide = jnp.broadcast_to(low1, (half, 128))

    def row_sigma(tile, r):
        t = jnp.concatenate([tile, jnp.zeros((128 - rows, 128), F32)], axis=0).T
        a = jnp.broadcast_to(t[:half, r : r + 1], (half, 128))
        b = jnp.broadcast_to(t[half : 2 * half, r : r + 1], (half, 128))
        return jnp.where(wide, a, b)

    lane_r = lax.broadcasted_iota(jnp.int32, (rows, 128), 1)

    def side_sigma(a, at_a, b, at_b):
        take = lambda x, at: jnp.take_along_axis(
            x, jnp.full((rows, 128), at, jnp.int32), axis=1, mode="promise_in_bounds"
        )
        return jnp.where(lane_r < 64, take(a, at_a), take(b, at_b))

    own_up, own_down = row_sigma(sig0, 0), row_sigma(sig0, rows - 1)
    own_side = side_sigma(sig0, 0, sig0, cols - 1)

    arrive(*xa1)
    x_scan(1)
    exchange(*xb1)

    for copy in halo:
        copy.wait()
    has_up = jnp.where(la > 0, 1.0, 0.0).astype(F32)
    has_down = jnp.where(la < n_lat - 1, 1.0, 0.0).astype(F32)
    has_left = jnp.where(lo > 0, 1.0, 0.0).astype(F32)
    has_right = jnp.where(lo < n_lon - 1, 1.0, 0.0).astype(F32)
    from_right = swap(halo_recv[pl.ds(2 * msg_r, rows), :]) * has_right
    from_left = swap(halo_recv[pl.ds(2 * msg_r + msg_c, rows), :]) * has_left
    outside = rows_of(
        [
            halo_recv[pl.ds(msg_r, half), :] * has_up,
            halo_recv[pl.ds(0, half), :] * has_down,
            pick(from_left, from_right),
        ]
    )
    outside = split_product(split_product(outside, mats[6]), mats[0])
    first_rows = pl.ds(0, half, stride=rows)
    last_rows = pl.ds(rows - 1, half, stride=rows)
    R.w0[first_rows, :] = R.w0[first_rows, :] - outside[:half] * own_up
    R.w0[last_rows, :] = R.w0[last_rows, :] - outside[half : 2 * half] * own_down
    side = outside[2 * half :] * own_side
    at_last = pl.ds((half - 1) * rows, rows)
    R.w0[pl.ds(0, rows), :] = R.w0[pl.ds(0, rows), :] - pick(side, zero_block)
    R.w0[at_last, :] = R.w0[at_last, :] - pick(zero_block, side)

    kept[0] = x_filter(0)
    exchange(*xa0, shared=True)
    w_states(1)
    exchange(*za1)
    w_states(0)
    exchange(*za0)

    arrive(*xb1)
    x_finish(1, kept[1])
    ends1 = y_filter(1)
    exchange(*ya1)
    arrive(*xa0, shared=True)
    x_scan(0)
    x_finish(0, kept[0])
    ends0 = y_filter(0)
    exchange(*ya0)

    up_sigma = row_sigma(halo_recv[pl.ds(msg_r + half, rows), :] * has_up, rows - 1)
    down_sigma = row_sigma(halo_recv[pl.ds(half, rows), :] * has_down, 0)
    side_out = side_sigma(
        halo_recv[pl.ds(2 * msg_r + msg_c + rows, rows), :] * has_left,
        cols - 1,
        halo_recv[pl.ds(2 * msg_r + rows, rows), :] * has_right,
        0,
    )

    R.e_send[...] = jnp.zeros_like(R.e_send)
    near1, near0 = local_energy(1), local_energy(0)

    arrive(*za1)
    arrive(*ya1)
    y_scan(1, near1)
    arrive(*za0)
    arrive(*ya0)
    y_scan(0, near0)
    ea = ("lon", lo, n_lon, 8, R.e_send, R.e_recv, R.e_ss, R.e_rs)
    exchange(*ea, shared=True)
    exchange(*yb1)
    exchange(*yb0)

    def total_of(ref, n):
        total = ref[pl.ds(0, 8), :]
        for e in range(1, n):
            total = total + ref[pl.ds(e * 8, 8), :]
        return total

    arrive(*ea, shared=True)
    R.f_send[...] = total_of(R.e_recv, n_lon)
    fa = ("lat", la, n_lat, 8, R.f_send, R.f_recv, R.f_ss, R.f_rs)
    exchange(*fa, shared=True)
    arrive(*yb1)
    y_finish(1, *ends1)
    mix_out(1)
    arrive(*yb0)
    y_finish(0, *ends0)
    mix_out(0)
    edges = split_product(
        rows_of([edge_rows[...], R.yf0[pl.ds(half, rows, stride=spec["y_stride0"]), :]]), mats[3]
    )
    edge_rows[pl.ds(0, half), :] = edges[:half] * up_sigma
    edge_rows[pl.ds(half, half), :] = edges[half : 2 * half] * down_sigma
    side = edges[2 * half :] * side_out
    close_columns(side, side)

    def unpair(v, js, values):
        for t in range(0, len(js), 2):
            even, odd = values[t], values[t + 1]
            k = lax.div(js[t], 2)
            out_ref[v, :, pl.ds(pl.multiple_of(k * 128, 128), 128)] = pick(even, swap(odd))
            out_ref[v, :, pl.ds(pl.multiple_of((k + half // 2) * 128, 128), 128)] = pick(swap(even), odd)

    def finish(b, _):
        js = batch(b)
        y = split_product(rows_of([laplace(j) for j in js]), mats[7])
        z0 = [block(temp, (j + 1) * rows) for j in js]
        unpair(0, js, z0)
        unpair(1, js, [block(R.w1, w_at(1, j)) + coupling * z for j, z in zip(js, z0)])
        unpair(2, js, [y[t * rows : (t + 1) * rows] + block(R.w1, w_at(2, j)) for t, j in enumerate(js)])
        return 0

    lax.fori_loop(0, half // 8, finish, 0, unroll=True)

    rank = (la * n_lon + lo).astype(F32)
    strict = (
        lax.broadcasted_iota(jnp.int32, (128, 128), 0) < lax.broadcasted_iota(jnp.int32, (128, 128), 1)
    ).astype(F32)
    before = jnp.zeros((1, 1), F32)
    weights = [[], [], []]
    scale = 1.0 / float(rows * n_lat * cols * n_lon)
    for v in range(3):
        mine = jnp.where(low1 & (owners[v] == rank), 1.0, 0.0)
        slot = jnp.dot(jnp.broadcast_to(mine, (8, 128)), strict, preferred_element_type=F32)[:1] + before
        before = before + jnp.sum(mine, axis=1, keepdims=True)
        for k in range(3):
            weights[k].append(jnp.where(slot == float(k), gain[v] * scale * mine, 0.0))
    zeros = jnp.zeros((5, 128), F32)
    weights = [rows_of(line + [zeros]) for line in weights]

    arrive(*fa, shared=True)
    total = total_of(R.f_recv, n_lat)
    total = total + swap(total)
    for k in range(3):
        share = jnp.sum(total * weights[k], axis=0, keepdims=True)
        energy_ref[:, k : k + 1] = jnp.sum(share, axis=1, keepdims=True)

    for one in (xa1, xb1, xa0, za1, za0, ya1, yb1, ya0, yb0, ea, fa):
        left_for_good(*one)


def shards(state, sigma, vert, bal_temp, chi_coef, scales, classes, owner):
    dims = (lax.axis_size("lat"), lax.axis_size("lon"), state.shape[1], sigma.shape[2])
    spec, scratch = layout(*dims, scales.shape[0])
    vmem = pl.BlockSpec(memory_space=pltpu.VMEM)
    return pl.pallas_call(
        functools.partial(kernel, dims, spec, tuple(scratch)),
        out_shape=(pltpu.VMEM(state.shape, F32), pltpu.VMEM((1, 3), F32)),
        in_specs=[pl.BlockSpec(memory_space=pltpu.MemorySpace.HBM)] * 8,
        out_specs=(vmem, vmem),
        scratch_shapes=list(scratch.values()),
        compiler_params=pltpu.CompilerParams(
            collective_id=0, has_side_effects=True, vmem_limit_bytes=56 * 1024 * 1024
        ),
        name="covariance",
    )(
        state,
        sigma,
        vert,
        bal_temp,
        chi_coef.reshape(1, -1),
        scales.reshape(1, -1),
        classes.reshape(1, -1),
        owner.reshape(1, -1),
    )


def solution(mesh):
    return jax.shard_map(
        shards,
        mesh=mesh,
        in_specs=(P(None, "lat", "lon"), P(None, "lat", "lon"), P(), P(), P(), P(), P(), P()),
        out_specs=(P(None, "lat", "lon"), P(("lat", "lon"), None)),
        check_vma=False,
    )
```
